256 devices in a mesh: section: 8 (over x, core), dp: 32 (over y, z).
Axes of the slice: x: 4, y: 4, z: 8, core: 2. Of those that a mesh axis runs over, the one named last changes fastest.
Arguments:
- inputs: bfloat16 [2, 32, 64, 1792], P(None, 'dp'), may hold values from -6 to 6
- cotangent: bfloat16 [2, 32, 64, 1792], P(None, 'dp'), may hold values from -180 to 180
- value_weight: bfloat16 [8, 1792, 1024], P('section', 'dp'), may hold values from -1 to 1
- output_weight: bfloat16 [8, 1024, 1792], P('section', 'dp'), may hold values from -1 to 1
- norm_gain: float32 [8, 1792], P('section'), may hold values from 0.5 to 2
- value_noise: float32 [8, 1792, 1024], P('section', 'dp'), may hold values from -6 to 6
- output_noise: float32 [8, 1024, 1792], P('section', 'dp'), may hold values from -6 to 6
Outputs:
- value_grad: float32 [8, 1792, 1024], P('section', 'dp')
- output_grad: float32 [8, 1024, 1792], P('section', 'dp')
The draws below stay inside these ranges and needn't reach their ends.
All inputs are finite; a program needn't handle non-finite values.
Results may differ from the reference program's by a relative error of at most 0.018.
Values may be sent and summed in bfloat16 or wider, within the bound.
A program may use at most 64 MiB of HBM per device.

```python
import math
import jax
import jax.numpy as jnp
from jax import lax

D = 1792
SEQ = 64
MICRO = 2
H = 1024
LAYERS = 8
EX = 32
N_DP = 32


def layer_scale(lowest):
    position = jnp.arange(LAYERS, dtype=jnp.float32)
    return lowest + position / max(LAYERS - 1, 1)


def projection_draw(key, shape, fan_in):
    base = jax.random.truncated_normal(key, -4.0, 4.0, shape, jnp.float32)
    scales = layer_scale(0.6)
    return (base * scales[:, None, None] / math.sqrt(fan_in)).astype(jnp.bfloat16)


def draw_value_weight(key, part):
    return projection_draw(jax.random.fold_in(key, 11), (LAYERS, D, H), D)


def draw_output_weight(key, part):
    return projection_draw(jax.random.fold_in(key, 23), (LAYERS, H, D), H)


def draw_inputs(key, part):
    keys = jax.random.split(jax.random.fold_in(key, 41), 2)
    shape = (MICRO, EX, SEQ, D)
    shared = jax.random.truncated_normal(keys[1], -4.0, 4.0, (MICRO, EX, 1, D), jnp.float32)
    base = jax.random.truncated_normal(keys[0], -4.0, 4.0, shape, jnp.float32)
    weight = 0.5
    return (base + weight * shared).astype(jnp.bfloat16)


def draw_cotangent(key, part):
    keys = jax.random.split(jax.random.fold_in(key, 37), 5)
    shape = (MICRO, EX, SEQ, D)
    shared = jax.random.truncated_normal(keys[4], -4.0, 4.0, (MICRO, EX, 1, D), jnp.float32)
    base = jax.random.truncated_normal(keys[0], -4.0, 4.0, shape, jnp.float32) + 0.5 * shared
    top = math.log(10.0)
    example_scale = jnp.exp(jax.random.uniform(keys[2], (MICRO, EX, 1, 1), jnp.float32, 0.0, top))
    feature_scale = jnp.exp(jax.random.uniform(keys[3], (1, 1, 1, D), jnp.float32, 0.0, top))
    return (base * example_scale * feature_scale / 10.0).astype(jnp.bfloat16)


def block_scale(own_key, dims, cuts, low, high):
    level = 1.0
    for dim, blocks in cuts:
        steps = jax.random.uniform(jax.random.fold_in(jax.random.fold_in(own_key, 6), dim), (blocks,), jnp.float32, low / len(cuts), high / len(cuts))
        level = level * jnp.repeat(jnp.exp(steps), dims[dim] // blocks).reshape((-1,) + (1,) * (len(dims) - 1 - dim))
    return level


def scatter_about(rng, extent, scale, most, cuts=(), kind=jnp.bfloat16):
    drawn = scale * jax.random.normal(rng, extent, jnp.float32)
    if cuts:
        drawn = drawn * block_scale(rng, extent, cuts, -0.22, 0.18)
    return jnp.clip(drawn, -most, most).astype(kind)


def setup_inputs(seed: int = 0) -> dict:
    streams_of = jax.random.split(jax.random.key(seed), 8)
    inputs = draw_inputs(jax.random.fold_in(streams_of[7], 71), 0)
    cotangent = draw_cotangent(jax.random.fold_in(streams_of[7], 71), 0)
    value_weight = draw_value_weight(jax.random.fold_in(streams_of[7], 71), 0)
    output_weight = draw_output_weight(jax.random.fold_in(streams_of[7], 71), 0)
    norm_gain = jnp.clip(jnp.exp(math.log(2.0) - 1.3862944 * jax.random.uniform(streams_of[4], (LAYERS, D), jnp.float32) ** block_scale(streams_of[4], (LAYERS, D), ((0, 8),), -0.2, 0.2)), 0.5, 2.0)
    value_noise = scatter_about(streams_of[5], (LAYERS, D, H), 1.0, 6.0, ((0, 8), (1, 32)), jnp.float32)
    output_noise = scatter_about(streams_of[6], (LAYERS, H, D), 1.0, 6.0, ((0, 8), (1, 32)), jnp.float32)
    return {"inputs": inputs, "cotangent": cotangent, "value_weight": value_weight, "output_weight": output_weight, "norm_gain": norm_gain, "value_noise": value_noise, "output_noise": output_noise}


def norm_parts(current, gains):
    widened = current.astype(jnp.float32)
    inverse = lax.rsqrt(lax.optimization_barrier(jnp.mean(widened * widened, axis=-1, keepdims=True)) + 1e-06)
    normed = (widened * inverse * gains).astype(jnp.bfloat16)
    return (widened, inverse, normed)

def layer_forward(current, gains, value_matrix, output_matrix):
    widened, inverse, normed = norm_parts(current, gains)
    values = jnp.dot(normed, value_matrix, preferred_element_type=jnp.float32).astype(jnp.bfloat16)
    result = (widened + jnp.dot(values, output_matrix, preferred_element_type=jnp.float32)).astype(jnp.bfloat16)
    return (values, result)

def layer_backward(current, incoming, gains, value_matrix, output_matrix):
    widened, inverse, normed = norm_parts(current, gains)
    dvalues = jnp.dot(incoming, output_matrix.T, preferred_element_type=jnp.float32).astype(jnp.bfloat16)
    dnormed = jnp.dot(dvalues, value_matrix.T, preferred_element_type=jnp.float32) * gains
    centred = widened * inverse
    through = inverse * (dnormed - centred * lax.optimization_barrier(jnp.mean(dnormed * centred, axis=-1, keepdims=True)))
    before = (incoming.astype(jnp.float32) + through).astype(jnp.bfloat16)
    return (normed, dvalues, before)

def pair_norms(left, right, seq_len):
    first = left.astype(jnp.float32).reshape(-1, seq_len, left.shape[-1])
    second = right.astype(jnp.float32).reshape(-1, seq_len, right.shape[-1])
    gram_first = jnp.einsum('eth,esh->ets', first, first, precision=lax.Precision.HIGHEST)
    gram_second = jnp.einsum('eth,esh->ets', second, second, precision=lax.Precision.HIGHEST)
    return lax.optimization_barrier(jnp.sum(gram_first * gram_second, axis=(1, 2)))

def group_sum(left, right, micro_count):
    first = left.reshape(micro_count, N_DP, -1, left.shape[-1]).transpose(1, 0, 2, 3).reshape(N_DP, -1, left.shape[-1])
    second = right.reshape(micro_count, N_DP, -1, right.shape[-1]).transpose(1, 0, 2, 3).reshape(N_DP, -1, right.shape[-1])

    def accumulate(total, pair):
        part = jnp.dot(pair[0].T, pair[1], preferred_element_type=jnp.float32).astype(jnp.bfloat16)
        part = lax.optimization_barrier(part)
        return (total + part.astype(jnp.float32), None)
    start_total = jnp.zeros((left.shape[-1], right.shape[-1]), jnp.float32)
    total, unused = lax.scan(accumulate, start_total, (first, second))
    return total

def reference(inputs, cotangent, value_weight, output_weight, norm_gain, value_noise, output_noise):
    micro_count, example_count, seq_len, feature_width = inputs.shape
    head_width = value_weight.shape[2]
    layer_count = value_weight.shape[0]
    current = inputs.reshape(micro_count, example_count * seq_len, feature_width)
    incoming = cotangent.reshape(micro_count, example_count * seq_len, feature_width)
    stored_inputs = []
    stored_values = []
    for layer_index in range(layer_count):
        stored_inputs.append(current)
        values, current = layer_forward(current, norm_gain[layer_index], value_weight[layer_index], output_weight[layer_index])
        stored_values.append(values)
    squares = jnp.zeros((micro_count * example_count,), jnp.float32)
    normed_all = [None] * layer_count
    dvalues_all = [None] * layer_count
    grads_all = [None] * layer_count
    for layer_index in reversed(range(layer_count)):
        normed, dvalues, before = layer_backward(stored_inputs[layer_index], incoming, norm_gain[layer_index], value_weight[layer_index], output_weight[layer_index])
        squares = squares + pair_norms(normed, dvalues, seq_len) + pair_norms(stored_values[layer_index], incoming, seq_len)
        normed_all[layer_index] = normed
        dvalues_all[layer_index] = dvalues
        grads_all[layer_index] = incoming
        incoming = before
    clip_weight = 1.0 / (jnp.sqrt(squares) + 0.01)
    token_weight = jnp.repeat(clip_weight.reshape(micro_count, example_count), seq_len, axis=1)[:, :, None]
    grad_scale = math.sqrt(feature_width * head_width)
    value_grads = []
    output_grads = []
    for layer_index in range(layer_count):
        scaled_dvalues = (dvalues_all[layer_index].astype(jnp.float32) * token_weight).astype(jnp.bfloat16)
        scaled_grads = (grads_all[layer_index].astype(jnp.float32) * token_weight).astype(jnp.bfloat16)
        value_total = group_sum(normed_all[layer_index], scaled_dvalues, micro_count)
        output_total = group_sum(stored_values[layer_index], scaled_grads, micro_count)
        value_grads.append(value_total * grad_scale + value_noise[layer_index])
        output_grads.append(output_total * grad_scale + output_noise[layer_index])
    return (jnp.stack(value_grads), jnp.stack(output_grads))
```

```python
import math

import jax
import jax.numpy as jnp
from jax import lax
from jax.sharding import Mesh, PartitionSpec as P


def from_behind(block, axis, distance):
    devices = range(lax.axis_size(axis))
    route = [(i - distance, i) for i in devices if i - distance in devices]
    return lax.ppermute(block, axis, route)


def norm_parts(current, gains):
    widened = current.astype(jnp.float32)
    inverse = lax.rsqrt(jnp.mean(widened * widened, axis=-1, keepdims=True) + 1e-06)
    normed = (widened * inverse * gains).astype(jnp.bfloat16)
    return (widened, inverse, normed)


def layer_forward(current, gains, value_matrix, output_matrix):
    widened, inverse, normed = norm_parts(current, gains)
    values = jnp.dot(normed, value_matrix, preferred_element_type=jnp.float32).astype(jnp.bfloat16)
    result = (widened + jnp.dot(values, output_matrix, preferred_element_type=jnp.float32)).astype(
        jnp.bfloat16
    )
    return (values, result)


def layer_backward(current, incoming, gains, value_matrix, output_matrix):
    widened, inverse, normed = norm_parts(current, gains)
    dvalues = jnp.dot(incoming, output_matrix.T, preferred_element_type=jnp.float32).astype(
        jnp.bfloat16
    )
    dnormed = jnp.dot(dvalues, value_matrix.T, preferred_element_type=jnp.float32) * gains
    centred = widened * inverse
    through = inverse * (dnormed - centred * jnp.mean(dnormed * centred, axis=-1, keepdims=True))
    before = (incoming.astype(jnp.float32) + through).astype(jnp.bfloat16)
    return (normed, dvalues, before)


def example_sums(left, right, seq_len):
    first = left.reshape(-1, seq_len, left.shape[-1])
    second = right.reshape(-1, seq_len, right.shape[-1])
    per_example = jnp.einsum("eth,etd->ehd", first, second, preferred_element_type=jnp.float32)
    return jnp.sum(per_example * per_example, axis=(1, 2))


def forward_chain(feed_rows, gains, value_matrix, output_matrix):
    section_count = lax.axis_size("section")
    section_place = lax.axis_index("section")
    micro_count, row_count, feature_width = feed_rows.shape
    head_width = value_matrix.shape[1]

    def forward_active_step(source):
        return layer_forward(source, gains, value_matrix, output_matrix)

    def forward_spare_step(source):
        return (
            jnp.zeros((row_count, head_width), jnp.bfloat16),
            jnp.zeros((row_count, feature_width), jnp.bfloat16),
        )

    def forward_time_step(counter, carried):
        incoming, kept_inputs, kept_values = carried
        which_micro = counter - section_place
        active = (which_micro >= 0) & (which_micro < micro_count)
        slot_index = jnp.clip(which_micro, 0, micro_count - 1)
        source = jnp.where(
            section_place == 0,
            lax.dynamic_index_in_dim(feed_rows, slot_index, 0, keepdims=False),
            incoming,
        )
        values, result = lax.cond(active, forward_active_step, forward_spare_step, source)
        old_inputs = lax.dynamic_index_in_dim(kept_inputs, slot_index, 0, keepdims=False)
        old_values = lax.dynamic_index_in_dim(kept_values, slot_index, 0, keepdims=False)
        kept_inputs = lax.dynamic_update_index_in_dim(
            kept_inputs, jnp.where(active, source, old_inputs), slot_index, 0
        )
        kept_values = lax.dynamic_update_index_in_dim(
            kept_values, jnp.where(active, values, old_values), slot_index, 0
        )
        incoming = from_behind(result, "section", 1)
        return (incoming, kept_inputs, kept_values)

    start_state = (
        jnp.zeros((row_count, feature_width), jnp.bfloat16),
        jnp.zeros((micro_count, row_count, feature_width), jnp.bfloat16),
        jnp.zeros((micro_count, row_count, head_width), jnp.bfloat16),
    )
    final_state = lax.fori_loop(0, section_count + micro_count - 1, forward_time_step, start_state)
    return (final_state[1], final_state[2])


def backward_chain(kept_inputs, kept_values, cot_rows, gains, value_matrix, output_matrix, seq_len):
    section_count = lax.axis_size("section")
    section_place = lax.axis_index("section")
    micro_count, row_count, feature_width = kept_inputs.shape
    head_width = kept_values.shape[-1]
    example_here = row_count // seq_len
    last_place = section_count - 1

    def backward_active_step(operands):
        inputs_here, values_here, grad_here = operands
        normed, dvalues, before = layer_backward(
            inputs_here, grad_here, gains, value_matrix, output_matrix
        )
        squares = example_sums(normed, dvalues, seq_len) + example_sums(
            values_here, grad_here, seq_len
        )
        return (before, dvalues, squares)

    def backward_spare_step(operands):
        return (
            jnp.zeros((row_count, feature_width), jnp.bfloat16),
            jnp.zeros((row_count, head_width), jnp.bfloat16),
            jnp.zeros((example_here,), jnp.float32),
        )

    def backward_time_step(counter, carried):
        incoming, kept_grads, kept_dvalues, squares_all = carried
        which_micro = counter - (last_place - section_place)
        active = (which_micro >= 0) & (which_micro < micro_count)
        slot_index = jnp.clip(which_micro, 0, micro_count - 1)
        grad_here = jnp.where(
            section_place == last_place,
            lax.dynamic_index_in_dim(cot_rows, slot_index, 0, keepdims=False),
            incoming,
        )
        inputs_here = lax.dynamic_index_in_dim(kept_inputs, slot_index, 0, keepdims=False)
        values_here = lax.dynamic_index_in_dim(kept_values, slot_index, 0, keepdims=False)
        before, dvalues, squares = lax.cond(
            active, backward_active_step, backward_spare_step, (inputs_here, values_here, grad_here)
        )
        old_grads = lax.dynamic_index_in_dim(kept_grads, slot_index, 0, keepdims=False)
        old_dvalues = lax.dynamic_index_in_dim(kept_dvalues, slot_index, 0, keepdims=False)
        old_squares = lax.dynamic_index_in_dim(squares_all, slot_index, 0, keepdims=False)
        kept_grads = lax.dynamic_update_index_in_dim(
            kept_grads, jnp.where(active, grad_here, old_grads), slot_index, 0
        )
        kept_dvalues = lax.dynamic_update_index_in_dim(
            kept_dvalues, jnp.where(active, dvalues, old_dvalues), slot_index, 0
        )
        squares_all = lax.dynamic_update_index_in_dim(
            squares_all, jnp.where(active, squares, old_squares), slot_index, 0
        )
        incoming = from_behind(before, "section", -1)
        return (incoming, kept_grads, kept_dvalues, squares_all)

    start_state = (
        jnp.zeros((row_count, feature_width), jnp.bfloat16),
        jnp.zeros((micro_count, row_count, feature_width), jnp.bfloat16),
        jnp.zeros((micro_count, row_count, head_width), jnp.bfloat16),
        jnp.zeros((micro_count, example_here), jnp.float32),
    )
    final_state = lax.fori_loop(0, section_count + micro_count - 1, backward_time_step, start_state)
    return (final_state[1], final_state[2], final_state[3])


DP = ("y", "z")


def gather_rows(shard):
    inner = lax.all_gather(shard, "z", axis=0, tiled=True)
    return lax.all_gather(inner, "y", axis=0, tiled=True)


def exchange_rows(shard):
    count = lax.axis_size(DP)
    copies = jnp.broadcast_to(shard[None], (count,) + shard.shape)
    parts = lax.all_to_all(copies, DP, 0, 0, tiled=False)
    return parts.reshape((-1,) + shard.shape[1:])


def scatter_in_stages(block):
    inner = lax.psum_scatter(block, "y", scatter_dimension=0, tiled=True)
    return lax.psum_scatter(inner, "z", scatter_dimension=0, tiled=True).astype(jnp.float32)


def scatter_by_exchange(block):
    count = lax.axis_size(DP)
    parts = block.reshape((count, block.shape[0] // count) + block.shape[1:])
    arrived = lax.all_to_all(parts, DP, 0, 0, tiled=False)
    return jnp.sum(arrived.astype(jnp.float32), axis=0)


def on_device(inputs, cotangent, value_weight, output_weight, norm_gain, value_noise, output_noise):
    micro_count, example_count, seq_len, feature_width = inputs.shape
    feed_rows = inputs.reshape(micro_count, example_count * seq_len, feature_width)
    cot_rows = cotangent.reshape(micro_count, example_count * seq_len, feature_width)
    value_matrix = gather_rows(value_weight[0])
    output_matrix = exchange_rows(output_weight[0])
    head_width = value_matrix.shape[1]
    gains = norm_gain[0]
    kept_inputs, kept_values = forward_chain(feed_rows, gains, value_matrix, output_matrix)
    kept_grads, kept_dvalues, partial_squares = backward_chain(
        kept_inputs, kept_values, cot_rows, gains, value_matrix, output_matrix, seq_len
    )
    total_squares = lax.psum(partial_squares, "section")
    clip_weight = 1.0 / (jnp.sqrt(total_squares) + 0.01)
    token_weight = jnp.repeat(clip_weight, seq_len, axis=1)[:, :, None]
    scaled_dvalues = (
        (kept_dvalues.astype(jnp.float32) * token_weight)
        .astype(jnp.bfloat16)
        .reshape(-1, head_width)
    )
    scaled_grads = (
        (kept_grads.astype(jnp.float32) * token_weight)
        .astype(jnp.bfloat16)
        .reshape(-1, feature_width)
    )
    unused_wide, unused_inverse, normed_rows = norm_parts(
        kept_inputs.reshape(-1, feature_width), gains
    )
    value_rows = kept_values.reshape(-1, head_width)
    columns = normed_rows
    value_part = scatter_in_stages(
        lax.dot_general(
            columns, scaled_dvalues, (((0,), (0,)), ((), ())), preferred_element_type=jnp.float32
        ).astype(jnp.bfloat16)
    )
    columns = value_rows
    output_part = scatter_by_exchange(
        lax.dot_general(
            columns, scaled_grads, (((0,), (0,)), ((), ())), preferred_element_type=jnp.float32
        ).astype(jnp.bfloat16)
    )
    grad_scale = math.sqrt(feature_width * head_width)
    value_grad = (value_part * grad_scale + value_noise[0])[None]
    output_grad = (output_part * grad_scale + output_noise[0])[None]
    return (value_grad, output_grad)


def split_dp(mesh):
    devices = mesh.devices
    sections, count = devices.shape
    try:
        across = len({d.coords[1] for d in devices[0]})
    except (AttributeError, IndexError, TypeError):
        across = 1
    if across < 1 or count % across:
        across = 1
    return Mesh(devices.reshape(sections, across, count // across), ("section",) + DP)


def solution(mesh):
    grid = split_dp(mesh)
    return jax.shard_map(
        on_device,
        mesh=grid,
        in_specs=(
            P(None, DP, None, None),
            P(None, DP, None, None),
            P("section", DP, None),
            P("section", DP, None),
            P("section", None),
            P("section", DP, None),
            P("section", DP, None),
        ),
        out_specs=(P("section", DP, None), P("section", DP, None)),
        check_vma=False,
    )
```

```python
import math

import jax
import jax.numpy as jnp
from jax import lax
from jax.sharding import Mesh, PartitionSpec as P


def from_behind(block, axis, distance):
    devices = range(lax.axis_size(axis))
    route = [(i - distance, i) for i in devices if i - distance in devices]
    return lax.ppermute(block, axis, route)


def norm_parts(current, gains):
    widened = current.astype(jnp.float32)
    inverse = lax.rsqrt(jnp.mean(widened * widened, axis=-1, keepdims=True) + 1e-06)
    normed = (widened * inverse * gains).astype(jnp.bfloat16)
    return (widened, inverse, normed)


def layer_forward(current, gains, value_matrix, output_matrix):
    widened, inverse, normed = norm_parts(current, gains)
    values = jnp.dot(normed, value_matrix, preferred_element_type=jnp.float32).astype(jnp.bfloat16)
    result = (widened + jnp.dot(values, output_matrix, preferred_element_type=jnp.float32)).astype(
        jnp.bfloat16
    )
    return (values, result)


def layer_backward(current, incoming, gains, value_matrix, output_matrix):
    widened, inverse, normed = norm_parts(current, gains)
    dvalues = jnp.dot(incoming, output_matrix.T, preferred_element_type=jnp.float32).astype(
        jnp.bfloat16
    )
    dnormed = jnp.dot(dvalues, value_matrix.T, preferred_element_type=jnp.float32) * gains
    centred = widened * inverse
    through = inverse * (dnormed - centred * jnp.mean(dnormed * centred, axis=-1, keepdims=True))
    before = (incoming.astype(jnp.float32) + through).astype(jnp.bfloat16)
    return (normed, dvalues, before)


def example_sums(left, right, seq_len):
    first = left.reshape(-1, seq_len, left.shape[-1])
    second = right.reshape(-1, seq_len, right.shape[-1])
    gram_first = jnp.einsum("eth,esh->ets", first, first, preferred_element_type=jnp.float32)
    gram_second = jnp.einsum("eth,esh->ets", second, second, preferred_element_type=jnp.float32)
    return jnp.sum(gram_first * gram_second, axis=(1, 2))


def forward_chain(feed_rows, gains, value_matrix, output_matrix):
    section_count = lax.axis_size("section")
    section_place = lax.axis_index("section")
    micro_count, row_count, feature_width = feed_rows.shape
    head_width = value_matrix.shape[1]

    def forward_active_step(source):
        return layer_forward(source, gains, value_matrix, output_matrix)

    def forward_spare_step(source):
        return (
            jnp.zeros((row_count, head_width), jnp.bfloat16),
            jnp.zeros((row_count, feature_width), jnp.bfloat16),
        )

    def forward_time_step(counter, carried):
        incoming, kept_inputs, kept_values = carried
        which_micro = counter - section_place
        active = (which_micro >= 0) & (which_micro < micro_count)
        slot_index = jnp.clip(which_micro, 0, micro_count - 1)
        source = jnp.where(
            section_place == 0,
            lax.dynamic_index_in_dim(feed_rows, slot_index, 0, keepdims=False),
            incoming,
        )
        values, result = lax.cond(active, forward_active_step, forward_spare_step, source)
        old_inputs = lax.dynamic_index_in_dim(kept_inputs, slot_index, 0, keepdims=False)
        old_values = lax.dynamic_index_in_dim(kept_values, slot_index, 0, keepdims=False)
        kept_inputs = lax.dynamic_update_index_in_dim(
            kept_inputs, jnp.where(active, source, old_inputs), slot_index, 0
        )
        kept_values = lax.dynamic_update_index_in_dim(
            kept_values, jnp.where(active, values, old_values), slot_index, 0
        )
        incoming = from_behind(result, "section", 1)
        return (incoming, kept_inputs, kept_values)

    start_state = (
        jnp.zeros((row_count, feature_width), jnp.bfloat16),
        jnp.zeros((micro_count, row_count, feature_width), jnp.bfloat16),
        jnp.zeros((micro_count, row_count, head_width), jnp.bfloat16),
    )
    final_state = lax.fori_loop(0, section_count + micro_count - 1, forward_time_step, start_state)
    return (final_state[1], final_state[2])


def backward_chain(kept_inputs, kept_values, cot_rows, gains, value_matrix, output_matrix, seq_len):
    section_count = lax.axis_size("section")
    section_place = lax.axis_index("section")
    micro_count, row_count, feature_width = kept_inputs.shape
    head_width = kept_values.shape[-1]
    last_place = section_count - 1

    def backward_active_step(operands):
        inputs_here, values_here, grad_here = operands
        normed, dvalues, before = layer_backward(
            inputs_here, grad_here, gains, value_matrix, output_matrix
        )
        return (before, dvalues)

    def backward_spare_step(operands):
        return (
            jnp.zeros((row_count, feature_width), jnp.bfloat16),
            jnp.zeros((row_count, head_width), jnp.bfloat16),
        )

    def backward_time_step(counter, carried):
        incoming, kept_grads, kept_dvalues = carried
        which_micro = counter - (last_place - section_place)
        active = (which_micro >= 0) & (which_micro < micro_count)
        slot_index = jnp.clip(which_micro, 0, micro_count - 1)
        grad_here = jnp.where(
            section_place == last_place,
            lax.dynamic_index_in_dim(cot_rows, slot_index, 0, keepdims=False),
            incoming,
        )
        inputs_here = lax.dynamic_index_in_dim(kept_inputs, slot_index, 0, keepdims=False)
        values_here = lax.dynamic_index_in_dim(kept_values, slot_index, 0, keepdims=False)
        before, dvalues = lax.cond(
            active, backward_active_step, backward_spare_step, (inputs_here, values_here, grad_here)
        )
        old_grads = lax.dynamic_index_in_dim(kept_grads, slot_index, 0, keepdims=False)
        old_dvalues = lax.dynamic_index_in_dim(kept_dvalues, slot_index, 0, keepdims=False)
        kept_grads = lax.dynamic_update_index_in_dim(
            kept_grads, jnp.where(active, grad_here, old_grads), slot_index, 0
        )
        kept_dvalues = lax.dynamic_update_index_in_dim(
            kept_dvalues, jnp.where(active, dvalues, old_dvalues), slot_index, 0
        )
        incoming = from_behind(before, "section", -1)
        return (incoming, kept_grads, kept_dvalues)

    start_state = (
        jnp.zeros((row_count, feature_width), jnp.bfloat16),
        jnp.zeros((micro_count, row_count, feature_width), jnp.bfloat16),
        jnp.zeros((micro_count, row_count, head_width), jnp.bfloat16),
    )
    final_state = lax.fori_loop(0, section_count + micro_count - 1, backward_time_step, start_state)
    return (final_state[1], final_state[2])


DP = ("y", "z")


def exchange_rows(shard):
    count = lax.axis_size(DP)
    copies = jnp.broadcast_to(shard[None], (count,) + shard.shape)
    parts = lax.all_to_all(copies, DP, 0, 0, tiled=False)
    return parts.reshape((-1,) + shard.shape[1:])


def scatter_in_stages(block):
    inner = lax.psum_scatter(block, "y", scatter_dimension=0, tiled=True)
    return lax.psum_scatter(inner, "z", scatter_dimension=0, tiled=True).astype(jnp.float32)


def scatter_by_exchange(block):
    count = lax.axis_size(DP)
    parts = block.reshape((count, block.shape[0] // count) + block.shape[1:])
    arrived = lax.all_to_all(parts, DP, 0, 0, tiled=False)
    return jnp.sum(arrived.astype(jnp.float32), axis=0)


def on_device(inputs, cotangent, value_weight, output_weight, norm_gain, value_noise, output_noise):
    micro_count, example_count, seq_len, feature_width = inputs.shape
    feed_rows = inputs.reshape(micro_count, example_count * seq_len, feature_width)
    cot_rows = cotangent.reshape(micro_count, example_count * seq_len, feature_width)
    value_matrix = lax.all_gather(value_weight[0], DP, axis=0, tiled=True)
    output_matrix = exchange_rows(output_weight[0])
    head_width = value_matrix.shape[1]
    gains = norm_gain[0]
    kept_inputs, kept_values = forward_chain(feed_rows, gains, value_matrix, output_matrix)
    kept_grads, kept_dvalues = backward_chain(
        kept_inputs, kept_values, cot_rows, gains, value_matrix, output_matrix, seq_len
    )
    unused_wide, unused_inverse, normed_rows = norm_parts(
        kept_inputs.reshape(-1, feature_width), gains
    )
    normed_kept = normed_rows.reshape(kept_inputs.shape)
    partial_squares = jnp.stack(
        [
            example_sums(normed_kept[m], kept_dvalues[m], seq_len)
            + example_sums(kept_values[m], kept_grads[m], seq_len)
            for m in range(micro_count)
        ]
    )
    total_squares = lax.psum(partial_squares, "section")
    clip_weight = 1.0 / (jnp.sqrt(total_squares) + 0.01)
    token_weight = jnp.repeat(clip_weight, seq_len, axis=1)[:, :, None]
    scaled_dvalues = (
        (kept_dvalues.astype(jnp.float32) * token_weight)
        .astype(jnp.bfloat16)
        .reshape(-1, head_width)
    )
    scaled_grads = (
        (kept_grads.astype(jnp.float32) * token_weight)
        .astype(jnp.bfloat16)
        .reshape(-1, feature_width)
    )
    value_rows = kept_values.reshape(-1, head_width)
    columns = normed_rows
    value_part = scatter_in_stages(
        lax.dot_general(
            columns, scaled_dvalues, (((0,), (0,)), ((), ())), preferred_element_type=jnp.float32
        ).astype(jnp.bfloat16)
    )
    columns = value_rows
    output_part = scatter_by_exchange(
        lax.dot_general(
            columns, scaled_grads, (((0,), (0,)), ((), ())), preferred_element_type=jnp.float32
        ).astype(jnp.bfloat16)
    )
    grad_scale = math.sqrt(feature_width * head_width)
    value_grad = (value_part * grad_scale + value_noise[0])[None]
    output_grad = (output_part * grad_scale + output_noise[0])[None]
    return (value_grad, output_grad)


def split_dp(mesh):
    devices = mesh.devices
    sections, count = devices.shape
    try:
        across = len({d.coords[1] for d in devices[0]})
    except (AttributeError, IndexError, TypeError):
        across = 1
    if across < 1 or count % across:
        across = 1
    return Mesh(devices.reshape(sections, across, count // across), ("section",) + DP)


def solution(mesh):
    grid = split_dp(mesh)
    return jax.shard_map(
        on_device,
        mesh=grid,
        in_specs=(
            P(None, DP, None, None),
            P(None, DP, None, None),
            P("section", DP, None),
            P("section", DP, None),
            P("section", None),
            P("section", DP, None),
            P("section", DP, None),
        ),
        out_specs=(P("section", DP, None), P("section", DP, None)),
        check_vma=False,
    )
```

```python
import functools
import math

import jax
import jax.numpy as jnp
from jax import lax
from jax.experimental import pallas as pl
from jax.experimental.pallas import tpu as pltpu
from jax.sharding import Mesh, PartitionSpec as P


def norm_parts(current, gains):
    widened = current.astype(jnp.float32)
    inverse = lax.rsqrt(jnp.mean(widened * widened, axis=-1, keepdims=True) + 1e-06)
    normed = (widened * inverse * gains).astype(jnp.bfloat16)
    return (widened, inverse, normed)


def layer_forward(current, gains, value_matrix, output_matrix):
    widened, inverse, normed = norm_parts(current, gains)
    values = jnp.dot(normed, value_matrix, preferred_element_type=jnp.float32).astype(jnp.bfloat16)
    result = (widened + jnp.dot(values, output_matrix, preferred_element_type=jnp.float32)).astype(
        jnp.bfloat16
    )
    return (values, result)


def layer_backward(current, incoming, gains, value_matrix, output_matrix):
    widened, inverse, normed = norm_parts(current, gains)
    dvalues = jnp.dot(incoming, output_matrix.T, preferred_element_type=jnp.float32).astype(
        jnp.bfloat16
    )
    dnormed = jnp.dot(dvalues, value_matrix.T, preferred_element_type=jnp.float32) * gains
    centred = widened * inverse
    through = inverse * (dnormed - centred * jnp.mean(dnormed * centred, axis=-1, keepdims=True))
    before = (incoming.astype(jnp.float32) + through).astype(jnp.bfloat16)
    return (normed, dvalues, before)


def example_sums(left, right, seq_len):
    first = left.reshape(-1, seq_len, left.shape[-1])
    second = right.reshape(-1, seq_len, right.shape[-1])
    gram_first = jnp.einsum("eth,esh->ets", first, first, preferred_element_type=jnp.float32)
    gram_second = jnp.einsum("eth,esh->ets", second, second, preferred_element_type=jnp.float32)
    return jnp.sum(gram_first * gram_second, axis=(1, 2))


TILE = 256


def chain_kernel(
    sections,
    seed_ref, cot_ref, gain_ref, wv_ref, wo_ref,
    kin_ref, kval_ref, kgrad_ref, kdv_ref,
    fbuf, fres, bbuf, bres, work, fsend, frecv, bsend, brecv,
):
    place = lax.axis_index("section")
    micro_count, rows, width = seed_ref.shape
    heads = wv_ref.shape[1]
    ahead = lax.rem(place + 1, sections)
    behind = lax.rem(place + sections - 1, sections)
    first = place == 0
    last = place == sections - 1

    barrier = pltpu.get_barrier_semaphore()

    @pl.when(place > 0)
    def _():
        pl.semaphore_signal(barrier, inc=1, device_id={"section": behind}, device_id_type=pl.DeviceIdType.MESH)

    @pl.when(place < sections - 1)
    def _():
        pl.semaphore_signal(barrier, inc=1, device_id={"section": ahead}, device_id_type=pl.DeviceIdType.MESH)

    peers = (place + sections - 1) // sections + (2 * sections - 2 - place) // sections
    pl.semaphore_wait(barrier, peers)

    @pl.when(first)
    def _():
        fbuf[...] = seed_ref[...]

    @pl.when(last)
    def _():
        bbuf[...] = cot_ref[...]

    def forward_copy(m):
        return pltpu.make_async_remote_copy(
            src_ref=fres.at[m], dst_ref=fbuf.at[m], send_sem=fsend.at[m], recv_sem=frecv.at[m],
            device_id={"section": ahead}, device_id_type=pl.DeviceIdType.MESH,
        )

    def backward_copy(m):
        return pltpu.make_async_remote_copy(
            src_ref=bres.at[m], dst_ref=bbuf.at[m], send_sem=bsend.at[m], recv_sem=brecv.at[m],
            device_id={"section": behind}, device_id_type=pl.DeviceIdType.MESH,
        )

    def columns(i):
        return pl.ds(pl.multiple_of(i * TILE, TILE), TILE)

    for m in range(micro_count):
        @pl.when(place > 0)
        def _():
            forward_copy(m).wait_recv()

        x = fbuf[m]
        kin_ref[m] = x
        wide = x.astype(jnp.float32)
        inverse = lax.rsqrt(jnp.mean(wide * wide, axis=-1, keepdims=True) + 1e-06)
        normed = (wide * inverse * gain_ref[...]).astype(jnp.bfloat16)

        def value_tile(i, carry):
            kval_ref[m, :, columns(i)] = jnp.dot(
                normed, wv_ref[:, columns(i)], preferred_element_type=jnp.float32
            ).astype(jnp.bfloat16)
            return carry

        lax.fori_loop(0, heads // TILE, value_tile, 0)
        values = kval_ref[m]

        def result_tile(i, carry):
            fres[m, :, columns(i)] = (
                fbuf[m, :, columns(i)].astype(jnp.float32)
                + jnp.dot(values, wo_ref[:, columns(i)], preferred_element_type=jnp.float32)
            ).astype(jnp.bfloat16)
            return carry

        lax.fori_loop(0, width // TILE, result_tile, 0)

        @pl.when(place < sections - 1)
        def _():
            forward_copy(m).start()

    contract = (((1,), (1,)), ((), ()))
    for m in range(micro_count):
        @pl.when(place < sections - 1)
        def _():
            backward_copy(m).wait_recv()

        grad = bbuf[m]
        kgrad_ref[m] = grad

        def dvalue_tile(i, carry):
            kdv_ref[m, :, columns(i)] = lax.dot_general(
                grad, wo_ref[columns(i), :], contract, preferred_element_type=jnp.float32
            ).astype(jnp.bfloat16)
            return carry

        lax.fori_loop(0, heads // TILE, dvalue_tile, 0)
        dvalues = kdv_ref[m]

        def dnormed_tile(i, carry):
            work[:, columns(i)] = lax.dot_general(
                dvalues, wv_ref[columns(i), :], contract, preferred_element_type=jnp.float32
            ) * gain_ref[:, columns(i)]
            return carry

        lax.fori_loop(0, width // TILE, dnormed_tile, 0)
        wide = kin_ref[m].astype(jnp.float32)
        inverse = lax.rsqrt(jnp.mean(wide * wide, axis=-1, keepdims=True) + 1e-06)
        dnormed = work[...]
        centred = wide * inverse
        through = inverse * (dnormed - centred * jnp.mean(dnormed * centred, axis=-1, keepdims=True))
        bres[m] = (grad.astype(jnp.float32) + through).astype(jnp.bfloat16)

        @pl.when(place > 0)
        def _():
            backward_copy(m).start()

    for m in range(micro_count):
        @pl.when(place < sections - 1)
        def _():
            forward_copy(m).wait_send()

        @pl.when(place > 0)
        def _():
            backward_copy(m).wait_send()


def run_chain(feed_rows, cot_rows, gains, value_matrix, output_matrix):
    sections = lax.axis_size("section")
    micro_count, rows, width = feed_rows.shape
    heads = value_matrix.shape[1]
    vmem = pl.BlockSpec(memory_space=pltpu.VMEM)
    act = jax.ShapeDtypeStruct((micro_count, rows, width), jnp.bfloat16)
    head_act = jax.ShapeDtypeStruct((micro_count, rows, heads), jnp.bfloat16)
    return pl.pallas_call(
        functools.partial(chain_kernel, sections),
        out_shape=(act, head_act, act, head_act),
        in_specs=[vmem] * 5,
        out_specs=(vmem,) * 4,
        scratch_shapes=[
            pltpu.VMEM((micro_count, rows, width), jnp.bfloat16),
            pltpu.VMEM((micro_count, rows, width), jnp.bfloat16),
            pltpu.VMEM((micro_count, rows, width), jnp.bfloat16),
            pltpu.VMEM((micro_count, rows, width), jnp.bfloat16),
            pltpu.VMEM((rows, width), jnp.float32),
            pltpu.SemaphoreType.DMA((micro_count,)),
            pltpu.SemaphoreType.DMA((micro_count,)),
            pltpu.SemaphoreType.DMA((micro_count,)),
            pltpu.SemaphoreType.DMA((micro_count,)),
        ],
        compiler_params=pltpu.CompilerParams(
            collective_id=0, has_side_effects=True, vmem_limit_bytes=48 * 1024 * 1024
        ),
    )(feed_rows, cot_rows, gains.reshape(1, width), value_matrix, output_matrix)


DP = ("y", "z")


def exchange_rows(shard):
    count = lax.axis_size(DP)
    copies = jnp.broadcast_to(shard[None], (count,) + shard.shape)
    parts = lax.all_to_all(copies, DP, 0, 0, tiled=False)
    return parts.reshape((-1,) + shard.shape[1:])


def scatter_in_stages(block):
    inner = lax.psum_scatter(block, "y", scatter_dimension=0, tiled=True)
    return lax.psum_scatter(inner, "z", scatter_dimension=0, tiled=True).astype(jnp.float32)


def scatter_by_exchange(block):
    count = lax.axis_size(DP)
    parts = block.reshape((count, block.shape[0] // count) + block.shape[1:])
    arrived = lax.all_to_all(parts, DP, 0, 0, tiled=False)
    return jnp.sum(arrived.astype(jnp.float32), axis=0)


def on_device(inputs, cotangent, value_weight, output_weight, norm_gain, value_noise, output_noise):
    micro_count, example_count, seq_len, feature_width = inputs.shape
    feed_rows = inputs.reshape(micro_count, example_count * seq_len, feature_width)
    cot_rows = cotangent.reshape(micro_count, example_count * seq_len, feature_width)
    value_matrix = lax.all_gather(value_weight[0], DP, axis=0, tiled=True)
    output_matrix = exchange_rows(output_weight[0])
    head_width = value_matrix.shape[1]
    gains = norm_gain[0]
    kept_inputs, kept_values, kept_grads, kept_dvalues = run_chain(
        feed_rows, cot_rows, gains, value_matrix, output_matrix
    )
    unused_wide, unused_inverse, normed_rows = norm_parts(
        kept_inputs.reshape(-1, feature_width), gains
    )
    normed_kept = normed_rows.reshape(kept_inputs.shape)
    partial_squares = jnp.stack(
        [
            example_sums(normed_kept[m], kept_dvalues[m], seq_len)
            + example_sums(kept_values[m], kept_grads[m], seq_len)
            for m in range(micro_count)
        ]
    )
    total_squares = lax.psum(partial_squares, "section")
    clip_weight = 1.0 / (jnp.sqrt(total_squares) + 0.01)
    token_weight = jnp.repeat(clip_weight, seq_len, axis=1)[:, :, None]
    scaled_dvalues = (
        (kept_dvalues.astype(jnp.float32) * token_weight)
        .astype(jnp.bfloat16)
        .reshape(-1, head_width)
    )
    scaled_grads = (
        (kept_grads.astype(jnp.float32) * token_weight)
        .astype(jnp.bfloat16)
        .reshape(-1, feature_width)
    )
    value_rows = kept_values.reshape(-1, head_width)
    columns = normed_rows
    value_part = scatter_in_stages(
        lax.dot_general(
            columns, scaled_dvalues, (((0,), (0,)), ((), ())), preferred_element_type=jnp.float32
        ).astype(jnp.bfloat16)
    )
    columns = value_rows
    output_part = scatter_by_exchange(
        lax.dot_general(
            columns, scaled_grads, (((0,), (0,)), ((), ())), preferred_element_type=jnp.float32
        ).astype(jnp.bfloat16)
    )
    grad_scale = math.sqrt(feature_width * head_width)
    value_grad = (value_part * grad_scale + value_noise[0])[None]
    output_grad = (output_part * grad_scale + output_noise[0])[None]
    return (value_grad, output_grad)


def split_dp(mesh):
    devices = mesh.devices
    sections, count = devices.shape
    try:
        across = len({d.coords[1] for d in devices[0]})
    except (AttributeError, IndexError, TypeError):
        across = 1
    if across < 1 or count % across:
        across = 1
    return Mesh(devices.reshape(sections, across, count // across), ("section",) + DP)


def solution(mesh):
    grid = split_dp(mesh)
    return jax.shard_map(
        on_device,
        mesh=grid,
        in_specs=(
            P(None, DP, None, None),
            P(None, DP, None, None),
            P("section", DP, None),
            P("section", DP, None),
            P("section", None),
            P("section", DP, None),
            P("section", DP, None),
        ),
        out_specs=(P("section", DP, None), P("section", DP, None)),
        check_vma=False,
    )
```

```python
import functools
import math

import jax
import jax.numpy as jnp
from jax import lax
from jax.experimental import pallas as pl
from jax.experimental.pallas import tpu as pltpu
from jax.sharding import Mesh, PartitionSpec as P


def norm_parts(current, gains):
    widened = current.astype(jnp.float32)
    inverse = lax.rsqrt(jnp.mean(widened * widened, axis=-1, keepdims=True) + 1e-06)
    normed = (widened * inverse * gains).astype(jnp.bfloat16)
    return (widened, inverse, normed)


def layer_forward(current, gains, value_matrix, output_matrix):
    widened, inverse, normed = norm_parts(current, gains)
    values = jnp.dot(normed, value_matrix, preferred_element_type=jnp.float32).astype(jnp.bfloat16)
    result = (widened + jnp.dot(values, output_matrix, preferred_element_type=jnp.float32)).astype(
        jnp.bfloat16
    )
    return (values, result)


def layer_backward(current, incoming, gains, value_matrix, output_matrix):
    widened, inverse, normed = norm_parts(current, gains)
    dvalues = jnp.dot(incoming, output_matrix.T, preferred_element_type=jnp.float32).astype(
        jnp.bfloat16
    )
    dnormed = jnp.dot(dvalues, value_matrix.T, preferred_element_type=jnp.float32) * gains
    centred = widened * inverse
    through = inverse * (dnormed - centred * jnp.mean(dnormed * centred, axis=-1, keepdims=True))
    before = (incoming.astype(jnp.float32) + through).astype(jnp.bfloat16)
    return (normed, dvalues, before)


def example_sums(left, right, seq_len):
    first = left.reshape(-1, seq_len, left.shape[-1])
    second = right.reshape(-1, seq_len, right.shape[-1])
    gram_first = jnp.einsum("eth,esh->ets", first, first, preferred_element_type=jnp.float32)
    gram_second = jnp.einsum("eth,esh->ets", second, second, preferred_element_type=jnp.float32)
    return jnp.sum(gram_first * gram_second, axis=(1, 2))


TILE = 256


def chain_kernel(
    sections,
    seed_ref, cot_ref, gain_ref, wv_ref, wo_ref,
    kin_ref, kval_ref, kgrad_ref, kdv_ref,
    fbuf, fres, bbuf, bres, work, fsend, frecv, bsend, brecv,
):
    place = lax.axis_index("section")
    micro_count, rows, width = seed_ref.shape
    heads = wv_ref.shape[1]
    ahead = lax.rem(place + 1, sections)
    behind = lax.rem(place + sections - 1, sections)
    first = place == 0
    last = place == sections - 1

    barrier = pltpu.get_barrier_semaphore()

    @pl.when(place > 0)
    def _():
        pl.semaphore_signal(barrier, inc=1, device_id={"section": behind}, device_id_type=pl.DeviceIdType.MESH)

    @pl.when(place < sections - 1)
    def _():
        pl.semaphore_signal(barrier, inc=1, device_id={"section": ahead}, device_id_type=pl.DeviceIdType.MESH)

    peers = (place + sections - 1) // sections + (2 * sections - 2 - place) // sections
    pl.semaphore_wait(barrier, peers)

    @pl.when(first)
    def _():
        fbuf[...] = seed_ref[...]

    @pl.when(last)
    def _():
        bbuf[...] = cot_ref[...]

    def forward_copy(m):
        return pltpu.make_async_remote_copy(
            src_ref=fres.at[m], dst_ref=fbuf.at[m], send_sem=fsend.at[m], recv_sem=frecv.at[m],
            device_id={"section": ahead}, device_id_type=pl.DeviceIdType.MESH,
        )

    def backward_copy(m):
        return pltpu.make_async_remote_copy(
            src_ref=bres.at[m], dst_ref=bbuf.at[m], send_sem=bsend.at[m], recv_sem=brecv.at[m],
            device_id={"section": behind}, device_id_type=pl.DeviceIdType.MESH,
        )

    def columns(i):
        return pl.ds(pl.multiple_of(i * TILE, TILE), TILE)

    for m in range(micro_count):
        @pl.when(place > 0)
        def _():
            forward_copy(m).wait_recv()

        x = fbuf[m]
        kin_ref[m] = x
        wide = x.astype(jnp.float32)
        inverse = lax.rsqrt(jnp.mean(wide * wide, axis=-1, keepdims=True) + 1e-06)
        normed = (wide * inverse * gain_ref[...]).astype(jnp.bfloat16)

        def value_tile(i, carry):
            kval_ref[m, :, columns(i)] = jnp.dot(
                normed, wv_ref[:, columns(i)], preferred_element_type=jnp.float32
            ).astype(jnp.bfloat16)
            return carry

        lax.fori_loop(0, heads // TILE, value_tile, 0)
        values = kval_ref[m]

        def result_tile(i, carry):
            fres[m, :, columns(i)] = (
                fbuf[m, :, columns(i)].astype(jnp.float32)
                + jnp.dot(values, wo_ref[:, columns(i)], preferred_element_type=jnp.float32)
            ).astype(jnp.bfloat16)
            return carry

        lax.fori_loop(0, width // TILE, result_tile, 0)

        @pl.when(place < sections - 1)
        def _():
            forward_copy(m).start()

    contract = (((1,), (1,)), ((), ()))
    for m in range(micro_count):
        @pl.when(place < sections - 1)
        def _():
            backward_copy(m).wait_recv()

        grad = bbuf[m]
        kgrad_ref[m] = grad

        def dvalue_tile(i, carry):
            kdv_ref[m, :, columns(i)] = lax.dot_general(
                grad, wo_ref[columns(i), :], contract, preferred_element_type=jnp.float32
            ).astype(jnp.bfloat16)
            return carry

        lax.fori_loop(0, heads // TILE, dvalue_tile, 0)
        dvalues = kdv_ref[m]

        def dnormed_tile(i, carry):
            work[:, columns(i)] = lax.dot_general(
                dvalues, wv_ref[columns(i), :], contract, preferred_element_type=jnp.float32
            ) * gain_ref[:, columns(i)]
            return carry

        lax.fori_loop(0, width // TILE, dnormed_tile, 0)
        wide = kin_ref[m].astype(jnp.float32)
        inverse = lax.rsqrt(jnp.mean(wide * wide, axis=-1, keepdims=True) + 1e-06)
        dnormed = work[...]
        centred = wide * inverse
        through = inverse * (dnormed - centred * jnp.mean(dnormed * centred, axis=-1, keepdims=True))
        bres[m] = (grad.astype(jnp.float32) + through).astype(jnp.bfloat16)

        @pl.when(place > 0)
        def _():
            backward_copy(m).start()

    for m in range(micro_count):
        @pl.when(place < sections - 1)
        def _():
            forward_copy(m).wait_send()

        @pl.when(place > 0)
        def _():
            backward_copy(m).wait_send()


def run_chain(feed_rows, cot_rows, gains, value_matrix, output_matrix):
    sections = lax.axis_size("section")
    micro_count, rows, width = feed_rows.shape
    heads = value_matrix.shape[1]
    vmem = pl.BlockSpec(memory_space=pltpu.VMEM)
    act = jax.ShapeDtypeStruct((micro_count, rows, width), jnp.bfloat16)
    head_act = jax.ShapeDtypeStruct((micro_count, rows, heads), jnp.bfloat16)
    return pl.pallas_call(
        functools.partial(chain_kernel, sections),
        out_shape=(act, head_act, act, head_act),
        in_specs=[vmem] * 5,
        out_specs=(vmem,) * 4,
        scratch_shapes=[
            pltpu.VMEM((micro_count, rows, width), jnp.bfloat16),
            pltpu.VMEM((micro_count, rows, width), jnp.bfloat16),
            pltpu.VMEM((micro_count, rows, width), jnp.bfloat16),
            pltpu.VMEM((micro_count, rows, width), jnp.bfloat16),
            pltpu.VMEM((rows, width), jnp.float32),
            pltpu.SemaphoreType.DMA((micro_count,)),
            pltpu.SemaphoreType.DMA((micro_count,)),
            pltpu.SemaphoreType.DMA((micro_count,)),
            pltpu.SemaphoreType.DMA((micro_count,)),
        ],
        compiler_params=pltpu.CompilerParams(
            collective_id=0, has_side_effects=True, vmem_limit_bytes=48 * 1024 * 1024
        ),
    )(feed_rows, cot_rows, gains.reshape(1, width), value_matrix, output_matrix)


def gather_kernel(ys, zs, wv_ref, wo_ref, wv_all, wo_all, own_sem, va_send, va_recv, vb_send, vb_recv, oa_send, oa_recv, ob_send, ob_recv):
    y = lax.axis_index("y")
    z = lax.axis_index("z")
    mesh_ids = pl.DeviceIdType.MESH
    barrier = pltpu.get_barrier_semaphore()
    for k in range(1, zs):
        pl.semaphore_signal(barrier, inc=1, device_id={"z": lax.rem(z + k, zs)}, device_id_type=mesh_ids)
    for k in range(1, ys):
        pl.semaphore_signal(barrier, inc=1, device_id={"y": lax.rem(y + k, ys)}, device_id_type=mesh_ids)
    pl.semaphore_wait(barrier, zs + ys - 2)

    own_v = pltpu.make_async_copy(wv_ref, wv_all.at[y, z], own_sem.at[0])
    own_o = pltpu.make_async_copy(wo_ref, wo_all.at[y, z], own_sem.at[1])
    own_v.start()
    own_o.start()

    def v_first(k, target):
        return pltpu.make_async_remote_copy(
            src_ref=wv_ref, dst_ref=wv_all.at[y, z], send_sem=va_send.at[k - 1],
            recv_sem=va_recv.at[k - 1], device_id={"z": target}, device_id_type=mesh_ids,
        )

    def o_first(k, target):
        return pltpu.make_async_remote_copy(
            src_ref=wo_ref, dst_ref=wo_all.at[y, z], send_sem=oa_send.at[k - 1],
            recv_sem=oa_recv.at[k - 1], device_id={"y": target}, device_id_type=mesh_ids,
        )

    def v_second(k, row, target):
        return pltpu.make_async_remote_copy(
            src_ref=wv_all.at[pl.ds(row, 1)], dst_ref=wv_all.at[pl.ds(row, 1)],
            send_sem=vb_send.at[k - 1], recv_sem=vb_recv.at[k - 1],
            device_id={"y": target}, device_id_type=mesh_ids,
        )

    def o_second(k, column, target):
        return pltpu.make_async_remote_copy(
            src_ref=wo_all.at[:, pl.ds(column, 1)], dst_ref=wo_all.at[:, pl.ds(column, 1)],
            send_sem=ob_send.at[k - 1], recv_sem=ob_recv.at[k - 1],
            device_id={"z": target}, device_id_type=mesh_ids,
        )

    for k in range(1, zs):
        v_first(k, lax.rem(z + k, zs)).start()
    for k in range(1, ys):
        o_first(k, lax.rem(y + k, ys)).start()
    own_v.wait()
    own_o.wait()
    for k in range(1, zs):
        pltpu.make_async_remote_copy(
            src_ref=wv_ref, dst_ref=wv_all.at[y, lax.rem(z + zs - k, zs)], send_sem=va_send.at[k - 1],
            recv_sem=va_recv.at[k - 1], device_id={"z": z}, device_id_type=mesh_ids,
        ).wait_recv()
    for k in range(1, ys):
        pltpu.make_async_remote_copy(
            src_ref=wo_ref, dst_ref=wo_all.at[lax.rem(y + ys - k, ys), z], send_sem=oa_send.at[k - 1],
            recv_sem=oa_recv.at[k - 1], device_id={"y": y}, device_id_type=mesh_ids,
        ).wait_recv()
    for k in range(1, ys):
        v_second(k, y, lax.rem(y + k, ys)).start()
    for k in range(1, zs):
        o_second(k, z, lax.rem(z + k, zs)).start()
    for k in range(1, zs):
        v_first(k, lax.rem(z + k, zs)).wait_send()
    for k in range(1, ys):
        o_first(k, lax.rem(y + k, ys)).wait_send()
    for k in range(1, ys):
        v_second(k, lax.rem(y + ys - k, ys), y).wait_recv()
    for k in range(1, zs):
        o_second(k, lax.rem(z + zs - k, zs), z).wait_recv()
    for k in range(1, ys):
        v_second(k, y, lax.rem(y + k, ys)).wait_send()
    for k in range(1, zs):
        o_second(k, z, lax.rem(z + k, zs)).wait_send()


def gather_weights(value_shard, output_shard):
    ys = lax.axis_size("y")
    zs = lax.axis_size("z")
    anywhere = pl.BlockSpec(memory_space=pl.ANY)
    wv_all, wo_all = pl.pallas_call(
        functools.partial(gather_kernel, ys, zs),
        out_shape=(
            jax.ShapeDtypeStruct((ys, zs) + value_shard.shape, value_shard.dtype),
            jax.ShapeDtypeStruct((ys, zs) + output_shard.shape, output_shard.dtype),
        ),
        in_specs=[anywhere] * 2,
        out_specs=(anywhere, anywhere),
        scratch_shapes=[pltpu.SemaphoreType.DMA((2,))]
        + [pltpu.SemaphoreType.DMA((zs - 1,))] * 2
        + [pltpu.SemaphoreType.DMA((ys - 1,))] * 2
        + [pltpu.SemaphoreType.DMA((ys - 1,))] * 2
        + [pltpu.SemaphoreType.DMA((zs - 1,))] * 2,
        compiler_params=pltpu.CompilerParams(collective_id=1, has_side_effects=True),
    )(value_shard, output_shard)
    return (
        wv_all.reshape((-1,) + value_shard.shape[1:]),
        wo_all.reshape((-1,) + output_shard.shape[1:]),
    )


DP = ("y", "z")


def scatter_in_stages(block):
    inner = lax.psum_scatter(block, "y", scatter_dimension=0, tiled=True)
    return lax.psum_scatter(inner, "z", scatter_dimension=0, tiled=True).astype(jnp.float32)


def scatter_by_exchange(block):
    count = lax.axis_size(DP)
    parts = block.reshape((count, block.shape[0] // count) + block.shape[1:])
    arrived = lax.all_to_all(parts, DP, 0, 0, tiled=False)
    return jnp.sum(arrived.astype(jnp.float32), axis=0)


def on_device(inputs, cotangent, value_weight, output_weight, norm_gain, value_noise, output_noise):
    micro_count, example_count, seq_len, feature_width = inputs.shape
    feed_rows = inputs.reshape(micro_count, example_count * seq_len, feature_width)
    cot_rows = cotangent.reshape(micro_count, example_count * seq_len, feature_width)
    value_matrix, output_matrix = gather_weights(value_weight[0], output_weight[0])
    head_width = value_matrix.shape[1]
    gains = norm_gain[0]
    kept_inputs, kept_values, kept_grads, kept_dvalues = run_chain(
        feed_rows, cot_rows, gains, value_matrix, output_matrix
    )
    unused_wide, unused_inverse, normed_rows = norm_parts(
        kept_inputs.reshape(-1, feature_width), gains
    )
    normed_kept = normed_rows.reshape(kept_inputs.shape)
    partial_squares = jnp.stack(
        [
            example_sums(normed_kept[m], kept_dvalues[m], seq_len)
            + example_sums(kept_values[m], kept_grads[m], seq_len)
            for m in range(micro_count)
        ]
    )
    total_squares = lax.psum(partial_squares, "section")
    clip_weight = 1.0 / (jnp.sqrt(total_squares) + 0.01)
    token_weight = jnp.repeat(clip_weight, seq_len, axis=1)[:, :, None]
    scaled_dvalues = (
        (kept_dvalues.astype(jnp.float32) * token_weight)
        .astype(jnp.bfloat16)
        .reshape(-1, head_width)
    )
    scaled_grads = (
        (kept_grads.astype(jnp.float32) * token_weight)
        .astype(jnp.bfloat16)
        .reshape(-1, feature_width)
    )
    value_rows = kept_values.reshape(-1, head_width)
    columns = normed_rows
    value_part = scatter_in_stages(
        lax.dot_general(
            columns, scaled_dvalues, (((0,), (0,)), ((), ())), preferred_element_type=jnp.float32
        ).astype(jnp.bfloat16)
    )
    columns = value_rows
    output_part = scatter_by_exchange(
        lax.dot_general(
            columns, scaled_grads, (((0,), (0,)), ((), ())), preferred_element_type=jnp.float32
        ).astype(jnp.bfloat16)
    )
    grad_scale = math.sqrt(feature_width * head_width)
    value_grad = (value_part * grad_scale + value_noise[0])[None]
    output_grad = (output_part * grad_scale + output_noise[0])[None]
    return (value_grad, output_grad)


def split_dp(mesh):
    devices = mesh.devices
    sections, count = devices.shape
    try:
        across = len({d.coords[1] for d in devices[0]})
    except (AttributeError, IndexError, TypeError):
        across = 1
    if across < 1 or count % across:
        across = 1
    return Mesh(devices.reshape(sections, across, count // across), ("section",) + DP)


def solution(mesh):
    grid = split_dp(mesh)
    return jax.shard_map(
        on_device,
        mesh=grid,
        in_specs=(
            P(None, DP, None, None),
            P(None, DP, None, None),
            P("section", DP, None),
            P("section", DP, None),
            P("section", None),
            P("section", DP, None),
            P("section", DP, None),
        ),
        out_specs=(P("section", DP, None), P("section", DP, None)),
        check_vma=False,
    )
```

```python
import functools
import math

import jax
import jax.numpy as jnp
from jax import lax
from jax.experimental import pallas as pl
from jax.experimental.pallas import tpu as pltpu
from jax.sharding import Mesh, PartitionSpec as P


def norm_parts(current, gains):
    widened = current.astype(jnp.float32)
    inverse = lax.rsqrt(jnp.mean(widened * widened, axis=-1, keepdims=True) + 1e-06)
    normed = (widened * inverse * gains).astype(jnp.bfloat16)
    return (widened, inverse, normed)


def layer_forward(current, gains, value_matrix, output_matrix):
    widened, inverse, normed = norm_parts(current, gains)
    values = jnp.dot(normed, value_matrix, preferred_element_type=jnp.float32).astype(jnp.bfloat16)
    result = (widened + jnp.dot(values, output_matrix, preferred_element_type=jnp.float32)).astype(
        jnp.bfloat16
    )
    return (values, result)


def layer_backward(current, incoming, gains, value_matrix, output_matrix):
    widened, inverse, normed = norm_parts(current, gains)
    dvalues = jnp.dot(incoming, output_matrix.T, preferred_element_type=jnp.float32).astype(
        jnp.bfloat16
    )
    dnormed = jnp.dot(dvalues, value_matrix.T, preferred_element_type=jnp.float32) * gains
    centred = widened * inverse
    through = inverse * (dnormed - centred * jnp.mean(dnormed * centred, axis=-1, keepdims=True))
    before = (incoming.astype(jnp.float32) + through).astype(jnp.bfloat16)
    return (normed, dvalues, before)


def example_sums(left, right, seq_len):
    first = left.reshape(-1, seq_len, left.shape[-1])
    second = right.reshape(-1, seq_len, right.shape[-1])
    gram_first = jnp.einsum("eth,esh->ets", first, first, preferred_element_type=jnp.float32)
    gram_second = jnp.einsum("eth,esh->ets", second, second, preferred_element_type=jnp.float32)
    return jnp.sum(gram_first * gram_second, axis=(1, 2))


TILE = 256


def chain_kernel(
    sections,
    seed_ref, cot_ref, gain_ref, wv_ref, wo_ref,
    kin_ref, kval_ref, kgrad_ref, kdv_ref,
    fbuf, fres, bbuf, bres, work, fsend, frecv, bsend, brecv,
):
    place = lax.axis_index("section")
    micro_count, rows, width = seed_ref.shape
    heads = wv_ref.shape[1]
    ahead = lax.rem(place + 1, sections)
    behind = lax.rem(place + sections - 1, sections)
    first = place == 0
    last = place == sections - 1

    barrier = pltpu.get_barrier_semaphore()

    @pl.when(place > 0)
    def _():
        pl.semaphore_signal(barrier, inc=1, device_id={"section": behind}, device_id_type=pl.DeviceIdType.MESH)

    @pl.when(place < sections - 1)
    def _():
        pl.semaphore_signal(barrier, inc=1, device_id={"section": ahead}, device_id_type=pl.DeviceIdType.MESH)

    peers = (place + sections - 1) // sections + (2 * sections - 2 - place) // sections
    pl.semaphore_wait(barrier, peers)

    @pl.when(first)
    def _():
        fbuf[...] = seed_ref[...]

    @pl.when(last)
    def _():
        bbuf[...] = cot_ref[...]

    def forward_copy(m):
        return pltpu.make_async_remote_copy(
            src_ref=fres.at[m], dst_ref=fbuf.at[m], send_sem=fsend.at[m], recv_sem=frecv.at[m],
            device_id={"section": ahead}, device_id_type=pl.DeviceIdType.MESH,
        )

    def backward_copy(m):
        return pltpu.make_async_remote_copy(
            src_ref=bres.at[m], dst_ref=bbuf.at[m], send_sem=bsend.at[m], recv_sem=brecv.at[m],
            device_id={"section": behind}, device_id_type=pl.DeviceIdType.MESH,
        )

    def columns(i):
        return pl.ds(pl.multiple_of(i * TILE, TILE), TILE)

    for m in range(micro_count):
        @pl.when(place > 0)
        def _():
            forward_copy(m).wait_recv()

        x = fbuf[m]
        kin_ref[m] = x
        wide = x.astype(jnp.float32)
        inverse = lax.rsqrt(jnp.mean(wide * wide, axis=-1, keepdims=True) + 1e-06)
        normed = (wide * inverse * gain_ref[...]).astype(jnp.bfloat16)

        def value_tile(i, carry):
            kval_ref[m, :, columns(i)] = jnp.dot(
                normed, wv_ref[:, columns(i)], preferred_element_type=jnp.float32
            ).astype(jnp.bfloat16)
            return carry

        lax.fori_loop(0, heads // TILE, value_tile, 0)
        values = kval_ref[m]

        def result_tile(i, carry):
            fres[m, :, columns(i)] = (
                fbuf[m, :, columns(i)].astype(jnp.float32)
                + jnp.dot(values, wo_ref[:, columns(i)], preferred_element_type=jnp.float32)
            ).astype(jnp.bfloat16)
            return carry

        lax.fori_loop(0, width // TILE, result_tile, 0)

        @pl.when(place < sections - 1)
        def _():
            forward_copy(m).start()

    contract = (((1,), (1,)), ((), ()))
    for m in range(micro_count):
        @pl.when(place < sections - 1)
        def _():
            backward_copy(m).wait_recv()

        grad = bbuf[m]
        kgrad_ref[m] = grad

        def dvalue_tile(i, carry):
            kdv_ref[m, :, columns(i)] = lax.dot_general(
                grad, wo_ref[columns(i), :], contract, preferred_element_type=jnp.float32
            ).astype(jnp.bfloat16)
            return carry

        lax.fori_loop(0, heads // TILE, dvalue_tile, 0)
        dvalues = kdv_ref[m]

        def dnormed_tile(i, carry):
            work[:, columns(i)] = lax.dot_general(
                dvalues, wv_ref[columns(i), :], contract, preferred_element_type=jnp.float32
            ) * gain_ref[:, columns(i)]
            return carry

        lax.fori_loop(0, width // TILE, dnormed_tile, 0)
        wide = kin_ref[m].astype(jnp.float32)
        inverse = lax.rsqrt(jnp.mean(wide * wide, axis=-1, keepdims=True) + 1e-06)
        dnormed = work[...]
        centred = wide * inverse
        through = inverse * (dnormed - centred * jnp.mean(dnormed * centred, axis=-1, keepdims=True))
        bres[m] = (grad.astype(jnp.float32) + through).astype(jnp.bfloat16)

        @pl.when(place > 0)
        def _():
            backward_copy(m).start()

    for m in range(micro_count):
        @pl.when(place < sections - 1)
        def _():
            forward_copy(m).wait_send()

        @pl.when(place > 0)
        def _():
            backward_copy(m).wait_send()


def run_chain(feed_rows, cot_rows, gains, value_matrix, output_matrix):
    sections = lax.axis_size("section")
    micro_count, rows, width = feed_rows.shape
    heads = value_matrix.shape[1]
    vmem = pl.BlockSpec(memory_space=pltpu.VMEM)
    act = jax.ShapeDtypeStruct((micro_count, rows, width), jnp.bfloat16)
    head_act = jax.ShapeDtypeStruct((micro_count, rows, heads), jnp.bfloat16)
    return pl.pallas_call(
        functools.partial(chain_kernel, sections),
        out_shape=(act, head_act, act, head_act),
        in_specs=[vmem] * 5,
        out_specs=(vmem,) * 4,
        scratch_shapes=[
            pltpu.VMEM((micro_count, rows, width), jnp.bfloat16),
            pltpu.VMEM((micro_count, rows, width), jnp.bfloat16),
            pltpu.VMEM((micro_count, rows, width), jnp.bfloat16),
            pltpu.VMEM((micro_count, rows, width), jnp.bfloat16),
            pltpu.VMEM((rows, width), jnp.float32),
            pltpu.SemaphoreType.DMA((micro_count,)),
            pltpu.SemaphoreType.DMA((micro_count,)),
            pltpu.SemaphoreType.DMA((micro_count,)),
            pltpu.SemaphoreType.DMA((micro_count,)),
        ],
        compiler_params=pltpu.CompilerParams(
            collective_id=0, has_side_effects=True, vmem_limit_bytes=48 * 1024 * 1024
        ),
    )(feed_rows, cot_rows, gains.reshape(1, width), value_matrix, output_matrix)


def ring_copies(window, first_src, z, zs, sems):
    mesh_ids = pl.DeviceIdType.MESH
    right_send, right_recv, left_send, left_recv = sems
    rights, lefts = zs // 2, (zs - 1) // 2

    def right(t):
        slot = lax.rem(z + zs - t, zs)
        return pltpu.make_async_remote_copy(
            src_ref=first_src if t == 0 else window(slot), dst_ref=window(slot),
            send_sem=right_send.at[t], recv_sem=right_recv.at[t],
            device_id={"z": lax.rem(z + 1, zs)}, device_id_type=mesh_ids,
        )

    def left(t):
        slot = lax.rem(z + t, zs)
        return pltpu.make_async_remote_copy(
            src_ref=first_src if t == 0 else window(slot), dst_ref=window(slot),
            send_sem=left_send.at[t], recv_sem=left_recv.at[t],
            device_id={"z": lax.rem(z + zs - 1, zs)}, device_id_type=mesh_ids,
        )

    def right_in(t):
        return pltpu.make_async_remote_copy(
            src_ref=first_src, dst_ref=window(lax.rem(z + 2 * zs - 1 - t, zs)),
            send_sem=right_send.at[t], recv_sem=right_recv.at[t],
            device_id={"z": z}, device_id_type=mesh_ids,
        )

    def left_in(t):
        return pltpu.make_async_remote_copy(
            src_ref=first_src, dst_ref=window(lax.rem(z + 1 + t, zs)),
            send_sem=left_send.at[t], recv_sem=left_recv.at[t],
            device_id={"z": z}, device_id_type=mesh_ids,
        )

    def run():
        for t in range(rights):
            right(t).start()
            if t < lefts:
                left(t).start()
            right_in(t).wait_recv()
            if t < lefts:
                left_in(t).wait_recv()

    def finish():
        for t in range(rights):
            right(t).wait_send()
        for t in range(lefts):
            left(t).wait_send()

    return run, finish


def gather_kernel(ys, zs, wv_ref, wo_ref, wv_all, wo_all, own_sem, va, vb_send, vb_recv, oa_send, oa_recv, ob):
    y = lax.axis_index("y")
    z = lax.axis_index("z")
    mesh_ids = pl.DeviceIdType.MESH
    barrier = pltpu.get_barrier_semaphore()
    pl.semaphore_signal(barrier, inc=1, device_id={"z": lax.rem(z + 1, zs)}, device_id_type=mesh_ids)
    pl.semaphore_signal(barrier, inc=1, device_id={"z": lax.rem(z + zs - 1, zs)}, device_id_type=mesh_ids)
    for k in range(1, ys):
        pl.semaphore_signal(barrier, inc=1, device_id={"y": lax.rem(y + k, ys)}, device_id_type=mesh_ids)
    pl.semaphore_wait(barrier, ys + 1)

    own_v = pltpu.make_async_copy(wv_ref, wv_all.at[y, z], own_sem.at[0])
    own_o = pltpu.make_async_copy(wo_ref, wo_all.at[y, z], own_sem.at[1])
    own_v.start()
    own_o.start()

    def o_first(k, target):
        return pltpu.make_async_remote_copy(
            src_ref=wo_ref, dst_ref=wo_all.at[y, z], send_sem=oa_send.at[k - 1],
            recv_sem=oa_recv.at[k - 1], device_id={"y": target}, device_id_type=mesh_ids,
        )

    def o_first_in(k):
        return pltpu.make_async_remote_copy(
            src_ref=wo_ref, dst_ref=wo_all.at[lax.rem(y + ys - k, ys), z], send_sem=oa_send.at[k - 1],
            recv_sem=oa_recv.at[k - 1], device_id={"y": y}, device_id_type=mesh_ids,
        )

    def v_second(k, row, target):
        return pltpu.make_async_remote_copy(
            src_ref=wv_all.at[pl.ds(row, 1)], dst_ref=wv_all.at[pl.ds(row, 1)],
            send_sem=vb_send.at[k - 1], recv_sem=vb_recv.at[k - 1],
            device_id={"y": target}, device_id_type=mesh_ids,
        )

    for k in range(1, ys):
        o_first(k, lax.rem(y + k, ys)).start()
    v_ring, v_ring_done = ring_copies(lambda o: wv_all.at[y, o], wv_ref, z, zs, va)
    v_ring()
    own_v.wait()
    own_o.wait()
    for k in range(1, ys):
        o_first_in(k).wait_recv()
    for k in range(1, ys):
        v_second(k, y, lax.rem(y + k, ys)).start()
    o_ring, o_ring_done = ring_copies(
        lambda o: wo_all.at[:, pl.ds(o, 1)], wo_all.at[:, pl.ds(z, 1)], z, zs, ob
    )
    o_ring()
    v_ring_done()
    for k in range(1, ys):
        o_first(k, lax.rem(y + k, ys)).wait_send()
    for k in range(1, ys):
        v_second(k, lax.rem(y + ys - k, ys), y).wait_recv()
    o_ring_done()
    for k in range(1, ys):
        v_second(k, y, lax.rem(y + k, ys)).wait_send()


def gather_weights(value_shard, output_shard):
    ys = lax.axis_size("y")
    zs = lax.axis_size("z")
    anywhere = pl.BlockSpec(memory_space=pl.ANY)
    ring_sems = [
        pltpu.SemaphoreType.DMA((zs // 2,)),
        pltpu.SemaphoreType.DMA((zs // 2,)),
        pltpu.SemaphoreType.DMA((max((zs - 1) // 2, 1),)),
        pltpu.SemaphoreType.DMA((max((zs - 1) // 2, 1),)),
    ]
    wv_all, wo_all = pl.pallas_call(
        functools.partial(gather_kernel, ys, zs),
        out_shape=(
            jax.ShapeDtypeStruct((ys, zs) + value_shard.shape, value_shard.dtype),
            jax.ShapeDtypeStruct((ys, zs) + output_shard.shape, output_shard.dtype),
        ),
        in_specs=[anywhere] * 2,
        out_specs=(anywhere, anywhere),
        scratch_shapes=[pltpu.SemaphoreType.DMA((2,)), ring_sems]
        + [pltpu.SemaphoreType.DMA((ys - 1,))] * 4
        + [ring_sems],
        compiler_params=pltpu.CompilerParams(collective_id=1, has_side_effects=True),
    )(value_shard, output_shard)
    return (
        wv_all.reshape((-1,) + value_shard.shape[1:]),
        wo_all.reshape((-1,) + output_shard.shape[1:]),
    )


DP = ("y", "z")


def scatter_in_stages(block):
    inner = lax.psum_scatter(block, "y", scatter_dimension=0, tiled=True)
    return lax.psum_scatter(inner, "z", scatter_dimension=0, tiled=True).astype(jnp.float32)


def scatter_by_exchange(block):
    count = lax.axis_size(DP)
    parts = block.reshape((count, block.shape[0] // count) + block.shape[1:])
    arrived = lax.all_to_all(parts, DP, 0, 0, tiled=False)
    return jnp.sum(arrived.astype(jnp.float32), axis=0)


def on_device(inputs, cotangent, value_weight, output_weight, norm_gain, value_noise, output_noise):
    micro_count, example_count, seq_len, feature_width = inputs.shape
    feed_rows = inputs.reshape(micro_count, example_count * seq_len, feature_width)
    cot_rows = cotangent.reshape(micro_count, example_count * seq_len, feature_width)
    value_matrix, output_matrix = gather_weights(value_weight[0], output_weight[0])
    head_width = value_matrix.shape[1]
    gains = norm_gain[0]
    kept_inputs, kept_values, kept_grads, kept_dvalues = run_chain(
        feed_rows, cot_rows, gains, value_matrix, output_matrix
    )
    unused_wide, unused_inverse, normed_rows = norm_parts(
        kept_inputs.reshape(-1, feature_width), gains
    )
    normed_kept = normed_rows.reshape(kept_inputs.shape)
    partial_squares = jnp.stack(
        [
            example_sums(normed_kept[m], kept_dvalues[m], seq_len)
            + example_sums(kept_values[m], kept_grads[m], seq_len)
            for m in range(micro_count)
        ]
    )
    total_squares = lax.psum(partial_squares, "section")
    clip_weight = 1.0 / (jnp.sqrt(total_squares) + 0.01)
    token_weight = jnp.repeat(clip_weight, seq_len, axis=1)[:, :, None]
    scaled_dvalues = (
        (kept_dvalues.astype(jnp.float32) * token_weight)
        .astype(jnp.bfloat16)
        .reshape(-1, head_width)
    )
    scaled_grads = (
        (kept_grads.astype(jnp.float32) * token_weight)
        .astype(jnp.bfloat16)
        .reshape(-1, feature_width)
    )
    value_rows = kept_values.reshape(-1, head_width)
    columns = normed_rows
    value_part = scatter_in_stages(
        lax.dot_general(
            columns, scaled_dvalues, (((0,), (0,)), ((), ())), preferred_element_type=jnp.float32
        ).astype(jnp.bfloat16)
    )
    columns = value_rows
    output_part = scatter_by_exchange(
        lax.dot_general(
            columns, scaled_grads, (((0,), (0,)), ((), ())), preferred_element_type=jnp.float32
        ).astype(jnp.bfloat16)
    )
    grad_scale = math.sqrt(feature_width * head_width)
    value_grad = (value_part * grad_scale + value_noise[0])[None]
    output_grad = (output_part * grad_scale + output_noise[0])[None]
    return (value_grad, output_grad)


def split_dp(mesh):
    devices = mesh.devices
    sections, count = devices.shape
    try:
        across = len({d.coords[1] for d in devices[0]})
    except (AttributeError, IndexError, TypeError):
        across = 1
    if across < 1 or count % across:
        across = 1
    return Mesh(devices.reshape(sections, across, count // across), ("section",) + DP)


def solution(mesh):
    grid = split_dp(mesh)
    return jax.shard_map(
        on_device,
        mesh=grid,
        in_specs=(
            P(None, DP, None, None),
            P(None, DP, None, None),
            P("section", DP, None),
            P("section", DP, None),
            P("section", None),
            P("section", DP, None),
            P("section", DP, None),
        ),
        out_specs=(P("section", DP, None), P("section", DP, None)),
        check_vma=False,
    )
```

```python
import functools
import math

import jax
import jax.numpy as jnp
from jax import lax
from jax.experimental import pallas as pl
from jax.experimental.pallas import tpu as pltpu
from jax.sharding import Mesh, PartitionSpec as P


def norm_parts(current, gains):
    widened = current.astype(jnp.float32)
    inverse = lax.rsqrt(jnp.mean(widened * widened, axis=-1, keepdims=True) + 1e-06)
    normed = (widened * inverse * gains).astype(jnp.bfloat16)
    return (widened, inverse, normed)


def layer_forward(current, gains, value_matrix, output_matrix):
    widened, inverse, normed = norm_parts(current, gains)
    values = jnp.dot(normed, value_matrix, preferred_element_type=jnp.float32).astype(jnp.bfloat16)
    result = (widened + jnp.dot(values, output_matrix, preferred_element_type=jnp.float32)).astype(
        jnp.bfloat16
    )
    return (values, result)


def layer_backward(current, incoming, gains, value_matrix, output_matrix):
    widened, inverse, normed = norm_parts(current, gains)
    dvalues = jnp.dot(incoming, output_matrix.T, preferred_element_type=jnp.float32).astype(
        jnp.bfloat16
    )
    dnormed = jnp.dot(dvalues, value_matrix.T, preferred_element_type=jnp.float32) * gains
    centred = widened * inverse
    through = inverse * (dnormed - centred * jnp.mean(dnormed * centred, axis=-1, keepdims=True))
    before = (incoming.astype(jnp.float32) + through).astype(jnp.bfloat16)
    return (normed, dvalues, before)


def example_sums(left, right, seq_len):
    first = left.reshape(-1, seq_len, left.shape[-1])
    second = right.reshape(-1, seq_len, right.shape[-1])
    gram_first = jnp.einsum("eth,esh->ets", first, first, preferred_element_type=jnp.float32)
    gram_second = jnp.einsum("eth,esh->ets", second, second, preferred_element_type=jnp.float32)
    return jnp.sum(gram_first * gram_second, axis=(1, 2))


TILE = 256


def chain_kernel(
    sections,
    seed_ref, cot_ref, gain_ref, wv_ref, wo_ref,
    kin_ref, kval_ref, kgrad_ref, kdv_ref,
    fbuf, fres, bbuf, bres, work, fsend, frecv, bsend, brecv,
):
    place = lax.axis_index("section")
    micro_count, rows, width = seed_ref.shape
    heads = wv_ref.shape[1]
    ahead = lax.rem(place + 1, sections)
    behind = lax.rem(place + sections - 1, sections)
    first = place == 0
    last = place == sections - 1

    barrier = pltpu.get_barrier_semaphore()

    @pl.when(place > 0)
    def _():
        pl.semaphore_signal(barrier, inc=1, device_id={"section": behind}, device_id_type=pl.DeviceIdType.MESH)

    @pl.when(place < sections - 1)
    def _():
        pl.semaphore_signal(barrier, inc=1, device_id={"section": ahead}, device_id_type=pl.DeviceIdType.MESH)

    peers = (place + sections - 1) // sections + (2 * sections - 2 - place) // sections
    pl.semaphore_wait(barrier, peers)

    @pl.when(first)
    def _():
        fbuf[...] = seed_ref[...]

    @pl.when(last)
    def _():
        bbuf[...] = cot_ref[...]

    def forward_copy(m):
        return pltpu.make_async_remote_copy(
            src_ref=fres.at[m], dst_ref=fbuf.at[m], send_sem=fsend.at[m], recv_sem=frecv.at[m],
            device_id={"section": ahead}, device_id_type=pl.DeviceIdType.MESH,
        )

    def backward_copy(m):
        return pltpu.make_async_remote_copy(
            src_ref=bres.at[m], dst_ref=bbuf.at[m], send_sem=bsend.at[m], recv_sem=brecv.at[m],
            device_id={"section": behind}, device_id_type=pl.DeviceIdType.MESH,
        )

    def columns(i):
        return pl.ds(pl.multiple_of(i * TILE, TILE), TILE)

    for m in range(micro_count):
        @pl.when(place > 0)
        def _():
            forward_copy(m).wait_recv()

        x = fbuf[m]
        kin_ref[m] = x
        wide = x.astype(jnp.float32)
        inverse = lax.rsqrt(jnp.mean(wide * wide, axis=-1, keepdims=True) + 1e-06)
        normed = (wide * inverse * gain_ref[...]).astype(jnp.bfloat16)

        def value_tile(i, carry):
            kval_ref[m, :, columns(i)] = jnp.dot(
                normed, wv_ref[:, columns(i)], preferred_element_type=jnp.float32
            ).astype(jnp.bfloat16)
            return carry

        lax.fori_loop(0, heads // TILE, value_tile, 0)
        values = kval_ref[m]

        def result_tile(i, carry):
            fres[m, :, columns(i)] = (
                fbuf[m, :, columns(i)].astype(jnp.float32)
                + jnp.dot(values, wo_ref[:, columns(i)], preferred_element_type=jnp.float32)
            ).astype(jnp.bfloat16)
            return carry

        lax.fori_loop(0, width // TILE, result_tile, 0)

        @pl.when(place < sections - 1)
        def _():
            forward_copy(m).start()

    contract = (((1,), (1,)), ((), ()))
    for m in range(micro_count):
        @pl.when(place < sections - 1)
        def _():
            backward_copy(m).wait_recv()

        grad = bbuf[m]
        kgrad_ref[m] = grad

        def dvalue_tile(i, carry):
            kdv_ref[m, :, columns(i)] = lax.dot_general(
                grad, wo_ref[columns(i), :], contract, preferred_element_type=jnp.float32
            ).astype(jnp.bfloat16)
            return carry

        lax.fori_loop(0, heads // TILE, dvalue_tile, 0)
        dvalues = kdv_ref[m]

        def dnormed_tile(i, carry):
            work[:, columns(i)] = lax.dot_general(
                dvalues, wv_ref[columns(i), :], contract, preferred_element_type=jnp.float32
            ) * gain_ref[:, columns(i)]
            return carry

        lax.fori_loop(0, width // TILE, dnormed_tile, 0)
        wide = kin_ref[m].astype(jnp.float32)
        inverse = lax.rsqrt(jnp.mean(wide * wide, axis=-1, keepdims=True) + 1e-06)
        dnormed = work[...]
        centred = wide * inverse
        through = inverse * (dnormed - centred * jnp.mean(dnormed * centred, axis=-1, keepdims=True))
        bres[m] = (grad.astype(jnp.float32) + through).astype(jnp.bfloat16)

        @pl.when(place > 0)
        def _():
            backward_copy(m).start()

    for m in range(micro_count):
        @pl.when(place < sections - 1)
        def _():
            forward_copy(m).wait_send()

        @pl.when(place > 0)
        def _():
            backward_copy(m).wait_send()


def run_chain(feed_rows, cot_rows, gains, value_matrix, output_matrix):
    sections = lax.axis_size("section")
    micro_count, rows, width = feed_rows.shape
    heads = value_matrix.shape[1]
    vmem = pl.BlockSpec(memory_space=pltpu.VMEM)
    act = jax.ShapeDtypeStruct((micro_count, rows, width), jnp.bfloat16)
    head_act = jax.ShapeDtypeStruct((micro_count, rows, heads), jnp.bfloat16)
    return pl.pallas_call(
        functools.partial(chain_kernel, sections),
        out_shape=(act, head_act, act, head_act),
        in_specs=[vmem] * 5,
        out_specs=(vmem,) * 4,
        scratch_shapes=[
            pltpu.VMEM((micro_count, rows, width), jnp.bfloat16),
            pltpu.VMEM((micro_count, rows, width), jnp.bfloat16),
            pltpu.VMEM((micro_count, rows, width), jnp.bfloat16),
            pltpu.VMEM((micro_count, rows, width), jnp.bfloat16),
            pltpu.VMEM((rows, width), jnp.float32),
            pltpu.SemaphoreType.DMA((micro_count,)),
            pltpu.SemaphoreType.DMA((micro_count,)),
            pltpu.SemaphoreType.DMA((micro_count,)),
            pltpu.SemaphoreType.DMA((micro_count,)),
        ],
        compiler_params=pltpu.CompilerParams(
            collective_id=0, has_side_effects=True, vmem_limit_bytes=48 * 1024 * 1024
        ),
    )(feed_rows, cot_rows, gains.reshape(1, width), value_matrix, output_matrix)


def ring_copies(window, first_src, z, zs, sems):
    mesh_ids = pl.DeviceIdType.MESH
    right_send, right_recv, left_send, left_recv = sems
    rights, lefts = zs // 2, (zs - 1) // 2

    def right(t):
        slot = lax.rem(z + zs - t, zs)
        return pltpu.make_async_remote_copy(
            src_ref=first_src if t == 0 else window(slot), dst_ref=window(slot),
            send_sem=right_send.at[t], recv_sem=right_recv.at[t],
            device_id={"z": lax.rem(z + 1, zs)}, device_id_type=mesh_ids,
        )

    def left(t):
        slot = lax.rem(z + t, zs)
        return pltpu.make_async_remote_copy(
            src_ref=first_src if t == 0 else window(slot), dst_ref=window(slot),
            send_sem=left_send.at[t], recv_sem=left_recv.at[t],
            device_id={"z": lax.rem(z + zs - 1, zs)}, device_id_type=mesh_ids,
        )

    def right_in(t):
        return pltpu.make_async_remote_copy(
            src_ref=first_src, dst_ref=window(lax.rem(z + 2 * zs - 1 - t, zs)),
            send_sem=right_send.at[t], recv_sem=right_recv.at[t],
            device_id={"z": z}, device_id_type=mesh_ids,
        )

    def left_in(t):
        return pltpu.make_async_remote_copy(
            src_ref=first_src, dst_ref=window(lax.rem(z + 1 + t, zs)),
            send_sem=left_send.at[t], recv_sem=left_recv.at[t],
            device_id={"z": z}, device_id_type=mesh_ids,
        )

    def run():
        for t in range(rights):
            right(t).start()
            if t < lefts:
                left(t).start()
            right_in(t).wait_recv()
            if t < lefts:
                left_in(t).wait_recv()

    def finish():
        for t in range(rights):
            right(t).wait_send()
        for t in range(lefts):
            left(t).wait_send()

    return run, finish


def gather_kernel(ys, zs, wv_ref, wo_ref, wv_all, wo_all, own_sem, va, vb_send, vb_recv, oa_send, oa_recv, ob):
    y = lax.axis_index("y")
    z = lax.axis_index("z")
    mesh_ids = pl.DeviceIdType.MESH
    barrier = pltpu.get_barrier_semaphore()
    pl.semaphore_signal(barrier, inc=1, device_id={"z": lax.rem(z + 1, zs)}, device_id_type=mesh_ids)
    pl.semaphore_signal(barrier, inc=1, device_id={"z": lax.rem(z + zs - 1, zs)}, device_id_type=mesh_ids)
    for k in range(1, ys):
        pl.semaphore_signal(barrier, inc=1, device_id={"y": lax.rem(y + k, ys)}, device_id_type=mesh_ids)
    pl.semaphore_wait(barrier, ys + 1)

    own_v = pltpu.make_async_copy(wv_ref, wv_all.at[y, z], own_sem.at[0])
    own_o = pltpu.make_async_copy(wo_ref, wo_all.at[y, z], own_sem.at[1])
    own_v.start()
    own_o.start()

    def o_first(k, target):
        return pltpu.make_async_remote_copy(
            src_ref=wo_ref, dst_ref=wo_all.at[y, z], send_sem=oa_send.at[k - 1],
            recv_sem=oa_recv.at[k - 1], device_id={"y": target}, device_id_type=mesh_ids,
        )

    def o_first_in(k):
        return pltpu.make_async_remote_copy(
            src_ref=wo_ref, dst_ref=wo_all.at[lax.rem(y + ys - k, ys), z], send_sem=oa_send.at[k - 1],
            recv_sem=oa_recv.at[k - 1], device_id={"y": y}, device_id_type=mesh_ids,
        )

    def v_second(k, row, target):
        return pltpu.make_async_remote_copy(
            src_ref=wv_all.at[pl.ds(row, 1)], dst_ref=wv_all.at[pl.ds(row, 1)],
            send_sem=vb_send.at[k - 1], recv_sem=vb_recv.at[k - 1],
            device_id={"y": target}, device_id_type=mesh_ids,
        )

    for k in range(1, ys):
        o_first(k, lax.rem(y + k, ys)).start()
    v_ring, v_ring_done = ring_copies(lambda o: wv_all.at[y, o], wv_ref, z, zs, va)
    v_ring()
    own_v.wait()
    own_o.wait()
    for k in range(1, ys):
        o_first_in(k).wait_recv()
    for k in range(1, ys):
        v_second(k, y, lax.rem(y + k, ys)).start()
    o_ring, o_ring_done = ring_copies(
        lambda o: wo_all.at[:, pl.ds(o, 1)], wo_all.at[:, pl.ds(z, 1)], z, zs, ob
    )
    o_ring()
    v_ring_done()
    for k in range(1, ys):
        o_first(k, lax.rem(y + k, ys)).wait_send()
    for k in range(1, ys):
        v_second(k, lax.rem(y + ys - k, ys), y).wait_recv()
    o_ring_done()
    for k in range(1, ys):
        v_second(k, y, lax.rem(y + k, ys)).wait_send()


def gather_weights(value_shard, output_shard):
    ys = lax.axis_size("y")
    zs = lax.axis_size("z")
    anywhere = pl.BlockSpec(memory_space=pl.ANY)
    ring_sems = [
        pltpu.SemaphoreType.DMA((zs // 2,)),
        pltpu.SemaphoreType.DMA((zs // 2,)),
        pltpu.SemaphoreType.DMA((max((zs - 1) // 2, 1),)),
        pltpu.SemaphoreType.DMA((max((zs - 1) // 2, 1),)),
    ]
    wv_all, wo_all = pl.pallas_call(
        functools.partial(gather_kernel, ys, zs),
        out_shape=(
            jax.ShapeDtypeStruct((ys, zs) + value_shard.shape, value_shard.dtype),
            jax.ShapeDtypeStruct((ys, zs) + output_shard.shape, output_shard.dtype),
        ),
        in_specs=[anywhere] * 2,
        out_specs=(anywhere, anywhere),
        scratch_shapes=[pltpu.SemaphoreType.DMA((2,)), ring_sems]
        + [pltpu.SemaphoreType.DMA((ys - 1,))] * 4
        + [ring_sems],
        compiler_params=pltpu.CompilerParams(collective_id=1, has_side_effects=True),
    )(value_shard, output_shard)
    return (
        wv_all.reshape((-1,) + value_shard.shape[1:]),
        wo_all.reshape((-1,) + output_shard.shape[1:]),
    )


def ring_sum(get, z, zs, bufs, sems):
    mesh_ids = pl.DeviceIdType.MESH
    rsend, rrecv, lsend, lrecv = bufs
    rs_send, rs_recv, ls_send, ls_recv = sems
    rights, lefts = zs // 2, (zs - 1) // 2

    def right(t):
        return pltpu.make_async_remote_copy(
            src_ref=rsend.at[t], dst_ref=rrecv.at[t], send_sem=rs_send.at[t], recv_sem=rs_recv.at[t],
            device_id={"z": lax.rem(z + 1, zs)}, device_id_type=mesh_ids,
        )

    def left(t):
        return pltpu.make_async_remote_copy(
            src_ref=lsend.at[t], dst_ref=lrecv.at[t], send_sem=ls_send.at[t], recv_sem=ls_recv.at[t],
            device_id={"z": lax.rem(z + zs - 1, zs)}, device_id_type=mesh_ids,
        )

    for t in range(rights):
        value = get(lax.rem(z + rights - t, zs))
        if t > 0:
            value = value + rrecv[t - 1].astype(jnp.float32)
        rsend[t] = value.astype(rsend.dtype)
        right(t).start()
        if t < lefts:
            value = get(lax.rem(z + zs - lefts + t, zs))
            if t > 0:
                value = value + lrecv[t - 1].astype(jnp.float32)
            lsend[t] = value.astype(lsend.dtype)
            left(t).start()
        right(t).wait_recv()
        if t < lefts:
            left(t).wait_recv()
    total = get(z) + rrecv[rights - 1].astype(jnp.float32)
    if lefts > 0:
        total = total + lrecv[lefts - 1].astype(jnp.float32)

    def finish():
        for t in range(rights):
            right(t).wait_send()
        for t in range(lefts):
            left(t).wait_send()

    return total, finish


def direct_copies(source, landing, axis, me, count, send_sems, recv_sems):
    def copy(k):
        return pltpu.make_async_remote_copy(
            src_ref=source.at[lax.rem(me + k, count)], dst_ref=landing.at[k - 1],
            send_sem=send_sems.at[k - 1], recv_sem=recv_sems.at[k - 1],
            device_id={axis: lax.rem(me + k, count)}, device_id_type=pl.DeviceIdType.MESH,
        )

    return [copy(k) for k in range(1, count)]


def scatter_kernel(
    ys, zs, xv_ref, xo_ref, out_v, out_o,
    v_land, v_part, o_part, o_send, o_land, v_ring, o_ring, v_sems, o_sems, vd_send, vd_recv, od_send, od_recv,
):
    y = lax.axis_index("y")
    z = lax.axis_index("z")
    mesh_ids = pl.DeviceIdType.MESH
    barrier = pltpu.get_barrier_semaphore()
    pl.semaphore_signal(barrier, inc=1, device_id={"z": lax.rem(z + 1, zs)}, device_id_type=mesh_ids)
    pl.semaphore_signal(barrier, inc=1, device_id={"z": lax.rem(z + zs - 1, zs)}, device_id_type=mesh_ids)
    for k in range(1, ys):
        pl.semaphore_signal(barrier, inc=1, device_id={"y": lax.rem(y + k, ys)}, device_id_type=mesh_ids)
    pl.semaphore_wait(barrier, ys + 1)

    v_copies = direct_copies(xv_ref, v_land, "y", y, ys, vd_send, vd_recv)
    for c in v_copies:
        c.start()
    o_total, o_finish = ring_sum(lambda d: xo_ref[d].astype(jnp.float32), z, zs, o_ring, o_sems)
    o_part[...] = o_total
    o_send[...] = o_total.astype(o_send.dtype)
    o_copies = direct_copies(o_send, o_land, "y", y, ys, od_send, od_recv)
    for c in o_copies:
        c.start()
    v_sum = xv_ref[y].astype(jnp.float32)
    for k, c in enumerate(v_copies):
        c.wait_recv()
        v_sum = v_sum + v_land[k].astype(jnp.float32)
    v_part[...] = v_sum
    v_total, v_finish = ring_sum(lambda d: v_part[d], z, zs, v_ring, v_sems)
    out_v[...] = v_total
    o_sum = o_part[y]
    for k, c in enumerate(o_copies):
        c.wait_recv()
        o_sum = o_sum + o_land[k].astype(jnp.float32)
    out_o[...] = o_sum
    o_finish()
    v_finish()
    for c in v_copies + o_copies:
        c.wait_send()


def scatter_grads(value_block, output_block):
    ys = lax.axis_size("y")
    zs = lax.axis_size("z")
    rows_v, cols_v = value_block.shape
    rows_o, cols_o = output_block.shape
    v_rows = rows_v // (ys * zs)
    o_rows = rows_o // (ys * zs)
    xv = value_block.reshape(ys, zs, v_rows, cols_v)
    xo = output_block.reshape(ys, zs, o_rows, cols_o).transpose(1, 0, 2, 3)
    vmem = pl.BlockSpec(memory_space=pltpu.VMEM)
    rights, lefts = zs // 2, max((zs - 1) // 2, 1)
    bf = value_block.dtype

    def ring_space(block):
        return [
            pltpu.VMEM((rights,) + block, bf),
            pltpu.VMEM((rights,) + block, bf),
            pltpu.VMEM((lefts,) + block, bf),
            pltpu.VMEM((lefts,) + block, bf),
        ]

    ring_sems = [
        pltpu.SemaphoreType.DMA((rights,)),
        pltpu.SemaphoreType.DMA((rights,)),
        pltpu.SemaphoreType.DMA((lefts,)),
        pltpu.SemaphoreType.DMA((lefts,)),
    ]
    return pl.pallas_call(
        functools.partial(scatter_kernel, ys, zs),
        out_shape=(
            jax.ShapeDtypeStruct((v_rows, cols_v), jnp.float32),
            jax.ShapeDtypeStruct((o_rows, cols_o), jnp.float32),
        ),
        in_specs=[vmem, vmem],
        out_specs=(vmem, vmem),
        scratch_shapes=[
            pltpu.VMEM((ys - 1, zs, v_rows, cols_v), bf),
            pltpu.VMEM((zs, v_rows, cols_v), jnp.float32),
            pltpu.VMEM((ys, o_rows, cols_o), jnp.float32),
            pltpu.VMEM((ys, o_rows, cols_o), bf),
            pltpu.VMEM((ys - 1, o_rows, cols_o), bf),
            ring_space((v_rows, cols_v)),
            ring_space((ys, o_rows, cols_o)),
            ring_sems,
            ring_sems,
            pltpu.SemaphoreType.DMA((ys - 1,)),
            pltpu.SemaphoreType.DMA((ys - 1,)),
            pltpu.SemaphoreType.DMA((ys - 1,)),
            pltpu.SemaphoreType.DMA((ys - 1,)),
        ],
        compiler_params=pltpu.CompilerParams(
            collective_id=2, has_side_effects=True, vmem_limit_bytes=48 * 1024 * 1024
        ),
    )(xv, xo)


DP = ("y", "z")


def on_device(inputs, cotangent, value_weight, output_weight, norm_gain, value_noise, output_noise):
    micro_count, example_count, seq_len, feature_width = inputs.shape
    feed_rows = inputs.reshape(micro_count, example_count * seq_len, feature_width)
    cot_rows = cotangent.reshape(micro_count, example_count * seq_len, feature_width)
    value_matrix, output_matrix = gather_weights(value_weight[0], output_weight[0])
    head_width = value_matrix.shape[1]
    gains = norm_gain[0]
    kept_inputs, kept_values, kept_grads, kept_dvalues = run_chain(
        feed_rows, cot_rows, gains, value_matrix, output_matrix
    )
    unused_wide, unused_inverse, normed_rows = norm_parts(
        kept_inputs.reshape(-1, feature_width), gains
    )
    normed_kept = normed_rows.reshape(kept_inputs.shape)
    partial_squares = jnp.stack(
        [
            example_sums(normed_kept[m], kept_dvalues[m], seq_len)
            + example_sums(kept_values[m], kept_grads[m], seq_len)
            for m in range(micro_count)
        ]
    )
    total_squares = lax.psum(partial_squares, "section")
    clip_weight = 1.0 / (jnp.sqrt(total_squares) + 0.01)
    token_weight = jnp.repeat(clip_weight, seq_len, axis=1)[:, :, None]
    scaled_dvalues = (
        (kept_dvalues.astype(jnp.float32) * token_weight)
        .astype(jnp.bfloat16)
        .reshape(-1, head_width)
    )
    scaled_grads = (
        (kept_grads.astype(jnp.float32) * token_weight)
        .astype(jnp.bfloat16)
        .reshape(-1, feature_width)
    )
    value_rows = kept_values.reshape(-1, head_width)
    columns = normed_rows
    value_block = lax.dot_general(
        normed_rows, scaled_dvalues, (((0,), (0,)), ((), ())), preferred_element_type=jnp.float32
    ).astype(jnp.bfloat16)
    output_block = lax.dot_general(
        value_rows, scaled_grads, (((0,), (0,)), ((), ())), preferred_element_type=jnp.float32
    ).astype(jnp.bfloat16)
    value_part, output_part = scatter_grads(value_block, output_block)
    grad_scale = math.sqrt(feature_width * head_width)
    value_grad = (value_part * grad_scale + value_noise[0])[None]
    output_grad = (output_part * grad_scale + output_noise[0])[None]
    return (value_grad, output_grad)


def split_dp(mesh):
    devices = mesh.devices
    sections, count = devices.shape
    try:
        across = len({d.coords[1] for d in devices[0]})
    except (AttributeError, IndexError, TypeError):
        across = 1
    if across < 1 or count % across:
        across = 1
    return Mesh(devices.reshape(sections, across, count // across), ("section",) + DP)


def solution(mesh):
    grid = split_dp(mesh)
    return jax.shard_map(
        on_device,
        mesh=grid,
        in_specs=(
            P(None, DP, None, None),
            P(None, DP, None, None),
            P("section", DP, None),
            P("section", DP, None),
            P("section", None),
            P("section", DP, None),
            P("section", DP, None),
        ),
        out_specs=(P("section", DP, None), P("section", DP, None)),
        check_vma=False,
    )
```

```python
import functools
import math

import jax
import jax.numpy as jnp
from jax import lax
from jax.experimental import pallas as pl
from jax.experimental.pallas import tpu as pltpu
from jax.sharding import Mesh, PartitionSpec as P


def norm_parts(current, gains):
    widened = current.astype(jnp.float32)
    inverse = lax.rsqrt(jnp.mean(widened * widened, axis=-1, keepdims=True) + 1e-06)
    normed = (widened * inverse * gains).astype(jnp.bfloat16)
    return (widened, inverse, normed)


def layer_forward(current, gains, value_matrix, output_matrix):
    widened, inverse, normed = norm_parts(current, gains)
    values = jnp.dot(normed, value_matrix, preferred_element_type=jnp.float32).astype(jnp.bfloat16)
    result = (widened + jnp.dot(values, output_matrix, preferred_element_type=jnp.float32)).astype(
        jnp.bfloat16
    )
    return (values, result)


def layer_backward(current, incoming, gains, value_matrix, output_matrix):
    widened, inverse, normed = norm_parts(current, gains)
    dvalues = jnp.dot(incoming, output_matrix.T, preferred_element_type=jnp.float32).astype(
        jnp.bfloat16
    )
    dnormed = jnp.dot(dvalues, value_matrix.T, preferred_element_type=jnp.float32) * gains
    centred = widened * inverse
    through = inverse * (dnormed - centred * jnp.mean(dnormed * centred, axis=-1, keepdims=True))
    before = (incoming.astype(jnp.float32) + through).astype(jnp.bfloat16)
    return (normed, dvalues, before)


def example_sums(left, right, seq_len):
    first = left.reshape(-1, seq_len, left.shape[-1])
    second = right.reshape(-1, seq_len, right.shape[-1])
    gram_first = jnp.einsum("eth,esh->ets", first, first, preferred_element_type=jnp.float32)
    gram_second = jnp.einsum("eth,esh->ets", second, second, preferred_element_type=jnp.float32)
    return jnp.sum(gram_first * gram_second, axis=(1, 2))


TILE = 256


def chain_kernel(
    sections,
    seed_ref, cot_ref, gain_ref, wv_ref, wo_ref,
    kin_ref, kval_ref, kgrad_ref, kdv_ref,
    fbuf, fres, bbuf, bres, work, fsend, frecv, bsend, brecv,
):
    place = lax.axis_index("section")
    micro_count, rows, width = seed_ref.shape
    heads = wv_ref.shape[1]
    ahead = lax.rem(place + 1, sections)
    behind = lax.rem(place + sections - 1, sections)
    first = place == 0
    last = place == sections - 1

    barrier = pltpu.get_barrier_semaphore()

    @pl.when(place > 0)
    def _():
        pl.semaphore_signal(barrier, inc=1, device_id={"section": behind}, device_id_type=pl.DeviceIdType.MESH)

    @pl.when(place < sections - 1)
    def _():
        pl.semaphore_signal(barrier, inc=1, device_id={"section": ahead}, device_id_type=pl.DeviceIdType.MESH)

    peers = (place + sections - 1) // sections + (2 * sections - 2 - place) // sections
    pl.semaphore_wait(barrier, peers)

    @pl.when(first)
    def _():
        fbuf[...] = seed_ref[...]

    @pl.when(last)
    def _():
        bbuf[...] = cot_ref[...]

    def forward_copy(m):
        return pltpu.make_async_remote_copy(
            src_ref=fres.at[m], dst_ref=fbuf.at[m], send_sem=fsend.at[m], recv_sem=frecv.at[m],
            device_id={"section": ahead}, device_id_type=pl.DeviceIdType.MESH,
        )

    def backward_copy(m):
        return pltpu.make_async_remote_copy(
            src_ref=bres.at[m], dst_ref=bbuf.at[m], send_sem=bsend.at[m], recv_sem=brecv.at[m],
            device_id={"section": behind}, device_id_type=pl.DeviceIdType.MESH,
        )

    def columns(i):
        return pl.ds(pl.multiple_of(i * TILE, TILE), TILE)

    for m in range(micro_count):
        @pl.when(place > 0)
        def _():
            forward_copy(m).wait_recv()

        x = fbuf[m]
        kin_ref[m] = x
        wide = x.astype(jnp.float32)
        inverse = lax.rsqrt(jnp.mean(wide * wide, axis=-1, keepdims=True) + 1e-06)
        normed = (wide * inverse * gain_ref[...]).astype(jnp.bfloat16)

        def value_tile(i, carry):
            kval_ref[m, :, columns(i)] = jnp.dot(
                normed, wv_ref[:, columns(i)], preferred_element_type=jnp.float32
            ).astype(jnp.bfloat16)
            return carry

        lax.fori_loop(0, heads // TILE, value_tile, 0)
        values = kval_ref[m]

        def result_tile(i, carry):
            fres[m, :, columns(i)] = (
                fbuf[m, :, columns(i)].astype(jnp.float32)
                + jnp.dot(values, wo_ref[:, columns(i)], preferred_element_type=jnp.float32)
            ).astype(jnp.bfloat16)
            return carry

        lax.fori_loop(0, width // TILE, result_tile, 0)

        @pl.when(place < sections - 1)
        def _():
            forward_copy(m).start()

    contract = (((1,), (1,)), ((), ()))
    for m in range(micro_count):
        @pl.when(place < sections - 1)
        def _():
            backward_copy(m).wait_recv()

        grad = bbuf[m]
        kgrad_ref[m] = grad

        def dvalue_tile(i, carry):
            kdv_ref[m, :, columns(i)] = lax.dot_general(
                grad, wo_ref[columns(i), :], contract, preferred_element_type=jnp.float32
            ).astype(jnp.bfloat16)
            return carry

        lax.fori_loop(0, heads // TILE, dvalue_tile, 0)
        dvalues = kdv_ref[m]

        def dnormed_tile(i, carry):
            work[:, columns(i)] = lax.dot_general(
                dvalues, wv_ref[columns(i), :], contract, preferred_element_type=jnp.float32
            ) * gain_ref[:, columns(i)]
            return carry

        lax.fori_loop(0, width // TILE, dnormed_tile, 0)
        wide = kin_ref[m].astype(jnp.float32)
        inverse = lax.rsqrt(jnp.mean(wide * wide, axis=-1, keepdims=True) + 1e-06)
        dnormed = work[...]
        centred = wide * inverse
        through = inverse * (dnormed - centred * jnp.mean(dnormed * centred, axis=-1, keepdims=True))
        bres[m] = (grad.astype(jnp.float32) + through).astype(jnp.bfloat16)

        @pl.when(place > 0)
        def _():
            backward_copy(m).start()

    for m in range(micro_count):
        @pl.when(place < sections - 1)
        def _():
            forward_copy(m).wait_send()

        @pl.when(place > 0)
        def _():
            backward_copy(m).wait_send()


def run_chain(feed_rows, cot_rows, gains, value_matrix, output_matrix):
    sections = lax.axis_size("section")
    micro_count, rows, width = feed_rows.shape
    heads = value_matrix.shape[1]
    vmem = pl.BlockSpec(memory_space=pltpu.VMEM)
    act = jax.ShapeDtypeStruct((micro_count, rows, width), jnp.bfloat16)
    head_act = jax.ShapeDtypeStruct((micro_count, rows, heads), jnp.bfloat16)
    return pl.pallas_call(
        functools.partial(chain_kernel, sections),
        out_shape=(act, head_act, act, head_act),
        in_specs=[vmem] * 5,
        out_specs=(vmem,) * 4,
        scratch_shapes=[
            pltpu.VMEM((micro_count, rows, width), jnp.bfloat16),
            pltpu.VMEM((micro_count, rows, width), jnp.bfloat16),
            pltpu.VMEM((micro_count, rows, width), jnp.bfloat16),
            pltpu.VMEM((micro_count, rows, width), jnp.bfloat16),
            pltpu.VMEM((rows, width), jnp.float32),
            pltpu.SemaphoreType.DMA((micro_count,)),
            pltpu.SemaphoreType.DMA((micro_count,)),
            pltpu.SemaphoreType.DMA((micro_count,)),
            pltpu.SemaphoreType.DMA((micro_count,)),
        ],
        compiler_params=pltpu.CompilerParams(
            collective_id=0, has_side_effects=True, vmem_limit_bytes=48 * 1024 * 1024
        ),
    )(feed_rows, cot_rows, gains.reshape(1, width), value_matrix, output_matrix)


class Ring:
    def __init__(self, me, n, axis, step):
        self.me, self.n, self.axis, self.step = me, n, axis, step
        self.rights, self.lefts = n // 2, (n - 1) // 2

    def at(self, offset):
        return lax.rem(self.me + 2 * self.n + self.step * offset, self.n)

    def copy(self, src, dst, send_sem, recv_sem, toward):
        return pltpu.make_async_remote_copy(
            src_ref=src, dst_ref=dst, send_sem=send_sem, recv_sem=recv_sem,
            device_id={self.axis: toward}, device_id_type=pl.DeviceIdType.MESH,
        )


def ring_copies(window, first_src, ring, sems):
    right_send, right_recv, left_send, left_recv = sems

    def right(t, slot):
        return ring.copy(first_src if t == 0 else window(slot), window(slot), right_send.at[t], right_recv.at[t], ring.at(1))

    def left(t, slot):
        return ring.copy(first_src if t == 0 else window(slot), window(slot), left_send.at[t], left_recv.at[t], ring.at(-1))

    def start(t):
        if t < ring.rights:
            right(t, ring.at(-t)).start()
        if t < ring.lefts:
            left(t, ring.at(t)).start()

    def wait(t):
        if t < ring.rights:
            ring.copy(first_src, window(ring.at(-1 - t)), right_send.at[t], right_recv.at[t], ring.me).wait_recv()
        if t < ring.lefts:
            ring.copy(first_src, window(ring.at(1 + t)), left_send.at[t], left_recv.at[t], ring.me).wait_recv()

    def finish():
        for t in range(ring.rights):
            right(t, ring.at(-t)).wait_send()
        for t in range(ring.lefts):
            left(t, ring.at(t)).wait_send()

    return start, wait, finish, ring.rights


def run_rings(rings):
    for t in range(max(r[3] for r in rings)):
        for r in rings:
            r[0](t)
        for r in rings:
            r[1](t)


def gather_kernel(ys, zs, wv_ref, wo_ref, wv_all, wo_all, own_sem, va, vb, vc, oa_send, oa_recv, ob, oc):
    y = lax.axis_index("y")
    z = lax.axis_index("z")
    mesh_ids = pl.DeviceIdType.MESH
    barrier = pltpu.get_barrier_semaphore()
    pl.semaphore_signal(barrier, inc=1, device_id={"z": lax.rem(z + 1, zs)}, device_id_type=mesh_ids)
    pl.semaphore_signal(barrier, inc=1, device_id={"z": lax.rem(z + zs - 1, zs)}, device_id_type=mesh_ids)
    for k in range(1, ys):
        pl.semaphore_signal(barrier, inc=1, device_id={"y": lax.rem(y + k, ys)}, device_id_type=mesh_ids)
    pl.semaphore_wait(barrier, ys + 1)

    own_v = pltpu.make_async_copy(wv_ref, wv_all.at[y, z], own_sem.at[0])
    own_o = pltpu.make_async_copy(wo_ref, wo_all.at[y, z], own_sem.at[1])
    own_v.start()
    own_o.start()

    def o_first(k, target):
        return pltpu.make_async_remote_copy(
            src_ref=wo_ref, dst_ref=wo_all.at[y, z], send_sem=oa_send.at[k - 1],
            recv_sem=oa_recv.at[k - 1], device_id={"y": target}, device_id_type=mesh_ids,
        )

    def o_first_in(k):
        return pltpu.make_async_remote_copy(
            src_ref=wo_ref, dst_ref=wo_all.at[lax.rem(y + ys - k, ys), z], send_sem=oa_send.at[k - 1],
            recv_sem=oa_recv.at[k - 1], device_id={"y": y}, device_id_type=mesh_ids,
        )

    for k in range(1, ys):
        o_first(k, lax.rem(y + k, ys)).start()
    v_ring = ring_copies(lambda o: wv_all.at[y, o], wv_ref, Ring(z, zs, "z", 1), va)
    run_rings([v_ring])
    own_v.wait()
    own_o.wait()
    for k in range(1, ys):
        o_first_in(k).wait_recv()
    v_half = wv_all.shape[-1] // 2
    o_half = wo_all.shape[-1] // 2
    second = []
    for part, (step, sems_v, sems_o) in enumerate(((1, vb, ob), (-1, vc, oc))):
        v_cols = pl.ds(part * v_half, v_half)
        o_cols = pl.ds(part * o_half, o_half)
        second.append(ring_copies(
            lambda o, c=v_cols: wv_all.at[pl.ds(o, 1), :, :, c], wv_all.at[pl.ds(y, 1), :, :, v_cols],
            Ring(y, ys, "y", step), sems_v,
        ))
        second.append(ring_copies(
            lambda o, c=o_cols: wo_all.at[:, pl.ds(o, 1), :, c], wo_all.at[:, pl.ds(z, 1), :, o_cols],
            Ring(z, zs, "z", step), sems_o,
        ))
    run_rings(second)
    v_ring[2]()
    for k in range(1, ys):
        o_first(k, lax.rem(y + k, ys)).wait_send()
    for r in second:
        r[2]()


def gather_weights(value_shard, output_shard):
    ys = lax.axis_size("y")
    zs = lax.axis_size("z")
    anywhere = pl.BlockSpec(memory_space=pl.ANY)
    def ring_sems(n):
        return [
            pltpu.SemaphoreType.DMA((n // 2,)),
            pltpu.SemaphoreType.DMA((n // 2,)),
            pltpu.SemaphoreType.DMA((max((n - 1) // 2, 1),)),
            pltpu.SemaphoreType.DMA((max((n - 1) // 2, 1),)),
        ]

    wv_all, wo_all = pl.pallas_call(
        functools.partial(gather_kernel, ys, zs),
        out_shape=(
            jax.ShapeDtypeStruct((ys, zs) + value_shard.shape, value_shard.dtype),
            jax.ShapeDtypeStruct((ys, zs) + output_shard.shape, output_shard.dtype),
        ),
        in_specs=[anywhere] * 2,
        out_specs=(anywhere, anywhere),
        scratch_shapes=[
            pltpu.SemaphoreType.DMA((2,)),
            ring_sems(zs),
            ring_sems(ys),
            ring_sems(ys),
            pltpu.SemaphoreType.DMA((ys - 1,)),
            pltpu.SemaphoreType.DMA((ys - 1,)),
            ring_sems(zs),
            ring_sems(zs),
        ],
        compiler_params=pltpu.CompilerParams(collective_id=1, has_side_effects=True),
    )(value_shard, output_shard)
    return (
        wv_all.reshape((-1,) + value_shard.shape[1:]),
        wo_all.reshape((-1,) + output_shard.shape[1:]),
    )


def ring_sum(get, ring, bufs, sems):
    rsend, rrecv, lsend, lrecv = bufs
    rs_send, rs_recv, ls_send, ls_recv = sems

    def right(t):
        return ring.copy(rsend.at[t], rrecv.at[t], rs_send.at[t], rs_recv.at[t], ring.at(1))

    def left(t):
        return ring.copy(lsend.at[t], lrecv.at[t], ls_send.at[t], ls_recv.at[t], ring.at(-1))

    def start(t):
        if t < ring.rights:
            value = get(ring.at(ring.rights - t))
            if t > 0:
                value = value + rrecv[t - 1].astype(jnp.float32)
            rsend[t] = value.astype(rsend.dtype)
            right(t).start()
        if t < ring.lefts:
            value = get(ring.at(t - ring.lefts))
            if t > 0:
                value = value + lrecv[t - 1].astype(jnp.float32)
            lsend[t] = value.astype(lsend.dtype)
            left(t).start()

    def wait(t):
        if t < ring.rights:
            right(t).wait_recv()
        if t < ring.lefts:
            left(t).wait_recv()

    def finish():
        for t in range(ring.rights):
            right(t).wait_send()
        for t in range(ring.lefts):
            left(t).wait_send()

    def total():
        result = get(ring.me) + rrecv[ring.rights - 1].astype(jnp.float32)
        if ring.lefts > 0:
            result = result + lrecv[ring.lefts - 1].astype(jnp.float32)
        return result

    return start, wait, finish, ring.rights, total


def direct_copies(source, landing, axis, me, count, send_sems, recv_sems):
    def copy(k):
        return pltpu.make_async_remote_copy(
            src_ref=source.at[lax.rem(me + k, count)], dst_ref=landing.at[k - 1],
            send_sem=send_sems.at[k - 1], recv_sem=recv_sems.at[k - 1],
            device_id={axis: lax.rem(me + k, count)}, device_id_type=pl.DeviceIdType.MESH,
        )

    return [copy(k) for k in range(1, count)]


def scatter_kernel(
    ys, zs, xv_ref, xo_ref, out_v, out_o,
    v_part, o_part, o_send, o_land, v_rings, o_rings, v_ring, v_sems, o_sems, vz_sems, od_send, od_recv,
):
    y = lax.axis_index("y")
    z = lax.axis_index("z")
    mesh_ids = pl.DeviceIdType.MESH
    barrier = pltpu.get_barrier_semaphore()
    pl.semaphore_signal(barrier, inc=1, device_id={"z": lax.rem(z + 1, zs)}, device_id_type=mesh_ids)
    pl.semaphore_signal(barrier, inc=1, device_id={"z": lax.rem(z + zs - 1, zs)}, device_id_type=mesh_ids)
    for k in range(1, ys):
        pl.semaphore_signal(barrier, inc=1, device_id={"y": lax.rem(y + k, ys)}, device_id_type=mesh_ids)
    pl.semaphore_wait(barrier, ys + 1)

    v_half = xv_ref.shape[-1] // 2
    o_half = xo_ref.shape[-1] // 2
    first = []
    for part, step in enumerate((1, -1)):
        vc = slice(part * v_half, (part + 1) * v_half)
        oc = slice(part * o_half, (part + 1) * o_half)
        first.append(ring_sum(
            lambda d, c=vc: xv_ref[d, :, :, c].astype(jnp.float32), Ring(y, ys, "y", step), v_rings[part], v_sems[part]
        ))
        first.append(ring_sum(
            lambda d, c=oc: xo_ref[d, :, :, c].astype(jnp.float32), Ring(z, zs, "z", step), o_rings[part], o_sems[part]
        ))
    run_rings(first)
    for part in range(2):
        o_total = first[2 * part + 1][4]()
        o_part[:, :, part * o_half:(part + 1) * o_half] = o_total
        o_send[:, :, part * o_half:(part + 1) * o_half] = o_total.astype(o_send.dtype)
        v_part[:, :, part * v_half:(part + 1) * v_half] = first[2 * part][4]()
    o_copies = direct_copies(o_send, o_land, "y", y, ys, od_send, od_recv)
    for c in o_copies:
        c.start()
    v_second = ring_sum(lambda d: v_part[d], Ring(z, zs, "z", 1), v_ring, vz_sems)
    run_rings([v_second])
    out_v[...] = v_second[4]()
    o_sum = o_part[y]
    for k, c in enumerate(o_copies):
        c.wait_recv()
        o_sum = o_sum + o_land[k].astype(jnp.float32)
    out_o[...] = o_sum
    for r in first + [v_second]:
        r[2]()
    for c in o_copies:
        c.wait_send()


def scatter_grads(value_block, output_block):
    ys = lax.axis_size("y")
    zs = lax.axis_size("z")
    rows_v, cols_v = value_block.shape
    rows_o, cols_o = output_block.shape
    v_rows = rows_v // (ys * zs)
    o_rows = rows_o // (ys * zs)
    xv = value_block.reshape(ys, zs, v_rows, cols_v)
    xo = output_block.reshape(ys, zs, o_rows, cols_o).transpose(1, 0, 2, 3)
    vmem = pl.BlockSpec(memory_space=pltpu.VMEM)
    bf = value_block.dtype

    def ring_space(n, block):
        return [
            pltpu.VMEM((n // 2,) + block, bf),
            pltpu.VMEM((n // 2,) + block, bf),
            pltpu.VMEM((max((n - 1) // 2, 1),) + block, bf),
            pltpu.VMEM((max((n - 1) // 2, 1),) + block, bf),
        ]

    def ring_sems(n):
        return [
            pltpu.SemaphoreType.DMA((n // 2,)),
            pltpu.SemaphoreType.DMA((n // 2,)),
            pltpu.SemaphoreType.DMA((max((n - 1) // 2, 1),)),
            pltpu.SemaphoreType.DMA((max((n - 1) // 2, 1),)),
        ]

    v_block = (zs, v_rows, cols_v // 2)
    o_block = (ys, o_rows, cols_o // 2)
    return pl.pallas_call(
        functools.partial(scatter_kernel, ys, zs),
        out_shape=(
            jax.ShapeDtypeStruct((v_rows, cols_v), jnp.float32),
            jax.ShapeDtypeStruct((o_rows, cols_o), jnp.float32),
        ),
        in_specs=[vmem, vmem],
        out_specs=(vmem, vmem),
        scratch_shapes=[
            pltpu.VMEM((zs, v_rows, cols_v), jnp.float32),
            pltpu.VMEM((ys, o_rows, cols_o), jnp.float32),
            pltpu.VMEM((ys, o_rows, cols_o), bf),
            pltpu.VMEM((ys - 1, o_rows, cols_o), bf),
            [ring_space(ys, v_block), ring_space(ys, v_block)],
            [ring_space(zs, o_block), ring_space(zs, o_block)],
            ring_space(zs, (v_rows, cols_v)),
            [ring_sems(ys), ring_sems(ys)],
            [ring_sems(zs), ring_sems(zs)],
            ring_sems(zs),
            pltpu.SemaphoreType.DMA((ys - 1,)),
            pltpu.SemaphoreType.DMA((ys - 1,)),
        ],
        compiler_params=pltpu.CompilerParams(
            collective_id=2, has_side_effects=True, vmem_limit_bytes=48 * 1024 * 1024
        ),
    )(xv, xo)


DP = ("y", "z")


def on_device(inputs, cotangent, value_weight, output_weight, norm_gain, value_noise, output_noise):
    micro_count, example_count, seq_len, feature_width = inputs.shape
    feed_rows = inputs.reshape(micro_count, example_count * seq_len, feature_width)
    cot_rows = cotangent.reshape(micro_count, example_count * seq_len, feature_width)
    value_matrix, output_matrix = gather_weights(value_weight[0], output_weight[0])
    head_width = value_matrix.shape[1]
    gains = norm_gain[0]
    kept_inputs, kept_values, kept_grads, kept_dvalues = run_chain(
        feed_rows, cot_rows, gains, value_matrix, output_matrix
    )
    unused_wide, unused_inverse, normed_rows = norm_parts(
        kept_inputs.reshape(-1, feature_width), gains
    )
    normed_kept = normed_rows.reshape(kept_inputs.shape)
    partial_squares = jnp.stack(
        [
            example_sums(normed_kept[m], kept_dvalues[m], seq_len)
            + example_sums(kept_values[m], kept_grads[m], seq_len)
            for m in range(micro_count)
        ]
    )
    total_squares = lax.psum(partial_squares, "section")
    clip_weight = 1.0 / (jnp.sqrt(total_squares) + 0.01)
    token_weight = jnp.repeat(clip_weight, seq_len, axis=1)[:, :, None]
    scaled_dvalues = (
        (kept_dvalues.astype(jnp.float32) * token_weight)
        .astype(jnp.bfloat16)
        .reshape(-1, head_width)
    )
    scaled_grads = (
        (kept_grads.astype(jnp.float32) * token_weight)
        .astype(jnp.bfloat16)
        .reshape(-1, feature_width)
    )
    value_rows = kept_values.reshape(-1, head_width)
    columns = normed_rows
    value_block = lax.dot_general(
        normed_rows, scaled_dvalues, (((0,), (0,)), ((), ())), preferred_element_type=jnp.float32
    ).astype(jnp.bfloat16)
    output_block = lax.dot_general(
        value_rows, scaled_grads, (((0,), (0,)), ((), ())), preferred_element_type=jnp.float32
    ).astype(jnp.bfloat16)
    value_part, output_part = scatter_grads(value_block, output_block)
    grad_scale = math.sqrt(feature_width * head_width)
    value_grad = (value_part * grad_scale + value_noise[0])[None]
    output_grad = (output_part * grad_scale + output_noise[0])[None]
    return (value_grad, output_grad)


def split_dp(mesh):
    devices = mesh.devices
    sections, count = devices.shape
    try:
        across = len({d.coords[1] for d in devices[0]})
    except (AttributeError, IndexError, TypeError):
        across = 1
    if across < 1 or count % across:
        across = 1
    return Mesh(devices.reshape(sections, across, count // across), ("section",) + DP)


def solution(mesh):
    grid = split_dp(mesh)
    return jax.shard_map(
        on_device,
        mesh=grid,
        in_specs=(
            P(None, DP, None, None),
            P(None, DP, None, None),
            P("section", DP, None),
            P("section", DP, None),
            P("section", None),
            P("section", DP, None),
            P("section", DP, None),
        ),
        out_specs=(P("section", DP, None), P("section", DP, None)),
        check_vma=False,
    )
```

```python
import functools
import math

import jax
import jax.numpy as jnp
from jax import lax
from jax.experimental import pallas as pl
from jax.experimental.pallas import tpu as pltpu
from jax.sharding import Mesh, PartitionSpec as P


def norm_parts(current, gains):
    widened = current.astype(jnp.float32)
    inverse = lax.rsqrt(jnp.mean(widened * widened, axis=-1, keepdims=True) + 1e-06)
    normed = (widened * inverse * gains).astype(jnp.bfloat16)
    return (widened, inverse, normed)


def layer_forward(current, gains, value_matrix, output_matrix):
    widened, inverse, normed = norm_parts(current, gains)
    values = jnp.dot(normed, value_matrix, preferred_element_type=jnp.float32).astype(jnp.bfloat16)
    result = (widened + jnp.dot(values, output_matrix, preferred_element_type=jnp.float32)).astype(
        jnp.bfloat16
    )
    return (values, result)


def layer_backward(current, incoming, gains, value_matrix, output_matrix):
    widened, inverse, normed = norm_parts(current, gains)
    dvalues = jnp.dot(incoming, output_matrix.T, preferred_element_type=jnp.float32).astype(
        jnp.bfloat16
    )
    dnormed = jnp.dot(dvalues, value_matrix.T, preferred_element_type=jnp.float32) * gains
    centred = widened * inverse
    through = inverse * (dnormed - centred * jnp.mean(dnormed * centred, axis=-1, keepdims=True))
    before = (incoming.astype(jnp.float32) + through).astype(jnp.bfloat16)
    return (normed, dvalues, before)


def example_sums(left, right, seq_len):
    first = left.reshape(-1, seq_len, left.shape[-1])
    second = right.reshape(-1, seq_len, right.shape[-1])
    gram_first = jnp.einsum("eth,esh->ets", first, first, preferred_element_type=jnp.float32)
    gram_second = jnp.einsum("eth,esh->ets", second, second, preferred_element_type=jnp.float32)
    return jnp.sum(gram_first * gram_second, axis=(1, 2))


TILE = 256


def chain_kernel(
    sections, seq_len,
    seed_ref, cot_ref, gain_ref, wv_ref, wo_ref,
    kin_ref, kval_ref, kgrad_ref, kdv_ref, total_ref,
    fbuf, fres, bbuf, bres, work, fsend, frecv, bsend, brecv, sq_mine, sq_all, sq_send, sq_recv,
):
    place = lax.axis_index("section")
    micro_count, rows, width = seed_ref.shape
    heads = wv_ref.shape[1]
    ahead = lax.rem(place + 1, sections)
    behind = lax.rem(place + sections - 1, sections)
    first = place == 0
    last = place == sections - 1

    barrier = pltpu.get_barrier_semaphore()
    for k in range(1, sections):
        pl.semaphore_signal(
            barrier, inc=1, device_id={"section": lax.rem(place + k, sections)}, device_id_type=pl.DeviceIdType.MESH
        )
    pl.semaphore_wait(barrier, sections - 1)

    @pl.when(first)
    def _():
        fbuf[...] = seed_ref[...]

    @pl.when(last)
    def _():
        bbuf[...] = cot_ref[...]

    def forward_copy(m):
        return pltpu.make_async_remote_copy(
            src_ref=fres.at[m], dst_ref=fbuf.at[m], send_sem=fsend.at[m], recv_sem=frecv.at[m],
            device_id={"section": ahead}, device_id_type=pl.DeviceIdType.MESH,
        )

    def backward_copy(m):
        return pltpu.make_async_remote_copy(
            src_ref=bres.at[m], dst_ref=bbuf.at[m], send_sem=bsend.at[m], recv_sem=brecv.at[m],
            device_id={"section": behind}, device_id_type=pl.DeviceIdType.MESH,
        )

    def columns(i):
        return pl.ds(pl.multiple_of(i * TILE, TILE), TILE)

    for m in range(micro_count):
        @pl.when(place > 0)
        def _():
            forward_copy(m).wait_recv()

        x = fbuf[m]
        kin_ref[m] = x
        wide = x.astype(jnp.float32)
        inverse = lax.rsqrt(jnp.mean(wide * wide, axis=-1, keepdims=True) + 1e-06)
        normed = (wide * inverse * gain_ref[...]).astype(jnp.bfloat16)

        def value_tile(i, carry):
            kval_ref[m, :, columns(i)] = jnp.dot(
                normed, wv_ref[:, columns(i)], preferred_element_type=jnp.float32
            ).astype(jnp.bfloat16)
            return carry

        lax.fori_loop(0, heads // TILE, value_tile, 0)
        values = kval_ref[m]

        def result_tile(i, carry):
            fres[m, :, columns(i)] = (
                fbuf[m, :, columns(i)].astype(jnp.float32)
                + jnp.dot(values, wo_ref[:, columns(i)], preferred_element_type=jnp.float32)
            ).astype(jnp.bfloat16)
            return carry

        lax.fori_loop(0, width // TILE, result_tile, 0)

        @pl.when(place < sections - 1)
        def _():
            forward_copy(m).start()

    contract = (((1,), (1,)), ((), ()))
    for m in range(micro_count):
        @pl.when(place < sections - 1)
        def _():
            backward_copy(m).wait_recv()

        grad = bbuf[m]
        kgrad_ref[m] = grad

        def dvalue_tile(i, carry):
            kdv_ref[m, :, columns(i)] = lax.dot_general(
                grad, wo_ref[columns(i), :], contract, preferred_element_type=jnp.float32
            ).astype(jnp.bfloat16)
            return carry

        lax.fori_loop(0, heads // TILE, dvalue_tile, 0)
        dvalues = kdv_ref[m]

        def dnormed_tile(i, carry):
            work[:, columns(i)] = lax.dot_general(
                dvalues, wv_ref[columns(i), :], contract, preferred_element_type=jnp.float32
            ) * gain_ref[:, columns(i)]
            return carry

        lax.fori_loop(0, width // TILE, dnormed_tile, 0)
        wide = kin_ref[m].astype(jnp.float32)
        inverse = lax.rsqrt(jnp.mean(wide * wide, axis=-1, keepdims=True) + 1e-06)
        dnormed = work[...]
        centred = wide * inverse
        through = inverse * (dnormed - centred * jnp.mean(dnormed * centred, axis=-1, keepdims=True))
        bres[m] = (grad.astype(jnp.float32) + through).astype(jnp.bfloat16)

        @pl.when(place > 0)
        def _():
            backward_copy(m).start()

    lane = lax.broadcasted_iota(jnp.int32, sq_mine.shape, 1)
    row = lax.broadcasted_iota(jnp.int32, sq_mine.shape, 0)
    squares = jnp.zeros(sq_mine.shape, jnp.float32)
    for m in range(micro_count):
        wide = kin_ref[m].astype(jnp.float32)
        inverse = lax.rsqrt(jnp.mean(wide * wide, axis=-1, keepdims=True) + 1e-06)
        normed = (wide * inverse * gain_ref[...]).astype(jnp.bfloat16)
        for e in range(rows // seq_len):
            span = slice(e * seq_len, (e + 1) * seq_len)
            pairs = ((normed[span], kdv_ref[m, span]), (kval_ref[m, span], kgrad_ref[m, span]))
            term = 0.0
            for left_part, right_part in pairs:
                gram_left = lax.dot_general(left_part, left_part, contract, preferred_element_type=jnp.float32)
                gram_right = lax.dot_general(right_part, right_part, contract, preferred_element_type=jnp.float32)
                term = term + jnp.sum(gram_left * gram_right)
            squares = jnp.where((row == m) & (lane == e), term, squares)
    sq_mine[...] = squares

    def share(k):
        return pltpu.make_async_remote_copy(
            src_ref=sq_mine, dst_ref=sq_all.at[k - 1], send_sem=sq_send.at[k - 1], recv_sem=sq_recv.at[k - 1],
            device_id={"section": lax.rem(place + k, sections)}, device_id_type=pl.DeviceIdType.MESH,
        )

    for k in range(1, sections):
        share(k).start()
    total = squares
    for k in range(1, sections):
        share(k).wait_recv()
        total = total + sq_all[k - 1]
    total_ref[...] = total

    for k in range(1, sections):
        share(k).wait_send()
    for m in range(micro_count):
        @pl.when(place < sections - 1)
        def _():
            forward_copy(m).wait_send()

        @pl.when(place > 0)
        def _():
            backward_copy(m).wait_send()


def run_chain(feed_rows, cot_rows, gains, value_matrix, output_matrix, seq_len):
    sections = lax.axis_size("section")
    micro_count, rows, width = feed_rows.shape
    heads = value_matrix.shape[1]
    vmem = pl.BlockSpec(memory_space=pltpu.VMEM)
    act = jax.ShapeDtypeStruct((micro_count, rows, width), jnp.bfloat16)
    head_act = jax.ShapeDtypeStruct((micro_count, rows, heads), jnp.bfloat16)
    return pl.pallas_call(
        functools.partial(chain_kernel, sections, seq_len),
        out_shape=(act, head_act, act, head_act, jax.ShapeDtypeStruct((8, 128), jnp.float32)),
        in_specs=[vmem] * 5,
        out_specs=(vmem,) * 5,
        scratch_shapes=[
            pltpu.VMEM((micro_count, rows, width), jnp.bfloat16),
            pltpu.VMEM((micro_count, rows, width), jnp.bfloat16),
            pltpu.VMEM((micro_count, rows, width), jnp.bfloat16),
            pltpu.VMEM((micro_count, rows, width), jnp.bfloat16),
            pltpu.VMEM((rows, width), jnp.float32),
            pltpu.SemaphoreType.DMA((micro_count,)),
            pltpu.SemaphoreType.DMA((micro_count,)),
            pltpu.SemaphoreType.DMA((micro_count,)),
            pltpu.SemaphoreType.DMA((micro_count,)),
            pltpu.VMEM((8, 128), jnp.float32),
            pltpu.VMEM((sections - 1, 8, 128), jnp.float32),
            pltpu.SemaphoreType.DMA((sections - 1,)),
            pltpu.SemaphoreType.DMA((sections - 1,)),
        ],
        compiler_params=pltpu.CompilerParams(
            collective_id=0, has_side_effects=True, vmem_limit_bytes=48 * 1024 * 1024
        ),
    )(feed_rows, cot_rows, gains.reshape(1, width), value_matrix, output_matrix)


def ring_copies(window, first_src, z, zs, sems):
    mesh_ids = pl.DeviceIdType.MESH
    right_send, right_recv, left_send, left_recv = sems
    rights, lefts = zs // 2, (zs - 1) // 2

    def right(t):
        slot = lax.rem(z + zs - t, zs)
        return pltpu.make_async_remote_copy(
            src_ref=first_src if t == 0 else window(slot), dst_ref=window(slot),
            send_sem=right_send.at[t], recv_sem=right_recv.at[t],
            device_id={"z": lax.rem(z + 1, zs)}, device_id_type=mesh_ids,
        )

    def left(t):
        slot = lax.rem(z + t, zs)
        return pltpu.make_async_remote_copy(
            src_ref=first_src if t == 0 else window(slot), dst_ref=window(slot),
            send_sem=left_send.at[t], recv_sem=left_recv.at[t],
            device_id={"z": lax.rem(z + zs - 1, zs)}, device_id_type=mesh_ids,
        )

    def right_in(t):
        return pltpu.make_async_remote_copy(
            src_ref=first_src, dst_ref=window(lax.rem(z + 2 * zs - 1 - t, zs)),
            send_sem=right_send.at[t], recv_sem=right_recv.at[t],
            device_id={"z": z}, device_id_type=mesh_ids,
        )

    def left_in(t):
        return pltpu.make_async_remote_copy(
            src_ref=first_src, dst_ref=window(lax.rem(z + 1 + t, zs)),
            send_sem=left_send.at[t], recv_sem=left_recv.at[t],
            device_id={"z": z}, device_id_type=mesh_ids,
        )

    def run():
        for t in range(rights):
            right(t).start()
            if t < lefts:
                left(t).start()
            right_in(t).wait_recv()
            if t < lefts:
                left_in(t).wait_recv()

    def finish():
        for t in range(rights):
            right(t).wait_send()
        for t in range(lefts):
            left(t).wait_send()

    return run, finish


def gather_kernel(ys, zs, wv_ref, wo_ref, wv_all, wo_all, own_sem, va, vb_send, vb_recv, oa_send, oa_recv, ob):
    y = lax.axis_index("y")
    z = lax.axis_index("z")
    mesh_ids = pl.DeviceIdType.MESH
    barrier = pltpu.get_barrier_semaphore()
    pl.semaphore_signal(barrier, inc=1, device_id={"z": lax.rem(z + 1, zs)}, device_id_type=mesh_ids)
    pl.semaphore_signal(barrier, inc=1, device_id={"z": lax.rem(z + zs - 1, zs)}, device_id_type=mesh_ids)
    for k in range(1, ys):
        pl.semaphore_signal(barrier, inc=1, device_id={"y": lax.rem(y + k, ys)}, device_id_type=mesh_ids)
    pl.semaphore_wait(barrier, ys + 1)

    own_v = pltpu.make_async_copy(wv_ref, wv_all.at[y, z], own_sem.at[0])
    own_o = pltpu.make_async_copy(wo_ref, wo_all.at[y, z], own_sem.at[1])
    own_v.start()
    own_o.start()

    def o_first(k, target):
        return pltpu.make_async_remote_copy(
            src_ref=wo_ref, dst_ref=wo_all.at[y, z], send_sem=oa_send.at[k - 1],
            recv_sem=oa_recv.at[k - 1], device_id={"y": target}, device_id_type=mesh_ids,
        )

    def o_first_in(k):
        return pltpu.make_async_remote_copy(
            src_ref=wo_ref, dst_ref=wo_all.at[lax.rem(y + ys - k, ys), z], send_sem=oa_send.at[k - 1],
            recv_sem=oa_recv.at[k - 1], device_id={"y": y}, device_id_type=mesh_ids,
        )

    def v_second(k, row, target):
        return pltpu.make_async_remote_copy(
            src_ref=wv_all.at[pl.ds(row, 1)], dst_ref=wv_all.at[pl.ds(row, 1)],
            send_sem=vb_send.at[k - 1], recv_sem=vb_recv.at[k - 1],
            device_id={"y": target}, device_id_type=mesh_ids,
        )

    for k in range(1, ys):
        o_first(k, lax.rem(y + k, ys)).start()
    v_ring, v_ring_done = ring_copies(lambda o: wv_all.at[y, o], wv_ref, z, zs, va)
    v_ring()
    own_v.wait()
    own_o.wait()
    for k in range(1, ys):
        o_first_in(k).wait_recv()
    for k in range(1, ys):
        v_second(k, y, lax.rem(y + k, ys)).start()
    o_ring, o_ring_done = ring_copies(
        lambda o: wo_all.at[:, pl.ds(o, 1)], wo_all.at[:, pl.ds(z, 1)], z, zs, ob
    )
    o_ring()
    v_ring_done()
    for k in range(1, ys):
        o_first(k, lax.rem(y + k, ys)).wait_send()
    for k in range(1, ys):
        v_second(k, lax.rem(y + ys - k, ys), y).wait_recv()
    o_ring_done()
    for k in range(1, ys):
        v_second(k, y, lax.rem(y + k, ys)).wait_send()


def gather_weights(value_shard, output_shard):
    ys = lax.axis_size("y")
    zs = lax.axis_size("z")
    anywhere = pl.BlockSpec(memory_space=pl.ANY)
    ring_sems = [
        pltpu.SemaphoreType.DMA((zs // 2,)),
        pltpu.SemaphoreType.DMA((zs // 2,)),
        pltpu.SemaphoreType.DMA((max((zs - 1) // 2, 1),)),
        pltpu.SemaphoreType.DMA((max((zs - 1) // 2, 1),)),
    ]
    wv_all, wo_all = pl.pallas_call(
        functools.partial(gather_kernel, ys, zs),
        out_shape=(
            jax.ShapeDtypeStruct((ys, zs) + value_shard.shape, value_shard.dtype),
            jax.ShapeDtypeStruct((ys, zs) + output_shard.shape, output_shard.dtype),
        ),
        in_specs=[anywhere] * 2,
        out_specs=(anywhere, anywhere),
        scratch_shapes=[pltpu.SemaphoreType.DMA((2,)), ring_sems]
        + [pltpu.SemaphoreType.DMA((ys - 1,))] * 4
        + [ring_sems],
        compiler_params=pltpu.CompilerParams(collective_id=1, has_side_effects=True),
    )(value_shard, output_shard)
    return (
        wv_all.reshape((-1,) + value_shard.shape[1:]),
        wo_all.reshape((-1,) + output_shard.shape[1:]),
    )


def ring_sum(get, z, zs, bufs, sems):
    mesh_ids = pl.DeviceIdType.MESH
    rsend, rrecv, lsend, lrecv = bufs
    rs_send, rs_recv, ls_send, ls_recv = sems
    rights, lefts = zs // 2, (zs - 1) // 2

    def right(t):
        return pltpu.make_async_remote_copy(
            src_ref=rsend.at[t], dst_ref=rrecv.at[t], send_sem=rs_send.at[t], recv_sem=rs_recv.at[t],
            device_id={"z": lax.rem(z + 1, zs)}, device_id_type=mesh_ids,
        )

    def left(t):
        return pltpu.make_async_remote_copy(
            src_ref=lsend.at[t], dst_ref=lrecv.at[t], send_sem=ls_send.at[t], recv_sem=ls_recv.at[t],
            device_id={"z": lax.rem(z + zs - 1, zs)}, device_id_type=mesh_ids,
        )

    for t in range(rights):
        value = get(lax.rem(z + rights - t, zs))
        if t > 0:
            value = value + rrecv[t - 1].astype(jnp.float32)
        rsend[t] = value.astype(rsend.dtype)
        right(t).start()
        if t < lefts:
            value = get(lax.rem(z + zs - lefts + t, zs))
            if t > 0:
                value = value + lrecv[t - 1].astype(jnp.float32)
            lsend[t] = value.astype(lsend.dtype)
            left(t).start()
        right(t).wait_recv()
        if t < lefts:
            left(t).wait_recv()
    total = get(z) + rrecv[rights - 1].astype(jnp.float32)
    if lefts > 0:
        total = total + lrecv[lefts - 1].astype(jnp.float32)

    def finish():
        for t in range(rights):
            right(t).wait_send()
        for t in range(lefts):
            left(t).wait_send()

    return total, finish


def direct_copies(source, landing, axis, me, count, send_sems, recv_sems):
    def copy(k):
        return pltpu.make_async_remote_copy(
            src_ref=source.at[lax.rem(me + k, count)], dst_ref=landing.at[k - 1],
            send_sem=send_sems.at[k - 1], recv_sem=recv_sems.at[k - 1],
            device_id={axis: lax.rem(me + k, count)}, device_id_type=pl.DeviceIdType.MESH,
        )

    return [copy(k) for k in range(1, count)]


def scatter_kernel(
    ys, zs, xv_ref, xo_ref, out_v, out_o,
    v_land, v_part, o_part, o_send, o_land, v_ring, o_ring, v_sems, o_sems, vd_send, vd_recv, od_send, od_recv,
):
    y = lax.axis_index("y")
    z = lax.axis_index("z")
    mesh_ids = pl.DeviceIdType.MESH
    barrier = pltpu.get_barrier_semaphore()
    pl.semaphore_signal(barrier, inc=1, device_id={"z": lax.rem(z + 1, zs)}, device_id_type=mesh_ids)
    pl.semaphore_signal(barrier, inc=1, device_id={"z": lax.rem(z + zs - 1, zs)}, device_id_type=mesh_ids)
    for k in range(1, ys):
        pl.semaphore_signal(barrier, inc=1, device_id={"y": lax.rem(y + k, ys)}, device_id_type=mesh_ids)
    pl.semaphore_wait(barrier, ys + 1)

    v_copies = direct_copies(xv_ref, v_land, "y", y, ys, vd_send, vd_recv)
    for c in v_copies:
        c.start()
    o_total, o_finish = ring_sum(lambda d: xo_ref[d].astype(jnp.float32), z, zs, o_ring, o_sems)
    o_part[...] = o_total
    o_send[...] = o_total.astype(o_send.dtype)
    o_copies = direct_copies(o_send, o_land, "y", y, ys, od_send, od_recv)
    for c in o_copies:
        c.start()
    v_sum = xv_ref[y].astype(jnp.float32)
    for k, c in enumerate(v_copies):
        c.wait_recv()
        v_sum = v_sum + v_land[k].astype(jnp.float32)
    v_part[...] = v_sum
    v_total, v_finish = ring_sum(lambda d: v_part[d], z, zs, v_ring, v_sems)
    out_v[...] = v_total
    o_sum = o_part[y]
    for k, c in enumerate(o_copies):
        c.wait_recv()
        o_sum = o_sum + o_land[k].astype(jnp.float32)
    out_o[...] = o_sum
    o_finish()
    v_finish()
    for c in v_copies + o_copies:
        c.wait_send()


def scatter_grads(value_block, output_block):
    ys = lax.axis_size("y")
    zs = lax.axis_size("z")
    rows_v, cols_v = value_block.shape
    rows_o, cols_o = output_block.shape
    v_rows = rows_v // (ys * zs)
    o_rows = rows_o // (ys * zs)
    xv = value_block.reshape(ys, zs, v_rows, cols_v)
    xo = output_block.reshape(ys, zs, o_rows, cols_o).transpose(1, 0, 2, 3)
    vmem = pl.BlockSpec(memory_space=pltpu.VMEM)
    rights, lefts = zs // 2, max((zs - 1) // 2, 1)
    bf = value_block.dtype

    def ring_space(block):
        return [
            pltpu.VMEM((rights,) + block, bf),
            pltpu.VMEM((rights,) + block, bf),
            pltpu.VMEM((lefts,) + block, bf),
            pltpu.VMEM((lefts,) + block, bf),
        ]

    ring_sems = [
        pltpu.SemaphoreType.DMA((rights,)),
        pltpu.SemaphoreType.DMA((rights,)),
        pltpu.SemaphoreType.DMA((lefts,)),
        pltpu.SemaphoreType.DMA((lefts,)),
    ]
    return pl.pallas_call(
        functools.partial(scatter_kernel, ys, zs),
        out_shape=(
            jax.ShapeDtypeStruct((v_rows, cols_v), jnp.float32),
            jax.ShapeDtypeStruct((o_rows, cols_o), jnp.float32),
        ),
        in_specs=[vmem, vmem],
        out_specs=(vmem, vmem),
        scratch_shapes=[
            pltpu.VMEM((ys - 1, zs, v_rows, cols_v), bf),
            pltpu.VMEM((zs, v_rows, cols_v), jnp.float32),
            pltpu.VMEM((ys, o_rows, cols_o), jnp.float32),
            pltpu.VMEM((ys, o_rows, cols_o), bf),
            pltpu.VMEM((ys - 1, o_rows, cols_o), bf),
            ring_space((v_rows, cols_v)),
            ring_space((ys, o_rows, cols_o)),
            ring_sems,
            ring_sems,
            pltpu.SemaphoreType.DMA((ys - 1,)),
            pltpu.SemaphoreType.DMA((ys - 1,)),
            pltpu.SemaphoreType.DMA((ys - 1,)),
            pltpu.SemaphoreType.DMA((ys - 1,)),
        ],
        compiler_params=pltpu.CompilerParams(
            collective_id=2, has_side_effects=True, vmem_limit_bytes=48 * 1024 * 1024
        ),
    )(xv, xo)


DP = ("y", "z")


def on_device(inputs, cotangent, value_weight, output_weight, norm_gain, value_noise, output_noise):
    micro_count, example_count, seq_len, feature_width = inputs.shape
    feed_rows = inputs.reshape(micro_count, example_count * seq_len, feature_width)
    cot_rows = cotangent.reshape(micro_count, example_count * seq_len, feature_width)
    value_matrix, output_matrix = gather_weights(value_weight[0], output_weight[0])
    head_width = value_matrix.shape[1]
    gains = norm_gain[0]
    kept_inputs, kept_values, kept_grads, kept_dvalues, square_table = run_chain(
        feed_rows, cot_rows, gains, value_matrix, output_matrix, seq_len
    )
    unused_wide, unused_inverse, normed_rows = norm_parts(
        kept_inputs.reshape(-1, feature_width), gains
    )
    total_squares = square_table[:micro_count, : example_count]
    clip_weight = 1.0 / (jnp.sqrt(total_squares) + 0.01)
    token_weight = jnp.repeat(clip_weight, seq_len, axis=1)[:, :, None]
    scaled_dvalues = (
        (kept_dvalues.astype(jnp.float32) * token_weight)
        .astype(jnp.bfloat16)
        .reshape(-1, head_width)
    )
    scaled_grads = (
        (kept_grads.astype(jnp.float32) * token_weight)
        .astype(jnp.bfloat16)
        .reshape(-1, feature_width)
    )
    value_rows = kept_values.reshape(-1, head_width)
    columns = normed_rows
    value_block = lax.dot_general(
        normed_rows, scaled_dvalues, (((0,), (0,)), ((), ())), preferred_element_type=jnp.float32
    ).astype(jnp.bfloat16)
    output_block = lax.dot_general(
        value_rows, scaled_grads, (((0,), (0,)), ((), ())), preferred_element_type=jnp.float32
    ).astype(jnp.bfloat16)
    value_part, output_part = scatter_grads(value_block, output_block)
    grad_scale = math.sqrt(feature_width * head_width)
    value_grad = (value_part * grad_scale + value_noise[0])[None]
    output_grad = (output_part * grad_scale + output_noise[0])[None]
    return (value_grad, output_grad)


def split_dp(mesh):
    devices = mesh.devices
    sections, count = devices.shape
    try:
        across = len({d.coords[1] for d in devices[0]})
    except (AttributeError, IndexError, TypeError):
        across = 1
    if across < 1 or count % across:
        across = 1
    return Mesh(devices.reshape(sections, across, count // across), ("section",) + DP)


def solution(mesh):
    grid = split_dp(mesh)
    return jax.shard_map(
        on_device,
        mesh=grid,
        in_specs=(
            P(None, DP, None, None),
            P(None, DP, None, None),
            P("section", DP, None),
            P("section", DP, None),
            P("section", None),
            P("section", DP, None),
            P("section", DP, None),
        ),
        out_specs=(P("section", DP, None), P("section", DP, None)),
        check_vma=False,
    )
```

```python
import functools
import math

import jax
import jax.numpy as jnp
from jax import lax
from jax.experimental import pallas as pl
from jax.experimental.pallas import tpu as pltpu
from jax.sharding import Mesh, PartitionSpec as P


def norm_parts(current, gains):
    widened = current.astype(jnp.float32)
    inverse = lax.rsqrt(jnp.mean(widened * widened, axis=-1, keepdims=True) + 1e-06)
    normed = (widened * inverse * gains).astype(jnp.bfloat16)
    return (widened, inverse, normed)


def layer_forward(current, gains, value_matrix, output_matrix):
    widened, inverse, normed = norm_parts(current, gains)
    values = jnp.dot(normed, value_matrix, preferred_element_type=jnp.float32).astype(jnp.bfloat16)
    result = (widened + jnp.dot(values, output_matrix, preferred_element_type=jnp.float32)).astype(
        jnp.bfloat16
    )
    return (values, result)


def layer_backward(current, incoming, gains, value_matrix, output_matrix):
    widened, inverse, normed = norm_parts(current, gains)
    dvalues = jnp.dot(incoming, output_matrix.T, preferred_element_type=jnp.float32).astype(
        jnp.bfloat16
    )
    dnormed = jnp.dot(dvalues, value_matrix.T, preferred_element_type=jnp.float32) * gains
    centred = widened * inverse
    through = inverse * (dnormed - centred * jnp.mean(dnormed * centred, axis=-1, keepdims=True))
    before = (incoming.astype(jnp.float32) + through).astype(jnp.bfloat16)
    return (normed, dvalues, before)


def example_sums(left, right, seq_len):
    first = left.reshape(-1, seq_len, left.shape[-1])
    second = right.reshape(-1, seq_len, right.shape[-1])
    gram_first = jnp.einsum("eth,esh->ets", first, first, preferred_element_type=jnp.float32)
    gram_second = jnp.einsum("eth,esh->ets", second, second, preferred_element_type=jnp.float32)
    return jnp.sum(gram_first * gram_second, axis=(1, 2))


def chain_kernel(
    sections, seq_len,
    seed_ref, cot_ref, gain_ref, wv_ref, wo_ref,
    kin_ref, kval_ref, kgrad_ref, kdv_ref, total_ref,
    fbuf, fres, bbuf, bres, work, fsend, frecv, bsend, brecv, sq_mine, sq_all, sq_send, sq_recv,
):
    place = lax.axis_index("section")
    micro_count, rows, width = seed_ref.shape
    heads = wv_ref.shape[1]
    ahead = lax.rem(place + 1, sections)
    behind = lax.rem(place + sections - 1, sections)
    first = place == 0
    last = place == sections - 1

    barrier = pltpu.get_barrier_semaphore()
    for k in range(1, sections):
        pl.semaphore_signal(
            barrier, inc=1, device_id={"section": lax.rem(place + k, sections)}, device_id_type=pl.DeviceIdType.MESH
        )
    pl.semaphore_wait(barrier, sections - 1)

    @pl.when(first)
    def _():
        fbuf[...] = seed_ref[...]

    @pl.when(last)
    def _():
        bbuf[...] = cot_ref[...]

    def forward_copy(m):
        return pltpu.make_async_remote_copy(
            src_ref=fres.at[m], dst_ref=fbuf.at[m], send_sem=fsend.at[m], recv_sem=frecv.at[m],
            device_id={"section": ahead}, device_id_type=pl.DeviceIdType.MESH,
        )

    def backward_copy(m):
        return pltpu.make_async_remote_copy(
            src_ref=bres.at[m], dst_ref=bbuf.at[m], send_sem=bsend.at[m], recv_sem=brecv.at[m],
            device_id={"section": behind}, device_id_type=pl.DeviceIdType.MESH,
        )

    head_tile, width_tile = heads, width

    def columns(i, tile):
        return pl.ds(pl.multiple_of(i * tile, tile), tile)

    for m in range(micro_count):
        @pl.when(place > 0)
        def _():
            forward_copy(m).wait_recv()

        x = fbuf[m]
        kin_ref[m] = x
        wide = x.astype(jnp.float32)
        inverse = lax.rsqrt(jnp.mean(wide * wide, axis=-1, keepdims=True) + 1e-06)
        normed = (wide * inverse * gain_ref[...]).astype(jnp.bfloat16)

        def value_tile(i, carry):
            kval_ref[m, :, columns(i, head_tile)] = jnp.dot(
                normed, wv_ref[:, columns(i, head_tile)], preferred_element_type=jnp.float32
            ).astype(jnp.bfloat16)
            return carry

        lax.fori_loop(0, heads // head_tile, value_tile, 0)
        values = kval_ref[m]

        def result_tile(i, carry):
            fres[m, :, columns(i, width_tile)] = (
                fbuf[m, :, columns(i, width_tile)].astype(jnp.float32)
                + jnp.dot(values, wo_ref[:, columns(i, width_tile)], preferred_element_type=jnp.float32)
            ).astype(jnp.bfloat16)
            return carry

        lax.fori_loop(0, width // width_tile, result_tile, 0)

        @pl.when(place < sections - 1)
        def _():
            forward_copy(m).start()

    contract = (((1,), (1,)), ((), ()))
    for m in range(micro_count):
        @pl.when(place < sections - 1)
        def _():
            backward_copy(m).wait_recv()

        grad = bbuf[m]
        kgrad_ref[m] = grad

        def dvalue_tile(i, carry):
            kdv_ref[m, :, columns(i, head_tile)] = lax.dot_general(
                grad, wo_ref[columns(i, head_tile), :], contract, preferred_element_type=jnp.float32
            ).astype(jnp.bfloat16)
            return carry

        lax.fori_loop(0, heads // head_tile, dvalue_tile, 0)
        dvalues = kdv_ref[m]

        def dnormed_tile(i, carry):
            work[:, columns(i, width_tile)] = lax.dot_general(
                dvalues, wv_ref[columns(i, width_tile), :], contract, preferred_element_type=jnp.float32
            ) * gain_ref[:, columns(i, width_tile)]
            return carry

        lax.fori_loop(0, width // width_tile, dnormed_tile, 0)
        wide = kin_ref[m].astype(jnp.float32)
        inverse = lax.rsqrt(jnp.mean(wide * wide, axis=-1, keepdims=True) + 1e-06)
        dnormed = work[...]
        centred = wide * inverse
        through = inverse * (dnormed - centred * jnp.mean(dnormed * centred, axis=-1, keepdims=True))
        bres[m] = (grad.astype(jnp.float32) + through).astype(jnp.bfloat16)

        @pl.when(place > 0)
        def _():
            backward_copy(m).start()

    lane = lax.broadcasted_iota(jnp.int32, sq_mine.shape, 1)
    row = lax.broadcasted_iota(jnp.int32, sq_mine.shape, 0)
    squares = jnp.zeros(sq_mine.shape, jnp.float32)
    for m in range(micro_count):
        wide = kin_ref[m].astype(jnp.float32)
        inverse = lax.rsqrt(jnp.mean(wide * wide, axis=-1, keepdims=True) + 1e-06)
        normed = (wide * inverse * gain_ref[...]).astype(jnp.bfloat16)
        for e in range(rows // seq_len):
            span = slice(e * seq_len, (e + 1) * seq_len)
            pairs = ((normed[span], kdv_ref[m, span]), (kval_ref[m, span], kgrad_ref[m, span]))
            term = 0.0
            for left_part, right_part in pairs:
                gram_left = lax.dot_general(left_part, left_part, contract, preferred_element_type=jnp.float32)
                gram_right = lax.dot_general(right_part, right_part, contract, preferred_element_type=jnp.float32)
                term = term + jnp.sum(gram_left * gram_right)
            squares = jnp.where((row == m) & (lane == e), term, squares)
    sq_mine[...] = squares

    def share(k):
        return pltpu.make_async_remote_copy(
            src_ref=sq_mine, dst_ref=sq_all.at[k - 1], send_sem=sq_send.at[k - 1], recv_sem=sq_recv.at[k - 1],
            device_id={"section": lax.rem(place + k, sections)}, device_id_type=pl.DeviceIdType.MESH,
        )

    for k in range(1, sections):
        share(k).start()
    total = squares
    for k in range(1, sections):
        share(k).wait_recv()
        total = total + sq_all[k - 1]
    total_ref[...] = total

    for k in range(1, sections):
        share(k).wait_send()
    for m in range(micro_count):
        @pl.when(place < sections - 1)
        def _():
            forward_copy(m).wait_send()

        @pl.when(place > 0)
        def _():
            backward_copy(m).wait_send()


def run_chain(feed_rows, cot_rows, gains, value_matrix, output_matrix, seq_len):
    sections = lax.axis_size("section")
    micro_count, rows, width = feed_rows.shape
    heads = value_matrix.shape[1]
    vmem = pl.BlockSpec(memory_space=pltpu.VMEM)
    act = jax.ShapeDtypeStruct((micro_count, rows, width), jnp.bfloat16)
    head_act = jax.ShapeDtypeStruct((micro_count, rows, heads), jnp.bfloat16)
    return pl.pallas_call(
        functools.partial(chain_kernel, sections, seq_len),
        out_shape=(act, head_act, act, head_act, jax.ShapeDtypeStruct((8, 128), jnp.float32)),
        in_specs=[vmem] * 5,
        out_specs=(vmem,) * 5,
        scratch_shapes=[
            pltpu.VMEM((micro_count, rows, width), jnp.bfloat16),
            pltpu.VMEM((micro_count, rows, width), jnp.bfloat16),
            pltpu.VMEM((micro_count, rows, width), jnp.bfloat16),
            pltpu.VMEM((micro_count, rows, width), jnp.bfloat16),
            pltpu.VMEM((rows, width), jnp.float32),
            pltpu.SemaphoreType.DMA((micro_count,)),
            pltpu.SemaphoreType.DMA((micro_count,)),
            pltpu.SemaphoreType.DMA((micro_count,)),
            pltpu.SemaphoreType.DMA((micro_count,)),
            pltpu.VMEM((8, 128), jnp.float32),
            pltpu.VMEM((sections - 1, 8, 128), jnp.float32),
            pltpu.SemaphoreType.DMA((sections - 1,)),
            pltpu.SemaphoreType.DMA((sections - 1,)),
        ],
        compiler_params=pltpu.CompilerParams(
            collective_id=0, has_side_effects=True, vmem_limit_bytes=48 * 1024 * 1024
        ),
    )(feed_rows, cot_rows, gains.reshape(1, width), value_matrix, output_matrix)


def ring_copies(window, first_src, z, zs, sems):
    mesh_ids = pl.DeviceIdType.MESH
    right_send, right_recv, left_send, left_recv = sems
    rights, lefts = zs // 2, (zs - 1) // 2

    def right(t):
        slot = lax.rem(z + zs - t, zs)
        return pltpu.make_async_remote_copy(
            src_ref=first_src if t == 0 else window(slot), dst_ref=window(slot),
            send_sem=right_send.at[t], recv_sem=right_recv.at[t],
            device_id={"z": lax.rem(z + 1, zs)}, device_id_type=mesh_ids,
        )

    def left(t):
        slot = lax.rem(z + t, zs)
        return pltpu.make_async_remote_copy(
            src_ref=first_src if t == 0 else window(slot), dst_ref=window(slot),
            send_sem=left_send.at[t], recv_sem=left_recv.at[t],
            device_id={"z": lax.rem(z + zs - 1, zs)}, device_id_type=mesh_ids,
        )

    def right_in(t):
        return pltpu.make_async_remote_copy(
            src_ref=first_src, dst_ref=window(lax.rem(z + 2 * zs - 1 - t, zs)),
            send_sem=right_send.at[t], recv_sem=right_recv.at[t],
            device_id={"z": z}, device_id_type=mesh_ids,
        )

    def left_in(t):
        return pltpu.make_async_remote_copy(
            src_ref=first_src, dst_ref=window(lax.rem(z + 1 + t, zs)),
            send_sem=left_send.at[t], recv_sem=left_recv.at[t],
            device_id={"z": z}, device_id_type=mesh_ids,
        )

    def run():
        for t in range(rights):
            right(t).start()
            if t < lefts:
                left(t).start()
            right_in(t).wait_recv()
            if t < lefts:
                left_in(t).wait_recv()

    def finish():
        for t in range(rights):
            right(t).wait_send()
        for t in range(lefts):
            left(t).wait_send()

    return run, finish


def gather_kernel(ys, zs, wv_ref, wo_ref, wv_all, wo_all, own_sem, va, vb_send, vb_recv, oa_send, oa_recv, ob):
    y = lax.axis_index("y")
    z = lax.axis_index("z")
    mesh_ids = pl.DeviceIdType.MESH
    barrier = pltpu.get_barrier_semaphore()
    pl.semaphore_signal(barrier, inc=1, device_id={"z": lax.rem(z + 1, zs)}, device_id_type=mesh_ids)
    pl.semaphore_signal(barrier, inc=1, device_id={"z": lax.rem(z + zs - 1, zs)}, device_id_type=mesh_ids)
    for k in range(1, ys):
        pl.semaphore_signal(barrier, inc=1, device_id={"y": lax.rem(y + k, ys)}, device_id_type=mesh_ids)
    pl.semaphore_wait(barrier, ys + 1)

    own_v = pltpu.make_async_copy(wv_ref, wv_all.at[y, z], own_sem.at[0])
    own_o = pltpu.make_async_copy(wo_ref, wo_all.at[y, z], own_sem.at[1])
    own_v.start()
    own_o.start()

    def o_first(k, target):
        return pltpu.make_async_remote_copy(
            src_ref=wo_ref, dst_ref=wo_all.at[y, z], send_sem=oa_send.at[k - 1],
            recv_sem=oa_recv.at[k - 1], device_id={"y": target}, device_id_type=mesh_ids,
        )

    def o_first_in(k):
        return pltpu.make_async_remote_copy(
            src_ref=wo_ref, dst_ref=wo_all.at[lax.rem(y + ys - k, ys), z], send_sem=oa_send.at[k - 1],
            recv_sem=oa_recv.at[k - 1], device_id={"y": y}, device_id_type=mesh_ids,
        )

    def v_second(k, row, target):
        return pltpu.make_async_remote_copy(
            src_ref=wv_all.at[pl.ds(row, 1)], dst_ref=wv_all.at[pl.ds(row, 1)],
            send_sem=vb_send.at[k - 1], recv_sem=vb_recv.at[k - 1],
            device_id={"y": target}, device_id_type=mesh_ids,
        )

    for k in range(1, ys):
        o_first(k, lax.rem(y + k, ys)).start()
    v_ring, v_ring_done = ring_copies(lambda o: wv_all.at[y, o], wv_ref, z, zs, va)
    v_ring()
    own_v.wait()
    own_o.wait()
    for k in range(1, ys):
        o_first_in(k).wait_recv()
    for k in range(1, ys):
        v_second(k, y, lax.rem(y + k, ys)).start()
    o_ring, o_ring_done = ring_copies(
        lambda o: wo_all.at[:, pl.ds(o, 1)], wo_all.at[:, pl.ds(z, 1)], z, zs, ob
    )
    o_ring()
    v_ring_done()
    for k in range(1, ys):
        o_first(k, lax.rem(y + k, ys)).wait_send()
    for k in range(1, ys):
        v_second(k, lax.rem(y + ys - k, ys), y).wait_recv()
    o_ring_done()
    for k in range(1, ys):
        v_second(k, y, lax.rem(y + k, ys)).wait_send()


def gather_weights(value_shard, output_shard):
    ys = lax.axis_size("y")
    zs = lax.axis_size("z")
    anywhere = pl.BlockSpec(memory_space=pl.ANY)
    ring_sems = [
        pltpu.SemaphoreType.DMA((zs // 2,)),
        pltpu.SemaphoreType.DMA((zs // 2,)),
        pltpu.SemaphoreType.DMA((max((zs - 1) // 2, 1),)),
        pltpu.SemaphoreType.DMA((max((zs - 1) // 2, 1),)),
    ]
    wv_all, wo_all = pl.pallas_call(
        functools.partial(gather_kernel, ys, zs),
        out_shape=(
            jax.ShapeDtypeStruct((ys, zs) + value_shard.shape, value_shard.dtype),
            jax.ShapeDtypeStruct((ys, zs) + output_shard.shape, output_shard.dtype),
        ),
        in_specs=[anywhere] * 2,
        out_specs=(anywhere, anywhere),
        scratch_shapes=[pltpu.SemaphoreType.DMA((2,)), ring_sems]
        + [pltpu.SemaphoreType.DMA((ys - 1,))] * 4
        + [ring_sems],
        compiler_params=pltpu.CompilerParams(collective_id=1, has_side_effects=True),
    )(value_shard, output_shard)
    return (
        wv_all.reshape((-1,) + value_shard.shape[1:]),
        wo_all.reshape((-1,) + output_shard.shape[1:]),
    )


def ring_sum(get, z, zs, bufs, sems):
    mesh_ids = pl.DeviceIdType.MESH
    rsend, rrecv, lsend, lrecv = bufs
    rs_send, rs_recv, ls_send, ls_recv = sems
    rights, lefts = zs // 2, (zs - 1) // 2

    def right(t):
        return pltpu.make_async_remote_copy(
            src_ref=rsend.at[t], dst_ref=rrecv.at[t], send_sem=rs_send.at[t], recv_sem=rs_recv.at[t],
            device_id={"z": lax.rem(z + 1, zs)}, device_id_type=mesh_ids,
        )

    def left(t):
        return pltpu.make_async_remote_copy(
            src_ref=lsend.at[t], dst_ref=lrecv.at[t], send_sem=ls_send.at[t], recv_sem=ls_recv.at[t],
            device_id={"z": lax.rem(z + zs - 1, zs)}, device_id_type=mesh_ids,
        )

    for t in range(rights):
        value = get(lax.rem(z + rights - t, zs))
        if t > 0:
            value = value + rrecv[t - 1].astype(jnp.float32)
        rsend[t] = value.astype(rsend.dtype)
        right(t).start()
        if t < lefts:
            value = get(lax.rem(z + zs - lefts + t, zs))
            if t > 0:
                value = value + lrecv[t - 1].astype(jnp.float32)
            lsend[t] = value.astype(lsend.dtype)
            left(t).start()
        right(t).wait_recv()
        if t < lefts:
            left(t).wait_recv()
    total = get(z) + rrecv[rights - 1].astype(jnp.float32)
    if lefts > 0:
        total = total + lrecv[lefts - 1].astype(jnp.float32)

    def finish():
        for t in range(rights):
            right(t).wait_send()
        for t in range(lefts):
            left(t).wait_send()

    return total, finish


def direct_copies(source, landing, axis, me, count, send_sems, recv_sems):
    def copy(k):
        return pltpu.make_async_remote_copy(
            src_ref=source.at[lax.rem(me + k, count)], dst_ref=landing.at[k - 1],
            send_sem=send_sems.at[k - 1], recv_sem=recv_sems.at[k - 1],
            device_id={axis: lax.rem(me + k, count)}, device_id_type=pl.DeviceIdType.MESH,
        )

    return [copy(k) for k in range(1, count)]


def scatter_kernel(
    ys, zs, xv_ref, xo_ref, out_v, out_o,
    v_land, v_part, o_part, o_send, o_land, v_ring, o_ring, v_sems, o_sems, vd_send, vd_recv, od_send, od_recv,
):
    y = lax.axis_index("y")
    z = lax.axis_index("z")
    mesh_ids = pl.DeviceIdType.MESH
    barrier = pltpu.get_barrier_semaphore()
    pl.semaphore_signal(barrier, inc=1, device_id={"z": lax.rem(z + 1, zs)}, device_id_type=mesh_ids)
    pl.semaphore_signal(barrier, inc=1, device_id={"z": lax.rem(z + zs - 1, zs)}, device_id_type=mesh_ids)
    for k in range(1, ys):
        pl.semaphore_signal(barrier, inc=1, device_id={"y": lax.rem(y + k, ys)}, device_id_type=mesh_ids)
    pl.semaphore_wait(barrier, ys + 1)

    v_copies = direct_copies(xv_ref, v_land, "y", y, ys, vd_send, vd_recv)
    for c in v_copies:
        c.start()
    o_total, o_finish = ring_sum(lambda d: xo_ref[d].astype(jnp.float32), z, zs, o_ring, o_sems)
    o_part[...] = o_total
    o_send[...] = o_total.astype(o_send.dtype)
    o_copies = direct_copies(o_send, o_land, "y", y, ys, od_send, od_recv)
    for c in o_copies:
        c.start()
    v_sum = xv_ref[y].astype(jnp.float32)
    for k, c in enumerate(v_copies):
        c.wait_recv()
        v_sum = v_sum + v_land[k].astype(jnp.float32)
    v_part[...] = v_sum
    v_total, v_finish = ring_sum(lambda d: v_part[d], z, zs, v_ring, v_sems)
    out_v[...] = v_total
    o_sum = o_part[y]
    for k, c in enumerate(o_copies):
        c.wait_recv()
        o_sum = o_sum + o_land[k].astype(jnp.float32)
    out_o[...] = o_sum
    o_finish()
    v_finish()
    for c in v_copies + o_copies:
        c.wait_send()


def scatter_grads(value_block, output_block):
    ys = lax.axis_size("y")
    zs = lax.axis_size("z")
    rows_v, cols_v = value_block.shape
    rows_o, cols_o = output_block.shape
    v_rows = rows_v // (ys * zs)
    o_rows = rows_o // (ys * zs)
    xv = value_block.reshape(ys, zs, v_rows, cols_v)
    xo = output_block.reshape(ys, zs, o_rows, cols_o).transpose(1, 0, 2, 3)
    vmem = pl.BlockSpec(memory_space=pltpu.VMEM)
    rights, lefts = zs // 2, max((zs - 1) // 2, 1)
    bf = value_block.dtype

    def ring_space(block):
        return [
            pltpu.VMEM((rights,) + block, bf),
            pltpu.VMEM((rights,) + block, bf),
            pltpu.VMEM((lefts,) + block, bf),
            pltpu.VMEM((lefts,) + block, bf),
        ]

    ring_sems = [
        pltpu.SemaphoreType.DMA((rights,)),
        pltpu.SemaphoreType.DMA((rights,)),
        pltpu.SemaphoreType.DMA((lefts,)),
        pltpu.SemaphoreType.DMA((lefts,)),
    ]
    return pl.pallas_call(
        functools.partial(scatter_kernel, ys, zs),
        out_shape=(
            jax.ShapeDtypeStruct((v_rows, cols_v), jnp.float32),
            jax.ShapeDtypeStruct((o_rows, cols_o), jnp.float32),
        ),
        in_specs=[vmem, vmem],
        out_specs=(vmem, vmem),
        scratch_shapes=[
            pltpu.VMEM((ys - 1, zs, v_rows, cols_v), bf),
            pltpu.VMEM((zs, v_rows, cols_v), jnp.float32),
            pltpu.VMEM((ys, o_rows, cols_o), jnp.float32),
            pltpu.VMEM((ys, o_rows, cols_o), bf),
            pltpu.VMEM((ys - 1, o_rows, cols_o), bf),
            ring_space((v_rows, cols_v)),
            ring_space((ys, o_rows, cols_o)),
            ring_sems,
            ring_sems,
            pltpu.SemaphoreType.DMA((ys - 1,)),
            pltpu.SemaphoreType.DMA((ys - 1,)),
            pltpu.SemaphoreType.DMA((ys - 1,)),
            pltpu.SemaphoreType.DMA((ys - 1,)),
        ],
        compiler_params=pltpu.CompilerParams(
            collective_id=2, has_side_effects=True, vmem_limit_bytes=48 * 1024 * 1024
        ),
    )(xv, xo)


DP = ("y", "z")


def on_device(inputs, cotangent, value_weight, output_weight, norm_gain, value_noise, output_noise):
    micro_count, example_count, seq_len, feature_width = inputs.shape
    feed_rows = inputs.reshape(micro_count, example_count * seq_len, feature_width)
    cot_rows = cotangent.reshape(micro_count, example_count * seq_len, feature_width)
    value_matrix, output_matrix = gather_weights(value_weight[0], output_weight[0])
    head_width = value_matrix.shape[1]
    gains = norm_gain[0]
    kept_inputs, kept_values, kept_grads, kept_dvalues, square_table = run_chain(
        feed_rows, cot_rows, gains, value_matrix, output_matrix, seq_len
    )
    unused_wide, unused_inverse, normed_rows = norm_parts(
        kept_inputs.reshape(-1, feature_width), gains
    )
    total_squares = square_table[:micro_count, : example_count]
    clip_weight = 1.0 / (jnp.sqrt(total_squares) + 0.01)
    token_weight = jnp.repeat(clip_weight, seq_len, axis=1)[:, :, None]
    scaled_dvalues = (
        (kept_dvalues.astype(jnp.float32) * token_weight)
        .astype(jnp.bfloat16)
        .reshape(-1, head_width)
    )
    scaled_grads = (
        (kept_grads.astype(jnp.float32) * token_weight)
        .astype(jnp.bfloat16)
        .reshape(-1, feature_width)
    )
    value_rows = kept_values.reshape(-1, head_width)
    columns = normed_rows
    value_block = lax.dot_general(
        normed_rows, scaled_dvalues, (((0,), (0,)), ((), ())), preferred_element_type=jnp.float32
    ).astype(jnp.bfloat16)
    output_block = lax.dot_general(
        value_rows, scaled_grads, (((0,), (0,)), ((), ())), preferred_element_type=jnp.float32
    ).astype(jnp.bfloat16)
    value_part, output_part = scatter_grads(value_block, output_block)
    grad_scale = math.sqrt(feature_width * head_width)
    value_grad = (value_part * grad_scale + value_noise[0])[None]
    output_grad = (output_part * grad_scale + output_noise[0])[None]
    return (value_grad, output_grad)


def split_dp(mesh):
    devices = mesh.devices
    sections, count = devices.shape
    try:
        across = len({d.coords[1] for d in devices[0]})
    except (AttributeError, IndexError, TypeError):
        across = 1
    if across < 1 or count % across:
        across = 1
    return Mesh(devices.reshape(sections, across, count // across), ("section",) + DP)


def solution(mesh):
    grid = split_dp(mesh)
    return jax.shard_map(
        on_device,
        mesh=grid,
        in_specs=(
            P(None, DP, None, None),
            P(None, DP, None, None),
            P("section", DP, None),
            P("section", DP, None),
            P("section", None),
            P("section", DP, None),
            P("section", DP, None),
        ),
        out_specs=(P("section", DP, None), P("section", DP, None)),
        check_vma=False,
    )
```

```python
import functools
import math

import jax
import jax.numpy as jnp
from jax import lax
from jax.experimental import pallas as pl
from jax.experimental.pallas import tpu as pltpu
from jax.sharding import Mesh, PartitionSpec as P


def norm_parts(current, gains):
    widened = current.astype(jnp.float32)
    inverse = lax.rsqrt(jnp.mean(widened * widened, axis=-1, keepdims=True) + 1e-06)
    normed = (widened * inverse * gains).astype(jnp.bfloat16)
    return (widened, inverse, normed)


def layer_forward(current, gains, value_matrix, output_matrix):
    widened, inverse, normed = norm_parts(current, gains)
    values = jnp.dot(normed, value_matrix, preferred_element_type=jnp.float32).astype(jnp.bfloat16)
    result = (widened + jnp.dot(values, output_matrix, preferred_element_type=jnp.float32)).astype(
        jnp.bfloat16
    )
    return (values, result)


def layer_backward(current, incoming, gains, value_matrix, output_matrix):
    widened, inverse, normed = norm_parts(current, gains)
    dvalues = jnp.dot(incoming, output_matrix.T, preferred_element_type=jnp.float32).astype(
        jnp.bfloat16
    )
    dnormed = jnp.dot(dvalues, value_matrix.T, preferred_element_type=jnp.float32) * gains
    centred = widened * inverse
    through = inverse * (dnormed - centred * jnp.mean(dnormed * centred, axis=-1, keepdims=True))
    before = (incoming.astype(jnp.float32) + through).astype(jnp.bfloat16)
    return (normed, dvalues, before)


def example_sums(left, right, seq_len):
    first = left.reshape(-1, seq_len, left.shape[-1])
    second = right.reshape(-1, seq_len, right.shape[-1])
    gram_first = jnp.einsum("eth,esh->ets", first, first, preferred_element_type=jnp.float32)
    gram_second = jnp.einsum("eth,esh->ets", second, second, preferred_element_type=jnp.float32)
    return jnp.sum(gram_first * gram_second, axis=(1, 2))


def chain_kernel(
    sections, seq_len,
    seed_ref, cot_ref, gain_ref, wv_ref, wo_ref,
    kin_ref, kval_ref, kgrad_ref, kdv_ref, total_ref,
    fbuf, fres, bbuf, bres, work, fsend, frecv, bsend, brecv, sq_mine, sq_all, sq_send, sq_recv,
):
    place = lax.axis_index("section")
    micro_count, rows, width = seed_ref.shape
    heads = wv_ref.shape[1]
    ahead = lax.rem(place + 1, sections)
    behind = lax.rem(place + sections - 1, sections)
    first = place == 0
    last = place == sections - 1

    barrier = pltpu.get_barrier_semaphore()
    for k in range(1, sections):
        pl.semaphore_signal(
            barrier, inc=1, device_id={"section": lax.rem(place + k, sections)}, device_id_type=pl.DeviceIdType.MESH
        )
    pl.semaphore_wait(barrier, sections - 1)

    @pl.when(first)
    def _():
        fbuf[...] = seed_ref[...]

    @pl.when(last)
    def _():
        bbuf[...] = cot_ref[...]

    def forward_copy(m):
        return pltpu.make_async_remote_copy(
            src_ref=fres.at[m], dst_ref=fbuf.at[m], send_sem=fsend.at[m], recv_sem=frecv.at[m],
            device_id={"section": ahead}, device_id_type=pl.DeviceIdType.MESH,
        )

    def backward_copy(m):
        return pltpu.make_async_remote_copy(
            src_ref=bres.at[m], dst_ref=bbuf.at[m], send_sem=bsend.at[m], recv_sem=brecv.at[m],
            device_id={"section": behind}, device_id_type=pl.DeviceIdType.MESH,
        )

    head_tile, width_tile = heads, width

    def columns(i, tile):
        return pl.ds(pl.multiple_of(i * tile, tile), tile)

    for m in range(micro_count):
        @pl.when(place > 0)
        def _():
            forward_copy(m).wait_recv()

        x = fbuf[m]
        kin_ref[m] = x
        wide = x.astype(jnp.float32)
        inverse = lax.rsqrt(jnp.mean(wide * wide, axis=-1, keepdims=True) + 1e-06)
        normed = (wide * inverse * gain_ref[...]).astype(jnp.bfloat16)

        def value_tile(i, carry):
            kval_ref[m, :, columns(i, head_tile)] = jnp.dot(
                normed, wv_ref[:, columns(i, head_tile)], preferred_element_type=jnp.float32
            ).astype(jnp.bfloat16)
            return carry

        lax.fori_loop(0, heads // head_tile, value_tile, 0)
        values = kval_ref[m]

        def result_tile(i, carry):
            fres[m, :, columns(i, width_tile)] = (
                fbuf[m, :, columns(i, width_tile)].astype(jnp.float32)
                + jnp.dot(values, wo_ref[:, columns(i, width_tile)], preferred_element_type=jnp.float32)
            ).astype(jnp.bfloat16)
            return carry

        @pl.when(place < sections - 1)
        def _():
            lax.fori_loop(0, width // width_tile, result_tile, 0)
            forward_copy(m).start()

    contract = (((1,), (1,)), ((), ()))
    for m in range(micro_count):
        @pl.when(place < sections - 1)
        def _():
            backward_copy(m).wait_recv()

        grad = bbuf[m]
        kgrad_ref[m] = grad

        def dvalue_tile(i, carry):
            kdv_ref[m, :, columns(i, head_tile)] = lax.dot_general(
                grad, wo_ref[columns(i, head_tile), :], contract, preferred_element_type=jnp.float32
            ).astype(jnp.bfloat16)
            return carry

        lax.fori_loop(0, heads // head_tile, dvalue_tile, 0)
        dvalues = kdv_ref[m]

        def dnormed_tile(i, carry):
            work[:, columns(i, width_tile)] = lax.dot_general(
                dvalues, wv_ref[columns(i, width_tile), :], contract, preferred_element_type=jnp.float32
            ) * gain_ref[:, columns(i, width_tile)]
            return carry

        lax.fori_loop(0, width // width_tile, dnormed_tile, 0)
        wide = kin_ref[m].astype(jnp.float32)
        inverse = lax.rsqrt(jnp.mean(wide * wide, axis=-1, keepdims=True) + 1e-06)
        dnormed = work[...]
        centred = wide * inverse
        through = inverse * (dnormed - centred * jnp.mean(dnormed * centred, axis=-1, keepdims=True))
        bres[m] = (grad.astype(jnp.float32) + through).astype(jnp.bfloat16)

        @pl.when(place > 0)
        def _():
            backward_copy(m).start()

    lane = lax.broadcasted_iota(jnp.int32, sq_mine.shape, 1)
    row = lax.broadcasted_iota(jnp.int32, sq_mine.shape, 0)
    squares = jnp.zeros(sq_mine.shape, jnp.float32)
    for m in range(micro_count):
        wide = kin_ref[m].astype(jnp.float32)
        inverse = lax.rsqrt(jnp.mean(wide * wide, axis=-1, keepdims=True) + 1e-06)
        normed = (wide * inverse * gain_ref[...]).astype(jnp.bfloat16)
        for e in range(rows // seq_len):
            span = slice(e * seq_len, (e + 1) * seq_len)
            pairs = ((normed[span], kdv_ref[m, span]), (kval_ref[m, span], kgrad_ref[m, span]))
            term = 0.0
            for left_part, right_part in pairs:
                gram_left = lax.dot_general(left_part, left_part, contract, preferred_element_type=jnp.float32)
                gram_right = lax.dot_general(right_part, right_part, contract, preferred_element_type=jnp.float32)
                term = term + jnp.sum(gram_left * gram_right)
            squares = jnp.where((row == m) & (lane == e), term, squares)
    sq_mine[...] = squares

    def share(k):
        return pltpu.make_async_remote_copy(
            src_ref=sq_mine, dst_ref=sq_all.at[k - 1], send_sem=sq_send.at[k - 1], recv_sem=sq_recv.at[k - 1],
            device_id={"section": lax.rem(place + k, sections)}, device_id_type=pl.DeviceIdType.MESH,
        )

    for k in range(1, sections):
        share(k).start()
    total = squares
    for k in range(1, sections):
        share(k).wait_recv()
        total = total + sq_all[k - 1]
    total_ref[...] = total

    for k in range(1, sections):
        share(k).wait_send()
    for m in range(micro_count):
        @pl.when(place < sections - 1)
        def _():
            forward_copy(m).wait_send()

        @pl.when(place > 0)
        def _():
            backward_copy(m).wait_send()


def run_chain(feed_rows, cot_rows, gains, value_matrix, output_matrix, seq_len):
    sections = lax.axis_size("section")
    micro_count, rows, width = feed_rows.shape
    heads = value_matrix.shape[1]
    vmem = pl.BlockSpec(memory_space=pltpu.VMEM)
    act = jax.ShapeDtypeStruct((micro_count, rows, width), jnp.bfloat16)
    head_act = jax.ShapeDtypeStruct((micro_count, rows, heads), jnp.bfloat16)
    return pl.pallas_call(
        functools.partial(chain_kernel, sections, seq_len),
        out_shape=(act, head_act, act, head_act, jax.ShapeDtypeStruct((8, 128), jnp.float32)),
        in_specs=[vmem] * 5,
        out_specs=(vmem,) * 5,
        scratch_shapes=[
            pltpu.VMEM((micro_count, rows, width), jnp.bfloat16),
            pltpu.VMEM((micro_count, rows, width), jnp.bfloat16),
            pltpu.VMEM((micro_count, rows, width), jnp.bfloat16),
            pltpu.VMEM((micro_count, rows, width), jnp.bfloat16),
            pltpu.VMEM((rows, width), jnp.float32),
            pltpu.SemaphoreType.DMA((micro_count,)),
            pltpu.SemaphoreType.DMA((micro_count,)),
            pltpu.SemaphoreType.DMA((micro_count,)),
            pltpu.SemaphoreType.DMA((micro_count,)),
            pltpu.VMEM((8, 128), jnp.float32),
            pltpu.VMEM((sections - 1, 8, 128), jnp.float32),
            pltpu.SemaphoreType.DMA((sections - 1,)),
            pltpu.SemaphoreType.DMA((sections - 1,)),
        ],
        compiler_params=pltpu.CompilerParams(
            collective_id=0, has_side_effects=True, vmem_limit_bytes=48 * 1024 * 1024
        ),
    )(feed_rows, cot_rows, gains.reshape(1, width), value_matrix, output_matrix)


def ring_copies(window, first_src, z, zs, sems):
    mesh_ids = pl.DeviceIdType.MESH
    right_send, right_recv, left_send, left_recv = sems
    rights, lefts = zs // 2, (zs - 1) // 2

    def right(t):
        slot = lax.rem(z + zs - t, zs)
        return pltpu.make_async_remote_copy(
            src_ref=first_src if t == 0 else window(slot), dst_ref=window(slot),
            send_sem=right_send.at[t], recv_sem=right_recv.at[t],
            device_id={"z": lax.rem(z + 1, zs)}, device_id_type=mesh_ids,
        )

    def left(t):
        slot = lax.rem(z + t, zs)
        return pltpu.make_async_remote_copy(
            src_ref=first_src if t == 0 else window(slot), dst_ref=window(slot),
            send_sem=left_send.at[t], recv_sem=left_recv.at[t],
            device_id={"z": lax.rem(z + zs - 1, zs)}, device_id_type=mesh_ids,
        )

    def right_in(t):
        return pltpu.make_async_remote_copy(
            src_ref=first_src, dst_ref=window(lax.rem(z + 2 * zs - 1 - t, zs)),
            send_sem=right_send.at[t], recv_sem=right_recv.at[t],
            device_id={"z": z}, device_id_type=mesh_ids,
        )

    def left_in(t):
        return pltpu.make_async_remote_copy(
            src_ref=first_src, dst_ref=window(lax.rem(z + 1 + t, zs)),
            send_sem=left_send.at[t], recv_sem=left_recv.at[t],
            device_id={"z": z}, device_id_type=mesh_ids,
        )

    def run():
        for t in range(rights):
            right(t).start()
            if t < lefts:
                left(t).start()
            right_in(t).wait_recv()
            if t < lefts:
                left_in(t).wait_recv()

    def finish():
        for t in range(rights):
            right(t).wait_send()
        for t in range(lefts):
            left(t).wait_send()

    return run, finish


def gather_kernel(ys, zs, wv_ref, wo_ref, wv_all, wo_all, own_sem, va, vb_send, vb_recv, oa_send, oa_recv, ob):
    y = lax.axis_index("y")
    z = lax.axis_index("z")
    mesh_ids = pl.DeviceIdType.MESH
    barrier = pltpu.get_barrier_semaphore()
    pl.semaphore_signal(barrier, inc=1, device_id={"z": lax.rem(z + 1, zs)}, device_id_type=mesh_ids)
    pl.semaphore_signal(barrier, inc=1, device_id={"z": lax.rem(z + zs - 1, zs)}, device_id_type=mesh_ids)
    for k in range(1, ys):
        pl.semaphore_signal(barrier, inc=1, device_id={"y": lax.rem(y + k, ys)}, device_id_type=mesh_ids)
    pl.semaphore_wait(barrier, ys + 1)

    own_v = pltpu.make_async_copy(wv_ref, wv_all.at[y, z], own_sem.at[0])
    own_o = pltpu.make_async_copy(wo_ref, wo_all.at[y, z], own_sem.at[1])
    own_v.start()
    own_o.start()

    def o_first(k, target):
        return pltpu.make_async_remote_copy(
            src_ref=wo_ref, dst_ref=wo_all.at[y, z], send_sem=oa_send.at[k - 1],
            recv_sem=oa_recv.at[k - 1], device_id={"y": target}, device_id_type=mesh_ids,
        )

    def o_first_in(k):
        return pltpu.make_async_remote_copy(
            src_ref=wo_ref, dst_ref=wo_all.at[lax.rem(y + ys - k, ys), z], send_sem=oa_send.at[k - 1],
            recv_sem=oa_recv.at[k - 1], device_id={"y": y}, device_id_type=mesh_ids,
        )

    def v_second(k, row, target):
        return pltpu.make_async_remote_copy(
            src_ref=wv_all.at[pl.ds(row, 1)], dst_ref=wv_all.at[pl.ds(row, 1)],
            send_sem=vb_send.at[k - 1], recv_sem=vb_recv.at[k - 1],
            device_id={"y": target}, device_id_type=mesh_ids,
        )

    for k in range(1, ys):
        o_first(k, lax.rem(y + k, ys)).start()
    v_ring, v_ring_done = ring_copies(lambda o: wv_all.at[y, o], wv_ref, z, zs, va)
    v_ring()
    own_v.wait()
    own_o.wait()
    for k in range(1, ys):
        o_first_in(k).wait_recv()
    for k in range(1, ys):
        v_second(k, y, lax.rem(y + k, ys)).start()
    o_ring, o_ring_done = ring_copies(
        lambda o: wo_all.at[:, pl.ds(o, 1)], wo_all.at[:, pl.ds(z, 1)], z, zs, ob
    )
    o_ring()
    v_ring_done()
    for k in range(1, ys):
        o_first(k, lax.rem(y + k, ys)).wait_send()
    for k in range(1, ys):
        v_second(k, lax.rem(y + ys - k, ys), y).wait_recv()
    o_ring_done()
    for k in range(1, ys):
        v_second(k, y, lax.rem(y + k, ys)).wait_send()


def gather_weights(value_shard, output_shard):
    ys = lax.axis_size("y")
    zs = lax.axis_size("z")
    anywhere = pl.BlockSpec(memory_space=pl.ANY)
    ring_sems = [
        pltpu.SemaphoreType.DMA((zs // 2,)),
        pltpu.SemaphoreType.DMA((zs // 2,)),
        pltpu.SemaphoreType.DMA((max((zs - 1) // 2, 1),)),
        pltpu.SemaphoreType.DMA((max((zs - 1) // 2, 1),)),
    ]
    wv_all, wo_all = pl.pallas_call(
        functools.partial(gather_kernel, ys, zs),
        out_shape=(
            jax.ShapeDtypeStruct((ys, zs) + value_shard.shape, value_shard.dtype),
            jax.ShapeDtypeStruct((ys, zs) + output_shard.shape, output_shard.dtype),
        ),
        in_specs=[anywhere] * 2,
        out_specs=(anywhere, anywhere),
        scratch_shapes=[pltpu.SemaphoreType.DMA((2,)), ring_sems]
        + [pltpu.SemaphoreType.DMA((ys - 1,))] * 4
        + [ring_sems],
        compiler_params=pltpu.CompilerParams(collective_id=1, has_side_effects=True),
    )(value_shard, output_shard)
    return (
        wv_all.reshape((-1,) + value_shard.shape[1:]),
        wo_all.reshape((-1,) + output_shard.shape[1:]),
    )


def ring_sum(get, z, zs, bufs, sems):
    mesh_ids = pl.DeviceIdType.MESH
    rsend, rrecv, lsend, lrecv = bufs
    rs_send, rs_recv, ls_send, ls_recv = sems
    rights, lefts = zs // 2, (zs - 1) // 2

    def right(t):
        return pltpu.make_async_remote_copy(
            src_ref=rsend.at[t], dst_ref=rrecv.at[t], send_sem=rs_send.at[t], recv_sem=rs_recv.at[t],
            device_id={"z": lax.rem(z + 1, zs)}, device_id_type=mesh_ids,
        )

    def left(t):
        return pltpu.make_async_remote_copy(
            src_ref=lsend.at[t], dst_ref=lrecv.at[t], send_sem=ls_send.at[t], recv_sem=ls_recv.at[t],
            device_id={"z": lax.rem(z + zs - 1, zs)}, device_id_type=mesh_ids,
        )

    for t in range(rights):
        value = get(lax.rem(z + rights - t, zs))
        if t > 0:
            value = value + rrecv[t - 1].astype(jnp.float32)
        rsend[t] = value.astype(rsend.dtype)
        right(t).start()
        if t < lefts:
            value = get(lax.rem(z + zs - lefts + t, zs))
            if t > 0:
                value = value + lrecv[t - 1].astype(jnp.float32)
            lsend[t] = value.astype(lsend.dtype)
            left(t).start()
        right(t).wait_recv()
        if t < lefts:
            left(t).wait_recv()
    total = get(z) + rrecv[rights - 1].astype(jnp.float32)
    if lefts > 0:
        total = total + lrecv[lefts - 1].astype(jnp.float32)

    def finish():
        for t in range(rights):
            right(t).wait_send()
        for t in range(lefts):
            left(t).wait_send()

    return total, finish


def direct_copies(source, landing, axis, me, count, send_sems, recv_sems):
    def copy(k):
        return pltpu.make_async_remote_copy(
            src_ref=source.at[lax.rem(me + k, count)], dst_ref=landing.at[k - 1],
            send_sem=send_sems.at[k - 1], recv_sem=recv_sems.at[k - 1],
            device_id={axis: lax.rem(me + k, count)}, device_id_type=pl.DeviceIdType.MESH,
        )

    return [copy(k) for k in range(1, count)]


def scatter_kernel(
    ys, zs, xv_ref, xo_ref, out_v, out_o,
    v_land, v_part, o_part, o_send, o_land, v_ring, o_ring, v_sems, o_sems, vd_send, vd_recv, od_send, od_recv,
):
    y = lax.axis_index("y")
    z = lax.axis_index("z")
    mesh_ids = pl.DeviceIdType.MESH
    barrier = pltpu.get_barrier_semaphore()
    pl.semaphore_signal(barrier, inc=1, device_id={"z": lax.rem(z + 1, zs)}, device_id_type=mesh_ids)
    pl.semaphore_signal(barrier, inc=1, device_id={"z": lax.rem(z + zs - 1, zs)}, device_id_type=mesh_ids)
    for k in range(1, ys):
        pl.semaphore_signal(barrier, inc=1, device_id={"y": lax.rem(y + k, ys)}, device_id_type=mesh_ids)
    pl.semaphore_wait(barrier, ys + 1)

    v_copies = direct_copies(xv_ref, v_land, "y", y, ys, vd_send, vd_recv)
    for c in v_copies:
        c.start()
    o_total, o_finish = ring_sum(lambda d: xo_ref[d].astype(jnp.float32), z, zs, o_ring, o_sems)
    o_part[...] = o_total
    o_send[...] = o_total.astype(o_send.dtype)
    o_copies = direct_copies(o_send, o_land, "y", y, ys, od_send, od_recv)
    for c in o_copies:
        c.start()
    v_sum = xv_ref[y].astype(jnp.float32)
    for k, c in enumerate(v_copies):
        c.wait_recv()
        v_sum = v_sum + v_land[k].astype(jnp.float32)
    v_part[...] = v_sum
    v_total, v_finish = ring_sum(lambda d: v_part[d], z, zs, v_ring, v_sems)
    out_v[...] = v_total
    o_sum = o_part[y]
    for k, c in enumerate(o_copies):
        c.wait_recv()
        o_sum = o_sum + o_land[k].astype(jnp.float32)
    out_o[...] = o_sum
    o_finish()
    v_finish()
    for c in v_copies + o_copies:
        c.wait_send()


def scatter_grads(value_block, output_block):
    ys = lax.axis_size("y")
    zs = lax.axis_size("z")
    rows_v, cols_v = value_block.shape
    rows_o, cols_o = output_block.shape
    v_rows = rows_v // (ys * zs)
    o_rows = rows_o // (ys * zs)
    xv = value_block.reshape(ys, zs, v_rows, cols_v)
    xo = output_block.reshape(ys, zs, o_rows, cols_o).transpose(1, 0, 2, 3)
    vmem = pl.BlockSpec(memory_space=pltpu.VMEM)
    rights, lefts = zs // 2, max((zs - 1) // 2, 1)
    bf = value_block.dtype

    def ring_space(block):
        return [
            pltpu.VMEM((rights,) + block, bf),
            pltpu.VMEM((rights,) + block, bf),
            pltpu.VMEM((lefts,) + block, bf),
            pltpu.VMEM((lefts,) + block, bf),
        ]

    ring_sems = [
        pltpu.SemaphoreType.DMA((rights,)),
        pltpu.SemaphoreType.DMA((rights,)),
        pltpu.SemaphoreType.DMA((lefts,)),
        pltpu.SemaphoreType.DMA((lefts,)),
    ]
    return pl.pallas_call(
        functools.partial(scatter_kernel, ys, zs),
        out_shape=(
            jax.ShapeDtypeStruct((v_rows, cols_v), jnp.float32),
            jax.ShapeDtypeStruct((o_rows, cols_o), jnp.float32),
        ),
        in_specs=[vmem, vmem],
        out_specs=(vmem, vmem),
        scratch_shapes=[
            pltpu.VMEM((ys - 1, zs, v_rows, cols_v), bf),
            pltpu.VMEM((zs, v_rows, cols_v), jnp.float32),
            pltpu.VMEM((ys, o_rows, cols_o), jnp.float32),
            pltpu.VMEM((ys, o_rows, cols_o), bf),
            pltpu.VMEM((ys - 1, o_rows, cols_o), bf),
            ring_space((v_rows, cols_v)),
            ring_space((ys, o_rows, cols_o)),
            ring_sems,
            ring_sems,
            pltpu.SemaphoreType.DMA((ys - 1,)),
            pltpu.SemaphoreType.DMA((ys - 1,)),
            pltpu.SemaphoreType.DMA((ys - 1,)),
            pltpu.SemaphoreType.DMA((ys - 1,)),
        ],
        compiler_params=pltpu.CompilerParams(
            collective_id=2, has_side_effects=True, vmem_limit_bytes=48 * 1024 * 1024
        ),
    )(xv, xo)


DP = ("y", "z")


def on_device(inputs, cotangent, value_weight, output_weight, norm_gain, value_noise, output_noise):
    micro_count, example_count, seq_len, feature_width = inputs.shape
    feed_rows = inputs.reshape(micro_count, example_count * seq_len, feature_width)
    cot_rows = cotangent.reshape(micro_count, example_count * seq_len, feature_width)
    value_matrix, output_matrix = gather_weights(value_weight[0], output_weight[0])
    head_width = value_matrix.shape[1]
    gains = norm_gain[0]
    kept_inputs, kept_values, kept_grads, kept_dvalues, square_table = run_chain(
        feed_rows, cot_rows, gains, value_matrix, output_matrix, seq_len
    )
    unused_wide, unused_inverse, normed_rows = norm_parts(
        kept_inputs.reshape(-1, feature_width), gains
    )
    total_squares = square_table[:micro_count, : example_count]
    clip_weight = 1.0 / (jnp.sqrt(total_squares) + 0.01)
    token_weight = jnp.repeat(clip_weight, seq_len, axis=1)[:, :, None]
    scaled_dvalues = (
        (kept_dvalues.astype(jnp.float32) * token_weight)
        .astype(jnp.bfloat16)
        .reshape(-1, head_width)
    )
    scaled_grads = (
        (kept_grads.astype(jnp.float32) * token_weight)
        .astype(jnp.bfloat16)
        .reshape(-1, feature_width)
    )
    value_rows = kept_values.reshape(-1, head_width)
    columns = normed_rows
    value_block = lax.dot_general(
        normed_rows, scaled_dvalues, (((0,), (0,)), ((), ())), preferred_element_type=jnp.float32
    ).astype(jnp.bfloat16)
    output_block = lax.dot_general(
        value_rows, scaled_grads, (((0,), (0,)), ((), ())), preferred_element_type=jnp.float32
    ).astype(jnp.bfloat16)
    value_part, output_part = scatter_grads(value_block, output_block)
    grad_scale = math.sqrt(feature_width * head_width)
    value_grad = (value_part * grad_scale + value_noise[0])[None]
    output_grad = (output_part * grad_scale + output_noise[0])[None]
    return (value_grad, output_grad)


def split_dp(mesh):
    devices = mesh.devices
    sections, count = devices.shape
    try:
        across = len({d.coords[1] for d in devices[0]})
    except (AttributeError, IndexError, TypeError):
        across = 1
    if across < 1 or count % across:
        across = 1
    return Mesh(devices.reshape(sections, across, count // across), ("section",) + DP)


def solution(mesh):
    grid = split_dp(mesh)
    return jax.shard_map(
        on_device,
        mesh=grid,
        in_specs=(
            P(None, DP, None, None),
            P(None, DP, None, None),
            P("section", DP, None),
            P("section", DP, None),
            P("section", None),
            P("section", DP, None),
            P("section", DP, None),
        ),
        out_specs=(P("section", DP, None), P("section", DP, None)),
        check_vma=False,
    )
```

```python
import functools
import math

import jax
import jax.numpy as jnp
from jax import lax
from jax.experimental import pallas as pl
from jax.experimental.pallas import tpu as pltpu
from jax.sharding import Mesh, PartitionSpec as P


def norm_parts(current, gains):
    widened = current.astype(jnp.float32)
    inverse = lax.rsqrt(jnp.mean(widened * widened, axis=-1, keepdims=True) + 1e-06)
    normed = (widened * inverse * gains).astype(jnp.bfloat16)
    return (widened, inverse, normed)


def layer_forward(current, gains, value_matrix, output_matrix):
    widened, inverse, normed = norm_parts(current, gains)
    values = jnp.dot(normed, value_matrix, preferred_element_type=jnp.float32).astype(jnp.bfloat16)
    result = (widened + jnp.dot(values, output_matrix, preferred_element_type=jnp.float32)).astype(
        jnp.bfloat16
    )
    return (values, result)


def layer_backward(current, incoming, gains, value_matrix, output_matrix):
    widened, inverse, normed = norm_parts(current, gains)
    dvalues = jnp.dot(incoming, output_matrix.T, preferred_element_type=jnp.float32).astype(
        jnp.bfloat16
    )
    dnormed = jnp.dot(dvalues, value_matrix.T, preferred_element_type=jnp.float32) * gains
    centred = widened * inverse
    through = inverse * (dnormed - centred * jnp.mean(dnormed * centred, axis=-1, keepdims=True))
    before = (incoming.astype(jnp.float32) + through).astype(jnp.bfloat16)
    return (normed, dvalues, before)


def example_sums(left, right, seq_len):
    first = left.reshape(-1, seq_len, left.shape[-1])
    second = right.reshape(-1, seq_len, right.shape[-1])
    gram_first = jnp.einsum("eth,esh->ets", first, first, preferred_element_type=jnp.float32)
    gram_second = jnp.einsum("eth,esh->ets", second, second, preferred_element_type=jnp.float32)
    return jnp.sum(gram_first * gram_second, axis=(1, 2))


def chain_kernel(
    sections, seq_len,
    seed_ref, cot_ref, gain_ref, wv_ref, wo_ref,
    kin_ref, kval_ref, kgrad_ref, kdv_ref, total_ref,
    fbuf, fres, bbuf, bres, work, fsend, frecv, bsend, brecv, sq_mine, sq_all, sq_send, sq_recv,
):
    place = lax.axis_index("section")
    micro_count, rows, width = seed_ref.shape
    heads = wv_ref.shape[1]
    ahead = lax.rem(place + 1, sections)
    behind = lax.rem(place + sections - 1, sections)
    first = place == 0
    last = place == sections - 1

    barrier = pltpu.get_barrier_semaphore()
    for k in range(1, sections):
        pl.semaphore_signal(
            barrier, inc=1, device_id={"section": lax.rem(place + k, sections)}, device_id_type=pl.DeviceIdType.MESH
        )
    pl.semaphore_wait(barrier, sections - 1)

    @pl.when(first)
    def _():
        fbuf[...] = seed_ref[...]

    @pl.when(last)
    def _():
        bbuf[...] = cot_ref[...]

    def forward_copy(m):
        return pltpu.make_async_remote_copy(
            src_ref=fres.at[m], dst_ref=fbuf.at[m], send_sem=fsend.at[m], recv_sem=frecv.at[m],
            device_id={"section": ahead}, device_id_type=pl.DeviceIdType.MESH,
        )

    def backward_copy(m):
        return pltpu.make_async_remote_copy(
            src_ref=bres.at[m], dst_ref=bbuf.at[m], send_sem=bsend.at[m], recv_sem=brecv.at[m],
            device_id={"section": behind}, device_id_type=pl.DeviceIdType.MESH,
        )

    head_tile, width_tile = heads, width

    def columns(i, tile):
        return pl.ds(pl.multiple_of(i * tile, tile), tile)

    for m in range(micro_count):
        @pl.when(place > 0)
        def _():
            forward_copy(m).wait_recv()

        x = fbuf[m]
        kin_ref[m] = x
        wide = x.astype(jnp.float32)
        inverse = lax.rsqrt(jnp.mean(wide * wide, axis=-1, keepdims=True) + 1e-06)
        normed = (wide * inverse * gain_ref[...]).astype(jnp.bfloat16)

        def value_tile(i, carry):
            kval_ref[m, :, columns(i, head_tile)] = jnp.dot(
                normed, wv_ref[:, columns(i, head_tile)], preferred_element_type=jnp.float32
            ).astype(jnp.bfloat16)
            return carry

        lax.fori_loop(0, heads // head_tile, value_tile, 0)
        values = kval_ref[m]

        def result_tile(i, carry):
            fres[m, :, columns(i, width_tile)] = (
                fbuf[m, :, columns(i, width_tile)].astype(jnp.float32)
                + jnp.dot(values, wo_ref[:, columns(i, width_tile)], preferred_element_type=jnp.float32)
            ).astype(jnp.bfloat16)
            return carry

        lax.fori_loop(0, width // width_tile, result_tile, 0)

        @pl.when(place < sections - 1)
        def _():
            forward_copy(m).start()

    contract = (((1,), (1,)), ((), ()))
    for m in range(micro_count):
        @pl.when(place < sections - 1)
        def _():
            backward_copy(m).wait_recv()

        grad = bbuf[m]
        kgrad_ref[m] = grad

        def dvalue_tile(i, carry):
            kdv_ref[m, :, columns(i, head_tile)] = lax.dot_general(
                grad, wo_ref[columns(i, head_tile), :], contract, preferred_element_type=jnp.float32
            ).astype(jnp.bfloat16)
            return carry

        lax.fori_loop(0, heads // head_tile, dvalue_tile, 0)
        dvalues = kdv_ref[m]

        def dnormed_tile(i, carry):
            work[:, columns(i, width_tile)] = lax.dot_general(
                dvalues, wv_ref[columns(i, width_tile), :], contract, preferred_element_type=jnp.float32
            ) * gain_ref[:, columns(i, width_tile)]
            return carry

        lax.fori_loop(0, width // width_tile, dnormed_tile, 0)
        wide = kin_ref[m].astype(jnp.float32)
        inverse = lax.rsqrt(jnp.mean(wide * wide, axis=-1, keepdims=True) + 1e-06)
        dnormed = work[...]
        centred = wide * inverse
        through = inverse * (dnormed - centred * jnp.mean(dnormed * centred, axis=-1, keepdims=True))
        bres[m] = (grad.astype(jnp.float32) + through).astype(jnp.bfloat16)

        @pl.when(place > 0)
        def _():
            backward_copy(m).start()

    lane = lax.broadcasted_iota(jnp.int32, sq_mine.shape, 1)
    row = lax.broadcasted_iota(jnp.int32, sq_mine.shape, 0)
    squares = jnp.zeros(sq_mine.shape, jnp.float32)
    for m in range(micro_count):
        wide = kin_ref[m].astype(jnp.float32)
        inverse = lax.rsqrt(jnp.mean(wide * wide, axis=-1, keepdims=True) + 1e-06)
        normed = (wide * inverse * gain_ref[...]).astype(jnp.bfloat16)
        for e in range(rows // seq_len):
            span = slice(e * seq_len, (e + 1) * seq_len)
            pairs = ((normed[span], kdv_ref[m, span]), (kval_ref[m, span], kgrad_ref[m, span]))
            term = 0.0
            for left_part, right_part in pairs:
                gram_left = lax.dot_general(left_part, left_part, contract, preferred_element_type=jnp.float32)
                gram_right = lax.dot_general(right_part, right_part, contract, preferred_element_type=jnp.float32)
                term = term + jnp.sum(gram_left * gram_right)
            squares = jnp.where((row == m) & (lane == e), term, squares)
    sq_mine[...] = squares

    def share(k):
        return pltpu.make_async_remote_copy(
            src_ref=sq_mine, dst_ref=sq_all.at[k - 1], send_sem=sq_send.at[k - 1], recv_sem=sq_recv.at[k - 1],
            device_id={"section": lax.rem(place + k, sections)}, device_id_type=pl.DeviceIdType.MESH,
        )

    for k in range(1, sections):
        share(k).start()
    total = squares
    for k in range(1, sections):
        share(k).wait_recv()
        total = total + sq_all[k - 1]
    total_ref[...] = total

    for k in range(1, sections):
        share(k).wait_send()
    for m in range(micro_count):
        @pl.when(place < sections - 1)
        def _():
            forward_copy(m).wait_send()

        @pl.when(place > 0)
        def _():
            backward_copy(m).wait_send()


def run_chain(feed_rows, cot_rows, gains, value_matrix, output_matrix, seq_len):
    sections = lax.axis_size("section")
    micro_count, rows, width = feed_rows.shape
    heads = value_matrix.shape[1]
    vmem = pl.BlockSpec(memory_space=pltpu.VMEM)
    act = jax.ShapeDtypeStruct((micro_count, rows, width), jnp.bfloat16)
    head_act = jax.ShapeDtypeStruct((micro_count, rows, heads), jnp.bfloat16)
    return pl.pallas_call(
        functools.partial(chain_kernel, sections, seq_len),
        out_shape=(act, head_act, act, head_act, jax.ShapeDtypeStruct((8, 128), jnp.float32)),
        in_specs=[vmem] * 5,
        out_specs=(vmem,) * 5,
        scratch_shapes=[
            pltpu.VMEM((micro_count, rows, width), jnp.bfloat16),
            pltpu.VMEM((micro_count, rows, width), jnp.bfloat16),
            pltpu.VMEM((micro_count, rows, width), jnp.bfloat16),
            pltpu.VMEM((micro_count, rows, width), jnp.bfloat16),
            pltpu.VMEM((rows, width), jnp.float32),
            pltpu.SemaphoreType.DMA((micro_count,)),
            pltpu.SemaphoreType.DMA((micro_count,)),
            pltpu.SemaphoreType.DMA((micro_count,)),
            pltpu.SemaphoreType.DMA((micro_count,)),
            pltpu.VMEM((8, 128), jnp.float32),
            pltpu.VMEM((sections - 1, 8, 128), jnp.float32),
            pltpu.SemaphoreType.DMA((sections - 1,)),
            pltpu.SemaphoreType.DMA((sections - 1,)),
        ],
        compiler_params=pltpu.CompilerParams(
            collective_id=0, has_side_effects=True, vmem_limit_bytes=48 * 1024 * 1024
        ),
    )(feed_rows, cot_rows, gains.reshape(1, width), value_matrix, output_matrix)


def ring_copies(window, first_src, z, zs, sems):
    mesh_ids = pl.DeviceIdType.MESH
    right_send, right_recv, left_send, left_recv = sems
    rights, lefts = zs // 2, (zs - 1) // 2

    def right(t):
        slot = lax.rem(z + zs - t, zs)
        return pltpu.make_async_remote_copy(
            src_ref=first_src if t == 0 else window(slot), dst_ref=window(slot),
            send_sem=right_send.at[t], recv_sem=right_recv.at[t],
            device_id={"z": lax.rem(z + 1, zs)}, device_id_type=mesh_ids,
        )

    def left(t):
        slot = lax.rem(z + t, zs)
        return pltpu.make_async_remote_copy(
            src_ref=first_src if t == 0 else window(slot), dst_ref=window(slot),
            send_sem=left_send.at[t], recv_sem=left_recv.at[t],
            device_id={"z": lax.rem(z + zs - 1, zs)}, device_id_type=mesh_ids,
        )

    def right_in(t):
        return pltpu.make_async_remote_copy(
            src_ref=first_src, dst_ref=window(lax.rem(z + 2 * zs - 1 - t, zs)),
            send_sem=right_send.at[t], recv_sem=right_recv.at[t],
            device_id={"z": z}, device_id_type=mesh_ids,
        )

    def left_in(t):
        return pltpu.make_async_remote_copy(
            src_ref=first_src, dst_ref=window(lax.rem(z + 1 + t, zs)),
            send_sem=left_send.at[t], recv_sem=left_recv.at[t],
            device_id={"z": z}, device_id_type=mesh_ids,
        )

    def run():
        for t in range(rights):
            right(t).start()
            if t < lefts:
                left(t).start()
            right_in(t).wait_recv()
            if t < lefts:
                left_in(t).wait_recv()

    def finish():
        for t in range(rights):
            right(t).wait_send()
        for t in range(lefts):
            left(t).wait_send()

    return run, finish


def gather_kernel(ys, zs, wv_ref, wo_ref, wv_all, wo_all, own_sem, va, vb_send, vb_recv, oa_send, oa_recv, ob):
    y = lax.axis_index("y")
    z = lax.axis_index("z")
    mesh_ids = pl.DeviceIdType.MESH
    barrier = pltpu.get_barrier_semaphore()
    pl.semaphore_signal(barrier, inc=1, device_id={"z": lax.rem(z + 1, zs)}, device_id_type=mesh_ids)
    pl.semaphore_signal(barrier, inc=1, device_id={"z": lax.rem(z + zs - 1, zs)}, device_id_type=mesh_ids)
    for k in range(1, ys):
        pl.semaphore_signal(barrier, inc=1, device_id={"y": lax.rem(y + k, ys)}, device_id_type=mesh_ids)
    pl.semaphore_wait(barrier, ys + 1)

    own_v = pltpu.make_async_copy(wv_ref, wv_all.at[y, z], own_sem.at[0])
    own_o = pltpu.make_async_copy(wo_ref, wo_all.at[y, z], own_sem.at[1])
    own_v.start()
    own_o.start()

    def o_first(k, target):
        return pltpu.make_async_remote_copy(
            src_ref=wo_ref, dst_ref=wo_all.at[y, z], send_sem=oa_send.at[k - 1],
            recv_sem=oa_recv.at[k - 1], device_id={"y": target}, device_id_type=mesh_ids,
        )

    def o_first_in(k):
        return pltpu.make_async_remote_copy(
            src_ref=wo_ref, dst_ref=wo_all.at[lax.rem(y + ys - k, ys), z], send_sem=oa_send.at[k - 1],
            recv_sem=oa_recv.at[k - 1], device_id={"y": y}, device_id_type=mesh_ids,
        )

    def v_second(k, row, target):
        return pltpu.make_async_remote_copy(
            src_ref=wv_all.at[pl.ds(row, 1)], dst_ref=wv_all.at[pl.ds(row, 1)],
            send_sem=vb_send.at[k - 1], recv_sem=vb_recv.at[k - 1],
            device_id={"y": target}, device_id_type=mesh_ids,
        )

    for k in range(1, ys):
        o_first(k, lax.rem(y + k, ys)).start()
    v_ring, v_ring_done = ring_copies(lambda o: wv_all.at[y, o], wv_ref, z, zs, va)
    v_ring()
    own_v.wait()
    own_o.wait()
    for k in range(1, ys):
        o_first_in(k).wait_recv()
    for k in range(1, ys):
        v_second(k, y, lax.rem(y + k, ys)).start()
    o_ring, o_ring_done = ring_copies(
        lambda o: wo_all.at[:, pl.ds(o, 1)], wo_all.at[:, pl.ds(z, 1)], z, zs, ob
    )
    o_ring()
    v_ring_done()
    for k in range(1, ys):
        o_first(k, lax.rem(y + k, ys)).wait_send()
    for k in range(1, ys):
        v_second(k, lax.rem(y + ys - k, ys), y).wait_recv()
    o_ring_done()
    for k in range(1, ys):
        v_second(k, y, lax.rem(y + k, ys)).wait_send()


def gather_weights(value_shard, output_shard):
    ys = lax.axis_size("y")
    zs = lax.axis_size("z")
    anywhere = pl.BlockSpec(memory_space=pl.ANY)
    ring_sems = [
        pltpu.SemaphoreType.DMA((zs // 2,)),
        pltpu.SemaphoreType.DMA((zs // 2,)),
        pltpu.SemaphoreType.DMA((max((zs - 1) // 2, 1),)),
        pltpu.SemaphoreType.DMA((max((zs - 1) // 2, 1),)),
    ]
    wv_all, wo_all = pl.pallas_call(
        functools.partial(gather_kernel, ys, zs),
        out_shape=(
            jax.ShapeDtypeStruct((ys, zs) + value_shard.shape, value_shard.dtype),
            jax.ShapeDtypeStruct((ys, zs) + output_shard.shape, output_shard.dtype),
        ),
        in_specs=[anywhere] * 2,
        out_specs=(anywhere, anywhere),
        scratch_shapes=[pltpu.SemaphoreType.DMA((2,)), ring_sems]
        + [pltpu.SemaphoreType.DMA((ys - 1,))] * 4
        + [ring_sems],
        compiler_params=pltpu.CompilerParams(collective_id=1, has_side_effects=True),
    )(value_shard, output_shard)
    return (
        wv_all.reshape((-1,) + value_shard.shape[1:]),
        wo_all.reshape((-1,) + output_shard.shape[1:]),
    )


def ring_sum(get, z, zs, bufs, sems):
    mesh_ids = pl.DeviceIdType.MESH
    rsend, rrecv, lsend, lrecv = bufs
    rs_send, rs_recv, ls_send, ls_recv = sems
    rights, lefts = zs // 2, (zs - 1) // 2

    def right(t):
        return pltpu.make_async_remote_copy(
            src_ref=rsend.at[t], dst_ref=rrecv.at[t], send_sem=rs_send.at[t], recv_sem=rs_recv.at[t],
            device_id={"z": lax.rem(z + 1, zs)}, device_id_type=mesh_ids,
        )

    def left(t):
        return pltpu.make_async_remote_copy(
            src_ref=lsend.at[t], dst_ref=lrecv.at[t], send_sem=ls_send.at[t], recv_sem=ls_recv.at[t],
            device_id={"z": lax.rem(z + zs - 1, zs)}, device_id_type=mesh_ids,
        )

    for t in range(rights):
        value = get(lax.rem(z + rights - t, zs))
        if t > 0:
            value = value + rrecv[t - 1].astype(jnp.float32)
        rsend[t] = value.astype(rsend.dtype)
        right(t).start()
        if t < lefts:
            value = get(lax.rem(z + zs - lefts + t, zs))
            if t > 0:
                value = value + lrecv[t - 1].astype(jnp.float32)
            lsend[t] = value.astype(lsend.dtype)
            left(t).start()
        right(t).wait_recv()
        if t < lefts:
            left(t).wait_recv()
    total = get(z) + rrecv[rights - 1].astype(jnp.float32)
    if lefts > 0:
        total = total + lrecv[lefts - 1].astype(jnp.float32)

    def finish():
        for t in range(rights):
            right(t).wait_send()
        for t in range(lefts):
            left(t).wait_send()

    return total, finish


def direct_copies(source, landing, axis, me, count, send_sems, recv_sems):
    def copy(k):
        return pltpu.make_async_remote_copy(
            src_ref=source.at[lax.rem(me + k, count)], dst_ref=landing.at[k - 1],
            send_sem=send_sems.at[k - 1], recv_sem=recv_sems.at[k - 1],
            device_id={axis: lax.rem(me + k, count)}, device_id_type=pl.DeviceIdType.MESH,
        )

    return [copy(k) for k in range(1, count)]


def scatter_kernel(
    ys, zs, ht_ref, sdu_ref, ut_ref, sg_ref, out_v, out_o,
    xv_ref, xo_ref, v_land, v_part, o_part, o_send, o_land, v_ring, o_ring, v_sems, o_sems, vd_send, vd_recv, od_send, od_recv,
):
    y = lax.axis_index("y")
    z = lax.axis_index("z")
    mesh_ids = pl.DeviceIdType.MESH
    barrier = pltpu.get_barrier_semaphore()
    pl.semaphore_signal(barrier, inc=1, device_id={"z": lax.rem(z + 1, zs)}, device_id_type=mesh_ids)
    pl.semaphore_signal(barrier, inc=1, device_id={"z": lax.rem(z + zs - 1, zs)}, device_id_type=mesh_ids)
    for k in range(1, ys):
        pl.semaphore_signal(barrier, inc=1, device_id={"y": lax.rem(y + k, ys)}, device_id_type=mesh_ids)
    pl.semaphore_wait(barrier, ys + 1)

    v_rows, o_rows = xv_ref.shape[2], xo_ref.shape[2]
    for a in range(ys):
        group = jnp.dot(
            ht_ref[a * zs * v_rows:(a + 1) * zs * v_rows, :], sdu_ref[...], preferred_element_type=jnp.float32
        )
        for b in range(zs):
            xv_ref[a, b] = group[b * v_rows:(b + 1) * v_rows].astype(xv_ref.dtype)
    for a in range(ys):
        group = jnp.dot(
            ut_ref[a * zs * o_rows:(a + 1) * zs * o_rows, :], sg_ref[...], preferred_element_type=jnp.float32
        )
        for b in range(zs):
            xo_ref[b, a] = group[b * o_rows:(b + 1) * o_rows].astype(xo_ref.dtype)

    v_copies = direct_copies(xv_ref, v_land, "y", y, ys, vd_send, vd_recv)
    for c in v_copies:
        c.start()
    o_total, o_finish = ring_sum(lambda d: xo_ref[d].astype(jnp.float32), z, zs, o_ring, o_sems)
    o_part[...] = o_total
    o_send[...] = o_total.astype(o_send.dtype)
    o_copies = direct_copies(o_send, o_land, "y", y, ys, od_send, od_recv)
    for c in o_copies:
        c.start()
    v_sum = xv_ref[y].astype(jnp.float32)
    for k, c in enumerate(v_copies):
        c.wait_recv()
        v_sum = v_sum + v_land[k].astype(jnp.float32)
    v_part[...] = v_sum
    v_total, v_finish = ring_sum(lambda d: v_part[d], z, zs, v_ring, v_sems)
    out_v[...] = v_total
    o_sum = o_part[y]
    for k, c in enumerate(o_copies):
        c.wait_recv()
        o_sum = o_sum + o_land[k].astype(jnp.float32)
    out_o[...] = o_sum
    o_finish()
    v_finish()
    for c in v_copies + o_copies:
        c.wait_send()


def scatter_grads(normed_rows, scaled_dvalues, value_rows, scaled_grads):
    ys = lax.axis_size("y")
    zs = lax.axis_size("z")
    rows_v, cols_v = normed_rows.shape[1], scaled_dvalues.shape[1]
    rows_o, cols_o = value_rows.shape[1], scaled_grads.shape[1]
    v_rows = rows_v // (ys * zs)
    o_rows = rows_o // (ys * zs)
    vmem = pl.BlockSpec(memory_space=pltpu.VMEM)
    rights, lefts = zs // 2, max((zs - 1) // 2, 1)
    bf = scaled_dvalues.dtype

    def ring_space(block):
        return [
            pltpu.VMEM((rights,) + block, bf),
            pltpu.VMEM((rights,) + block, bf),
            pltpu.VMEM((lefts,) + block, bf),
            pltpu.VMEM((lefts,) + block, bf),
        ]

    ring_sems = [
        pltpu.SemaphoreType.DMA((rights,)),
        pltpu.SemaphoreType.DMA((rights,)),
        pltpu.SemaphoreType.DMA((lefts,)),
        pltpu.SemaphoreType.DMA((lefts,)),
    ]
    return pl.pallas_call(
        functools.partial(scatter_kernel, ys, zs),
        out_shape=(
            jax.ShapeDtypeStruct((v_rows, cols_v), jnp.float32),
            jax.ShapeDtypeStruct((o_rows, cols_o), jnp.float32),
        ),
        in_specs=[vmem] * 4,
        out_specs=(vmem, vmem),
        scratch_shapes=[
            pltpu.VMEM((ys, zs, v_rows, cols_v), bf),
            pltpu.VMEM((zs, ys, o_rows, cols_o), bf),
            pltpu.VMEM((ys - 1, zs, v_rows, cols_v), bf),
            pltpu.VMEM((zs, v_rows, cols_v), jnp.float32),
            pltpu.VMEM((ys, o_rows, cols_o), jnp.float32),
            pltpu.VMEM((ys, o_rows, cols_o), bf),
            pltpu.VMEM((ys - 1, o_rows, cols_o), bf),
            ring_space((v_rows, cols_v)),
            ring_space((ys, o_rows, cols_o)),
            ring_sems,
            ring_sems,
            pltpu.SemaphoreType.DMA((ys - 1,)),
            pltpu.SemaphoreType.DMA((ys - 1,)),
            pltpu.SemaphoreType.DMA((ys - 1,)),
            pltpu.SemaphoreType.DMA((ys - 1,)),
        ],
        compiler_params=pltpu.CompilerParams(
            collective_id=2, has_side_effects=True, vmem_limit_bytes=48 * 1024 * 1024
        ),
    )(normed_rows.T, scaled_dvalues, value_rows.T, scaled_grads)


DP = ("y", "z")


def on_device(inputs, cotangent, value_weight, output_weight, norm_gain, value_noise, output_noise):
    micro_count, example_count, seq_len, feature_width = inputs.shape
    feed_rows = inputs.reshape(micro_count, example_count * seq_len, feature_width)
    cot_rows = cotangent.reshape(micro_count, example_count * seq_len, feature_width)
    value_matrix, output_matrix = gather_weights(value_weight[0], output_weight[0])
    head_width = value_matrix.shape[1]
    gains = norm_gain[0]
    kept_inputs, kept_values, kept_grads, kept_dvalues, square_table = run_chain(
        feed_rows, cot_rows, gains, value_matrix, output_matrix, seq_len
    )
    unused_wide, unused_inverse, normed_rows = norm_parts(
        kept_inputs.reshape(-1, feature_width), gains
    )
    total_squares = square_table[:micro_count, : example_count]
    clip_weight = 1.0 / (jnp.sqrt(total_squares) + 0.01)
    token_weight = jnp.repeat(clip_weight, seq_len, axis=1)[:, :, None]
    scaled_dvalues = (
        (kept_dvalues.astype(jnp.float32) * token_weight)
        .astype(jnp.bfloat16)
        .reshape(-1, head_width)
    )
    scaled_grads = (
        (kept_grads.astype(jnp.float32) * token_weight)
        .astype(jnp.bfloat16)
        .reshape(-1, feature_width)
    )
    value_rows = kept_values.reshape(-1, head_width)
    columns = normed_rows
    value_part, output_part = scatter_grads(normed_rows, scaled_dvalues, value_rows, scaled_grads)
    grad_scale = math.sqrt(feature_width * head_width)
    value_grad = (value_part * grad_scale + value_noise[0])[None]
    output_grad = (output_part * grad_scale + output_noise[0])[None]
    return (value_grad, output_grad)


def split_dp(mesh):
    devices = mesh.devices
    sections, count = devices.shape
    try:
        across = len({d.coords[1] for d in devices[0]})
    except (AttributeError, IndexError, TypeError):
        across = 1
    if across < 1 or count % across:
        across = 1
    return Mesh(devices.reshape(sections, across, count // across), ("section",) + DP)


def solution(mesh):
    grid = split_dp(mesh)
    return jax.shard_map(
        on_device,
        mesh=grid,
        in_specs=(
            P(None, DP, None, None),
            P(None, DP, None, None),
            P("section", DP, None),
            P("section", DP, None),
            P("section", None),
            P("section", DP, None),
            P("section", DP, None),
        ),
        out_specs=(P("section", DP, None), P("section", DP, None)),
        check_vma=False,
    )
```

```python
import functools
import math

import jax
import jax.numpy as jnp
from jax import lax
from jax.experimental import pallas as pl
from jax.experimental.pallas import tpu as pltpu
from jax.sharding import Mesh, PartitionSpec as P


def norm_parts(current, gains):
    widened = current.astype(jnp.float32)
    inverse = lax.rsqrt(jnp.mean(widened * widened, axis=-1, keepdims=True) + 1e-06)
    normed = (widened * inverse * gains).astype(jnp.bfloat16)
    return (widened, inverse, normed)


def layer_forward(current, gains, value_matrix, output_matrix):
    widened, inverse, normed = norm_parts(current, gains)
    values = jnp.dot(normed, value_matrix, preferred_element_type=jnp.float32).astype(jnp.bfloat16)
    result = (widened + jnp.dot(values, output_matrix, preferred_element_type=jnp.float32)).astype(
        jnp.bfloat16
    )
    return (values, result)


def layer_backward(current, incoming, gains, value_matrix, output_matrix):
    widened, inverse, normed = norm_parts(current, gains)
    dvalues = jnp.dot(incoming, output_matrix.T, preferred_element_type=jnp.float32).astype(
        jnp.bfloat16
    )
    dnormed = jnp.dot(dvalues, value_matrix.T, preferred_element_type=jnp.float32) * gains
    centred = widened * inverse
    through = inverse * (dnormed - centred * jnp.mean(dnormed * centred, axis=-1, keepdims=True))
    before = (incoming.astype(jnp.float32) + through).astype(jnp.bfloat16)
    return (normed, dvalues, before)


def example_sums(left, right, seq_len):
    first = left.reshape(-1, seq_len, left.shape[-1])
    second = right.reshape(-1, seq_len, right.shape[-1])
    gram_first = jnp.einsum("eth,esh->ets", first, first, preferred_element_type=jnp.float32)
    gram_second = jnp.einsum("eth,esh->ets", second, second, preferred_element_type=jnp.float32)
    return jnp.sum(gram_first * gram_second, axis=(1, 2))


def chain_kernel(
    sections, seq_len,
    seed_ref, cot_ref, gain_ref, wv_ref, wo_ref,
    kin_ref, kval_ref, kgrad_ref, kdv_ref, total_ref,
    fbuf, fres, bbuf, bres, work, fsend, frecv, bsend, brecv, sq_mine, sq_all, sq_send, sq_recv,
):
    place = lax.axis_index("section")
    micro_count, rows, width = seed_ref.shape
    heads = wv_ref.shape[1]
    ahead = lax.rem(place + 1, sections)
    behind = lax.rem(place + sections - 1, sections)
    first = place == 0
    last = place == sections - 1

    barrier = pltpu.get_barrier_semaphore()
    for k in range(1, sections):
        pl.semaphore_signal(
            barrier, inc=1, device_id={"section": lax.rem(place + k, sections)}, device_id_type=pl.DeviceIdType.MESH
        )
    pl.semaphore_wait(barrier, sections - 1)

    @pl.when(first)
    def _():
        fbuf[...] = seed_ref[...]

    @pl.when(last)
    def _():
        bbuf[...] = cot_ref[...]

    def forward_copy(m):
        return pltpu.make_async_remote_copy(
            src_ref=fres.at[m], dst_ref=fbuf.at[m], send_sem=fsend.at[m], recv_sem=frecv.at[m],
            device_id={"section": ahead}, device_id_type=pl.DeviceIdType.MESH,
        )

    def backward_copy(m):
        return pltpu.make_async_remote_copy(
            src_ref=bres.at[m], dst_ref=bbuf.at[m], send_sem=bsend.at[m], recv_sem=brecv.at[m],
            device_id={"section": behind}, device_id_type=pl.DeviceIdType.MESH,
        )

    head_tile, width_tile = heads, width

    def columns(i, tile):
        return pl.ds(pl.multiple_of(i * tile, tile), tile)

    for m in range(micro_count):
        @pl.when(place > 0)
        def _():
            forward_copy(m).wait_recv()

        x = fbuf[m]
        kin_ref[m] = x
        wide = x.astype(jnp.float32)
        inverse = lax.rsqrt(jnp.mean(wide * wide, axis=-1, keepdims=True) + 1e-06)
        normed = (wide * inverse * gain_ref[...]).astype(jnp.bfloat16)

        def value_tile(i, carry):
            kval_ref[m, :, columns(i, head_tile)] = jnp.dot(
                normed, wv_ref[:, columns(i, head_tile)], preferred_element_type=jnp.float32
            ).astype(jnp.bfloat16)
            return carry

        lax.fori_loop(0, heads // head_tile, value_tile, 0)
        values = kval_ref[m]

        def result_tile(i, carry):
            fres[m, :, columns(i, width_tile)] = (
                fbuf[m, :, columns(i, width_tile)].astype(jnp.float32)
                + jnp.dot(values, wo_ref[:, columns(i, width_tile)], preferred_element_type=jnp.float32)
            ).astype(jnp.bfloat16)
            return carry

        lax.fori_loop(0, width // width_tile, result_tile, 0)

        @pl.when(place < sections - 1)
        def _():
            forward_copy(m).start()

    contract = (((1,), (1,)), ((), ()))
    for m in range(micro_count):
        @pl.when(place < sections - 1)
        def _():
            backward_copy(m).wait_recv()

        grad = bbuf[m]
        kgrad_ref[m] = grad

        def dvalue_tile(i, carry):
            kdv_ref[m, :, columns(i, head_tile)] = lax.dot_general(
                grad, wo_ref[columns(i, head_tile), :], contract, preferred_element_type=jnp.float32
            ).astype(jnp.bfloat16)
            return carry

        lax.fori_loop(0, heads // head_tile, dvalue_tile, 0)
        dvalues = kdv_ref[m]

        def dnormed_tile(i, carry):
            work[:, columns(i, width_tile)] = lax.dot_general(
                dvalues, wv_ref[columns(i, width_tile), :], contract, preferred_element_type=jnp.float32
            ) * gain_ref[:, columns(i, width_tile)]
            return carry

        lax.fori_loop(0, width // width_tile, dnormed_tile, 0)
        wide = kin_ref[m].astype(jnp.float32)
        inverse = lax.rsqrt(jnp.mean(wide * wide, axis=-1, keepdims=True) + 1e-06)
        dnormed = work[...]
        centred = wide * inverse
        through = inverse * (dnormed - centred * jnp.mean(dnormed * centred, axis=-1, keepdims=True))
        bres[m] = (grad.astype(jnp.float32) + through).astype(jnp.bfloat16)

        @pl.when(place > 0)
        def _():
            backward_copy(m).start()

    lane = lax.broadcasted_iota(jnp.int32, sq_mine.shape, 1)
    row = lax.broadcasted_iota(jnp.int32, sq_mine.shape, 0)
    squares = jnp.zeros(sq_mine.shape, jnp.float32)
    for m in range(micro_count):
        wide = kin_ref[m].astype(jnp.float32)
        inverse = lax.rsqrt(jnp.mean(wide * wide, axis=-1, keepdims=True) + 1e-06)
        normed = (wide * inverse * gain_ref[...]).astype(jnp.bfloat16)
        for e in range(rows // seq_len):
            span = slice(e * seq_len, (e + 1) * seq_len)
            pairs = ((normed[span], kdv_ref[m, span]), (kval_ref[m, span], kgrad_ref[m, span]))
            term = 0.0
            for left_part, right_part in pairs:
                gram_left = lax.dot_general(left_part, left_part, contract, preferred_element_type=jnp.float32)
                gram_right = lax.dot_general(right_part, right_part, contract, preferred_element_type=jnp.float32)
                term = term + jnp.sum(gram_left * gram_right)
            squares = jnp.where((row == m) & (lane == e), term, squares)
    sq_mine[...] = squares

    def share(k):
        return pltpu.make_async_remote_copy(
            src_ref=sq_mine, dst_ref=sq_all.at[k - 1], send_sem=sq_send.at[k - 1], recv_sem=sq_recv.at[k - 1],
            device_id={"section": lax.rem(place + k, sections)}, device_id_type=pl.DeviceIdType.MESH,
        )

    for k in range(1, sections):
        share(k).start()
    total = squares
    for k in range(1, sections):
        share(k).wait_recv()
        total = total + sq_all[k - 1]
    total_ref[...] = total

    for k in range(1, sections):
        share(k).wait_send()
    for m in range(micro_count):
        @pl.when(place < sections - 1)
        def _():
            forward_copy(m).wait_send()

        @pl.when(place > 0)
        def _():
            backward_copy(m).wait_send()


def run_chain(feed_rows, cot_rows, gains, value_matrix, output_matrix, seq_len):
    sections = lax.axis_size("section")
    micro_count, rows, width = feed_rows.shape
    heads = value_matrix.shape[1]
    vmem = pl.BlockSpec(memory_space=pltpu.VMEM)
    act = jax.ShapeDtypeStruct((micro_count, rows, width), jnp.bfloat16)
    head_act = jax.ShapeDtypeStruct((micro_count, rows, heads), jnp.bfloat16)
    return pl.pallas_call(
        functools.partial(chain_kernel, sections, seq_len),
        out_shape=(act, head_act, act, head_act, jax.ShapeDtypeStruct((8, 128), jnp.float32)),
        in_specs=[vmem] * 5,
        out_specs=(vmem,) * 5,
        scratch_shapes=[
            pltpu.VMEM((micro_count, rows, width), jnp.bfloat16),
            pltpu.VMEM((micro_count, rows, width), jnp.bfloat16),
            pltpu.VMEM((micro_count, rows, width), jnp.bfloat16),
            pltpu.VMEM((micro_count, rows, width), jnp.bfloat16),
            pltpu.VMEM((rows, width), jnp.float32),
            pltpu.SemaphoreType.DMA((micro_count,)),
            pltpu.SemaphoreType.DMA((micro_count,)),
            pltpu.SemaphoreType.DMA((micro_count,)),
            pltpu.SemaphoreType.DMA((micro_count,)),
            pltpu.VMEM((8, 128), jnp.float32),
            pltpu.VMEM((sections - 1, 8, 128), jnp.float32),
            pltpu.SemaphoreType.DMA((sections - 1,)),
            pltpu.SemaphoreType.DMA((sections - 1,)),
        ],
        compiler_params=pltpu.CompilerParams(
            collective_id=0, has_side_effects=True, vmem_limit_bytes=48 * 1024 * 1024
        ),
    )(feed_rows, cot_rows, gains.reshape(1, width), value_matrix, output_matrix)


def ring_copies(window, first_src, z, zs, sems):
    mesh_ids = pl.DeviceIdType.MESH
    right_send, right_recv, left_send, left_recv = sems
    rights, lefts = zs // 2, (zs - 1) // 2

    def right(t):
        slot = lax.rem(z + zs - t, zs)
        return pltpu.make_async_remote_copy(
            src_ref=first_src if t == 0 else window(slot), dst_ref=window(slot),
            send_sem=right_send.at[t], recv_sem=right_recv.at[t],
            device_id={"z": lax.rem(z + 1, zs)}, device_id_type=mesh_ids,
        )

    def left(t):
        slot = lax.rem(z + t, zs)
        return pltpu.make_async_remote_copy(
            src_ref=first_src if t == 0 else window(slot), dst_ref=window(slot),
            send_sem=left_send.at[t], recv_sem=left_recv.at[t],
            device_id={"z": lax.rem(z + zs - 1, zs)}, device_id_type=mesh_ids,
        )

    def right_in(t):
        return pltpu.make_async_remote_copy(
            src_ref=first_src, dst_ref=window(lax.rem(z + 2 * zs - 1 - t, zs)),
            send_sem=right_send.at[t], recv_sem=right_recv.at[t],
            device_id={"z": z}, device_id_type=mesh_ids,
        )

    def left_in(t):
        return pltpu.make_async_remote_copy(
            src_ref=first_src, dst_ref=window(lax.rem(z + 1 + t, zs)),
            send_sem=left_send.at[t], recv_sem=left_recv.at[t],
            device_id={"z": z}, device_id_type=mesh_ids,
        )

    def run():
        for t in range(rights):
            right(t).start()
            if t < lefts:
                left(t).start()
            right_in(t).wait_recv()
            if t < lefts:
                left_in(t).wait_recv()

    def finish():
        for t in range(rights):
            right(t).wait_send()
        for t in range(lefts):
            left(t).wait_send()

    return run, finish


def gather_kernel(ys, zs, wv_ref, wo_ref, wv_all, wo_all, own_sem, va, vb_send, vb_recv, oa_send, oa_recv, ob):
    y = lax.axis_index("y")
    z = lax.axis_index("z")
    mesh_ids = pl.DeviceIdType.MESH
    barrier = pltpu.get_barrier_semaphore()
    pl.semaphore_signal(barrier, inc=1, device_id={"z": lax.rem(z + 1, zs)}, device_id_type=mesh_ids)
    pl.semaphore_signal(barrier, inc=1, device_id={"z": lax.rem(z + zs - 1, zs)}, device_id_type=mesh_ids)
    for k in range(1, ys):
        pl.semaphore_signal(barrier, inc=1, device_id={"y": lax.rem(y + k, ys)}, device_id_type=mesh_ids)
    pl.semaphore_wait(barrier, ys + 1)

    own_v = pltpu.make_async_copy(wv_ref, wv_all.at[y, z], own_sem.at[0])
    own_o = pltpu.make_async_copy(wo_ref, wo_all.at[y, z], own_sem.at[1])
    own_v.start()
    own_o.start()

    def o_first(k, target):
        return pltpu.make_async_remote_copy(
            src_ref=wo_ref, dst_ref=wo_all.at[y, z], send_sem=oa_send.at[k - 1],
            recv_sem=oa_recv.at[k - 1], device_id={"y": target}, device_id_type=mesh_ids,
        )

    def o_first_in(k):
        return pltpu.make_async_remote_copy(
            src_ref=wo_ref, dst_ref=wo_all.at[lax.rem(y + ys - k, ys), z], send_sem=oa_send.at[k - 1],
            recv_sem=oa_recv.at[k - 1], device_id={"y": y}, device_id_type=mesh_ids,
        )

    def v_second(k, row, target):
        return pltpu.make_async_remote_copy(
            src_ref=wv_all.at[pl.ds(row, 1)], dst_ref=wv_all.at[pl.ds(row, 1)],
            send_sem=vb_send.at[k - 1], recv_sem=vb_recv.at[k - 1],
            device_id={"y": target}, device_id_type=mesh_ids,
        )

    for k in range(1, ys):
        o_first(k, lax.rem(y + k, ys)).start()
    v_ring, v_ring_done = ring_copies(lambda o: wv_all.at[y, o], wv_ref, z, zs, va)
    v_ring()
    own_v.wait()
    own_o.wait()
    for k in range(1, ys):
        o_first_in(k).wait_recv()
    for k in range(1, ys):
        v_second(k, y, lax.rem(y + k, ys)).start()
    o_ring, o_ring_done = ring_copies(
        lambda o: wo_all.at[:, pl.ds(o, 1)], wo_all.at[:, pl.ds(z, 1)], z, zs, ob
    )
    o_ring()
    v_ring_done()
    for k in range(1, ys):
        o_first(k, lax.rem(y + k, ys)).wait_send()
    for k in range(1, ys):
        v_second(k, lax.rem(y + ys - k, ys), y).wait_recv()
    o_ring_done()
    for k in range(1, ys):
        v_second(k, y, lax.rem(y + k, ys)).wait_send()


def gather_weights(value_shard, output_shard):
    ys = lax.axis_size("y")
    zs = lax.axis_size("z")
    anywhere = pl.BlockSpec(memory_space=pl.ANY)
    ring_sems = [
        pltpu.SemaphoreType.DMA((zs // 2,)),
        pltpu.SemaphoreType.DMA((zs // 2,)),
        pltpu.SemaphoreType.DMA((max((zs - 1) // 2, 1),)),
        pltpu.SemaphoreType.DMA((max((zs - 1) // 2, 1),)),
    ]
    wv_all, wo_all = pl.pallas_call(
        functools.partial(gather_kernel, ys, zs),
        out_shape=(
            jax.ShapeDtypeStruct((ys, zs) + value_shard.shape, value_shard.dtype),
            jax.ShapeDtypeStruct((ys, zs) + output_shard.shape, output_shard.dtype),
        ),
        in_specs=[anywhere] * 2,
        out_specs=(anywhere, anywhere),
        scratch_shapes=[pltpu.SemaphoreType.DMA((2,)), ring_sems]
        + [pltpu.SemaphoreType.DMA((ys - 1,))] * 4
        + [ring_sems],
        compiler_params=pltpu.CompilerParams(collective_id=1, has_side_effects=True),
    )(value_shard, output_shard)
    return (
        wv_all.reshape((-1,) + value_shard.shape[1:]),
        wo_all.reshape((-1,) + output_shard.shape[1:]),
    )


def ring_sum(get, z, zs, bufs, sems):
    mesh_ids = pl.DeviceIdType.MESH
    rsend, rrecv, lsend, lrecv = bufs
    rs_send, rs_recv, ls_send, ls_recv = sems
    rights, lefts = zs // 2, (zs - 1) // 2

    def right(t):
        return pltpu.make_async_remote_copy(
            src_ref=rsend.at[t], dst_ref=rrecv.at[t], send_sem=rs_send.at[t], recv_sem=rs_recv.at[t],
            device_id={"z": lax.rem(z + 1, zs)}, device_id_type=mesh_ids,
        )

    def left(t):
        return pltpu.make_async_remote_copy(
            src_ref=lsend.at[t], dst_ref=lrecv.at[t], send_sem=ls_send.at[t], recv_sem=ls_recv.at[t],
            device_id={"z": lax.rem(z + zs - 1, zs)}, device_id_type=mesh_ids,
        )

    for t in range(rights):
        value = get(lax.rem(z + rights - t, zs))
        if t > 0:
            value = value + rrecv[t - 1].astype(jnp.float32)
        rsend[t] = value.astype(rsend.dtype)
        right(t).start()
        if t < lefts:
            value = get(lax.rem(z + zs - lefts + t, zs))
            if t > 0:
                value = value + lrecv[t - 1].astype(jnp.float32)
            lsend[t] = value.astype(lsend.dtype)
            left(t).start()
        right(t).wait_recv()
        if t < lefts:
            left(t).wait_recv()
    total = get(z) + rrecv[rights - 1].astype(jnp.float32)
    if lefts > 0:
        total = total + lrecv[lefts - 1].astype(jnp.float32)

    def finish():
        for t in range(rights):
            right(t).wait_send()
        for t in range(lefts):
            left(t).wait_send()

    return total, finish


def direct_copies(source, landing, axis, me, count, send_sems, recv_sems):
    def copy(k):
        return pltpu.make_async_remote_copy(
            src_ref=source.at[lax.rem(me + k, count)], dst_ref=landing.at[k - 1],
            send_sem=send_sems.at[k - 1], recv_sem=recv_sems.at[k - 1],
            device_id={axis: lax.rem(me + k, count)}, device_id_type=pl.DeviceIdType.MESH,
        )

    return [copy(k) for k in range(1, count)]


def scatter_kernel(
    ys, zs, ht_ref, sdu_ref, ut_ref, sg_ref, out_v, out_o,
    xv_ref, xo_ref, v_land, v_part, o_part, o_send, o_land, v_ring, o_ring, v_sems, o_sems, vd_send, vd_recv, od_send, od_recv,
):
    y = lax.axis_index("y")
    z = lax.axis_index("z")
    mesh_ids = pl.DeviceIdType.MESH
    barrier = pltpu.get_barrier_semaphore()
    pl.semaphore_signal(barrier, inc=1, device_id={"z": lax.rem(z + 1, zs)}, device_id_type=mesh_ids)
    pl.semaphore_signal(barrier, inc=1, device_id={"z": lax.rem(z + zs - 1, zs)}, device_id_type=mesh_ids)
    for k in range(1, ys):
        pl.semaphore_signal(barrier, inc=1, device_id={"y": lax.rem(y + k, ys)}, device_id_type=mesh_ids)
    v_rows, o_rows = xv_ref.shape[2], xo_ref.shape[2]
    for a in range(ys):
        group = jnp.dot(
            ht_ref[a * zs * v_rows:(a + 1) * zs * v_rows, :], sdu_ref[...], preferred_element_type=jnp.float32
        )
        for b in range(zs):
            xv_ref[a, b] = group[b * v_rows:(b + 1) * v_rows].astype(xv_ref.dtype)
    for a in range(ys):
        group = jnp.dot(
            ut_ref[a * zs * o_rows:(a + 1) * zs * o_rows, :], sg_ref[...], preferred_element_type=jnp.float32
        )
        for b in range(zs):
            xo_ref[b, a] = group[b * o_rows:(b + 1) * o_rows].astype(xo_ref.dtype)
    pl.semaphore_wait(barrier, ys + 1)

    v_copies = direct_copies(xv_ref, v_land, "y", y, ys, vd_send, vd_recv)
    for c in v_copies:
        c.start()
    o_total, o_finish = ring_sum(lambda d: xo_ref[d].astype(jnp.float32), z, zs, o_ring, o_sems)
    o_part[...] = o_total
    o_send[...] = o_total.astype(o_send.dtype)
    o_copies = direct_copies(o_send, o_land, "y", y, ys, od_send, od_recv)
    for c in o_copies:
        c.start()
    v_sum = xv_ref[y].astype(jnp.float32)
    for k, c in enumerate(v_copies):
        c.wait_recv()
        v_sum = v_sum + v_land[k].astype(jnp.float32)
    v_part[...] = v_sum
    v_total, v_finish = ring_sum(lambda d: v_part[d], z, zs, v_ring, v_sems)
    out_v[...] = v_total
    o_sum = o_part[y]
    for k, c in enumerate(o_copies):
        c.wait_recv()
        o_sum = o_sum + o_land[k].astype(jnp.float32)
    out_o[...] = o_sum
    o_finish()
    v_finish()
    for c in v_copies + o_copies:
        c.wait_send()


def scatter_grads(normed_rows, scaled_dvalues, value_rows, scaled_grads):
    ys = lax.axis_size("y")
    zs = lax.axis_size("z")
    rows_v, cols_v = normed_rows.shape[1], scaled_dvalues.shape[1]
    rows_o, cols_o = value_rows.shape[1], scaled_grads.shape[1]
    v_rows = rows_v // (ys * zs)
    o_rows = rows_o // (ys * zs)
    vmem = pl.BlockSpec(memory_space=pltpu.VMEM)
    rights, lefts = zs // 2, max((zs - 1) // 2, 1)
    bf = scaled_dvalues.dtype

    def ring_space(block):
        return [
            pltpu.VMEM((rights,) + block, bf),
            pltpu.VMEM((rights,) + block, bf),
            pltpu.VMEM((lefts,) + block, bf),
            pltpu.VMEM((lefts,) + block, bf),
        ]

    ring_sems = [
        pltpu.SemaphoreType.DMA((rights,)),
        pltpu.SemaphoreType.DMA((rights,)),
        pltpu.SemaphoreType.DMA((lefts,)),
        pltpu.SemaphoreType.DMA((lefts,)),
    ]
    return pl.pallas_call(
        functools.partial(scatter_kernel, ys, zs),
        out_shape=(
            jax.ShapeDtypeStruct((v_rows, cols_v), jnp.float32),
            jax.ShapeDtypeStruct((o_rows, cols_o), jnp.float32),
        ),
        in_specs=[vmem] * 4,
        out_specs=(vmem, vmem),
        scratch_shapes=[
            pltpu.VMEM((ys, zs, v_rows, cols_v), bf),
            pltpu.VMEM((zs, ys, o_rows, cols_o), bf),
            pltpu.VMEM((ys - 1, zs, v_rows, cols_v), bf),
            pltpu.VMEM((zs, v_rows, cols_v), jnp.float32),
            pltpu.VMEM((ys, o_rows, cols_o), jnp.float32),
            pltpu.VMEM((ys, o_rows, cols_o), bf),
            pltpu.VMEM((ys - 1, o_rows, cols_o), bf),
            ring_space((v_rows, cols_v)),
            ring_space((ys, o_rows, cols_o)),
            ring_sems,
            ring_sems,
            pltpu.SemaphoreType.DMA((ys - 1,)),
            pltpu.SemaphoreType.DMA((ys - 1,)),
            pltpu.SemaphoreType.DMA((ys - 1,)),
            pltpu.SemaphoreType.DMA((ys - 1,)),
        ],
        compiler_params=pltpu.CompilerParams(
            collective_id=2, has_side_effects=True, vmem_limit_bytes=48 * 1024 * 1024
        ),
    )(normed_rows.T, scaled_dvalues, value_rows.T, scaled_grads)


DP = ("y", "z")


def on_device(inputs, cotangent, value_weight, output_weight, norm_gain, value_noise, output_noise):
    micro_count, example_count, seq_len, feature_width = inputs.shape
    feed_rows = inputs.reshape(micro_count, example_count * seq_len, feature_width)
    cot_rows = cotangent.reshape(micro_count, example_count * seq_len, feature_width)
    value_matrix, output_matrix = gather_weights(value_weight[0], output_weight[0])
    head_width = value_matrix.shape[1]
    gains = norm_gain[0]
    kept_inputs, kept_values, kept_grads, kept_dvalues, square_table = run_chain(
        feed_rows, cot_rows, gains, value_matrix, output_matrix, seq_len
    )
    unused_wide, unused_inverse, normed_rows = norm_parts(
        kept_inputs.reshape(-1, feature_width), gains
    )
    total_squares = square_table[:micro_count, : example_count]
    clip_weight = 1.0 / (jnp.sqrt(total_squares) + 0.01)
    token_weight = jnp.repeat(clip_weight, seq_len, axis=1)[:, :, None]
    scaled_dvalues = (
        (kept_dvalues.astype(jnp.float32) * token_weight)
        .astype(jnp.bfloat16)
        .reshape(-1, head_width)
    )
    scaled_grads = (
        (kept_grads.astype(jnp.float32) * token_weight)
        .astype(jnp.bfloat16)
        .reshape(-1, feature_width)
    )
    value_rows = kept_values.reshape(-1, head_width)
    columns = normed_rows
    value_part, output_part = scatter_grads(normed_rows, scaled_dvalues, value_rows, scaled_grads)
    grad_scale = math.sqrt(feature_width * head_width)
    value_grad = (value_part * grad_scale + value_noise[0])[None]
    output_grad = (output_part * grad_scale + output_noise[0])[None]
    return (value_grad, output_grad)


def split_dp(mesh):
    devices = mesh.devices
    sections, count = devices.shape
    try:
        across = len({d.coords[1] for d in devices[0]})
    except (AttributeError, IndexError, TypeError):
        across = 1
    if across < 1 or count % across:
        across = 1
    return Mesh(devices.reshape(sections, across, count // across), ("section",) + DP)


def solution(mesh):
    grid = split_dp(mesh)
    return jax.shard_map(
        on_device,
        mesh=grid,
        in_specs=(
            P(None, DP, None, None),
            P(None, DP, None, None),
            P("section", DP, None),
            P("section", DP, None),
            P("section", None),
            P("section", DP, None),
            P("section", DP, None),
        ),
        out_specs=(P("section", DP, None), P("section", DP, None)),
        check_vma=False,
    )
```

```python
import functools
import math

import jax
import jax.numpy as jnp
from jax import lax
from jax.experimental import pallas as pl
from jax.experimental.pallas import tpu as pltpu
from jax.sharding import Mesh, PartitionSpec as P


def norm_parts(current, gains):
    widened = current.astype(jnp.float32)
    inverse = lax.rsqrt(jnp.mean(widened * widened, axis=-1, keepdims=True) + 1e-06)
    normed = (widened * inverse * gains).astype(jnp.bfloat16)
    return (widened, inverse, normed)


def layer_forward(current, gains, value_matrix, output_matrix):
    widened, inverse, normed = norm_parts(current, gains)
    values = jnp.dot(normed, value_matrix, preferred_element_type=jnp.float32).astype(jnp.bfloat16)
    result = (widened + jnp.dot(values, output_matrix, preferred_element_type=jnp.float32)).astype(
        jnp.bfloat16
    )
    return (values, result)


def layer_backward(current, incoming, gains, value_matrix, output_matrix):
    widened, inverse, normed = norm_parts(current, gains)
    dvalues = jnp.dot(incoming, output_matrix.T, preferred_element_type=jnp.float32).astype(
        jnp.bfloat16
    )
    dnormed = jnp.dot(dvalues, value_matrix.T, preferred_element_type=jnp.float32) * gains
    centred = widened * inverse
    through = inverse * (dnormed - centred * jnp.mean(dnormed * centred, axis=-1, keepdims=True))
    before = (incoming.astype(jnp.float32) + through).astype(jnp.bfloat16)
    return (normed, dvalues, before)


def example_sums(left, right, seq_len):
    first = left.reshape(-1, seq_len, left.shape[-1])
    second = right.reshape(-1, seq_len, right.shape[-1])
    gram_first = jnp.einsum("eth,esh->ets", first, first, preferred_element_type=jnp.float32)
    gram_second = jnp.einsum("eth,esh->ets", second, second, preferred_element_type=jnp.float32)
    return jnp.sum(gram_first * gram_second, axis=(1, 2))


def chain_kernel(
    sections, seq_len,
    seed_ref, cot_ref, gain_ref, wv_ref, wo_ref,
    kin_ref, kval_ref, kgrad_ref, kdv_ref, total_ref,
    fbuf, fres, bbuf, bres, work, fsend, frecv, bsend, brecv, sq_mine, sq_all, sq_send, sq_recv,
):
    place = lax.axis_index("section")
    micro_count, rows, width = seed_ref.shape
    heads = wv_ref.shape[1]
    ahead = lax.rem(place + 1, sections)
    behind = lax.rem(place + sections - 1, sections)
    first = place == 0
    last = place == sections - 1

    barrier = pltpu.get_barrier_semaphore()
    for k in range(1, sections):
        pl.semaphore_signal(
            barrier, inc=1, device_id={"section": lax.rem(place + k, sections)}, device_id_type=pl.DeviceIdType.MESH
        )

    @pl.when(first)
    def _():
        fbuf[...] = seed_ref[...]

    @pl.when(last)
    def _():
        bbuf[...] = cot_ref[...]

    pl.semaphore_wait(barrier, sections - 1)

    def forward_copy(m):
        return pltpu.make_async_remote_copy(
            src_ref=fres.at[m], dst_ref=fbuf.at[m], send_sem=fsend.at[m], recv_sem=frecv.at[m],
            device_id={"section": ahead}, device_id_type=pl.DeviceIdType.MESH,
        )

    def backward_copy(m):
        return pltpu.make_async_remote_copy(
            src_ref=bres.at[m], dst_ref=bbuf.at[m], send_sem=bsend.at[m], recv_sem=brecv.at[m],
            device_id={"section": behind}, device_id_type=pl.DeviceIdType.MESH,
        )

    head_tile, width_tile = heads, width

    def columns(i, tile):
        return pl.ds(pl.multiple_of(i * tile, tile), tile)

    for m in range(micro_count):
        @pl.when(place > 0)
        def _():
            forward_copy(m).wait_recv()

        x = fbuf[m]
        kin_ref[m] = x
        wide = x.astype(jnp.float32)
        inverse = lax.rsqrt(jnp.mean(wide * wide, axis=-1, keepdims=True) + 1e-06)
        normed = (wide * inverse * gain_ref[...]).astype(jnp.bfloat16)

        def value_tile(i, carry):
            kval_ref[m, :, columns(i, head_tile)] = jnp.dot(
                normed, wv_ref[:, columns(i, head_tile)], preferred_element_type=jnp.float32
            ).astype(jnp.bfloat16)
            return carry

        lax.fori_loop(0, heads // head_tile, value_tile, 0)
        values = kval_ref[m]

        def result_tile(i, carry):
            fres[m, :, columns(i, width_tile)] = (
                fbuf[m, :, columns(i, width_tile)].astype(jnp.float32)
                + jnp.dot(values, wo_ref[:, columns(i, width_tile)], preferred_element_type=jnp.float32)
            ).astype(jnp.bfloat16)
            return carry

        lax.fori_loop(0, width // width_tile, result_tile, 0)

        @pl.when(place < sections - 1)
        def _():
            forward_copy(m).start()

    contract = (((1,), (1,)), ((), ()))
    for m in range(micro_count):
        @pl.when(place < sections - 1)
        def _():
            backward_copy(m).wait_recv()

        grad = bbuf[m]
        kgrad_ref[m] = grad

        def dvalue_tile(i, carry):
            kdv_ref[m, :, columns(i, head_tile)] = lax.dot_general(
                grad, wo_ref[columns(i, head_tile), :], contract, preferred_element_type=jnp.float32
            ).astype(jnp.bfloat16)
            return carry

        lax.fori_loop(0, heads // head_tile, dvalue_tile, 0)
        dvalues = kdv_ref[m]

        def dnormed_tile(i, carry):
            work[:, columns(i, width_tile)] = lax.dot_general(
                dvalues, wv_ref[columns(i, width_tile), :], contract, preferred_element_type=jnp.float32
            ) * gain_ref[:, columns(i, width_tile)]
            return carry

        lax.fori_loop(0, width // width_tile, dnormed_tile, 0)
        wide = kin_ref[m].astype(jnp.float32)
        inverse = lax.rsqrt(jnp.mean(wide * wide, axis=-1, keepdims=True) + 1e-06)
        dnormed = work[...]
        centred = wide * inverse
        through = inverse * (dnormed - centred * jnp.mean(dnormed * centred, axis=-1, keepdims=True))
        bres[m] = (grad.astype(jnp.float32) + through).astype(jnp.bfloat16)

        @pl.when(place > 0)
        def _():
            backward_copy(m).start()

    lane = lax.broadcasted_iota(jnp.int32, sq_mine.shape, 1)
    row = lax.broadcasted_iota(jnp.int32, sq_mine.shape, 0)
    squares = jnp.zeros(sq_mine.shape, jnp.float32)
    for m in range(micro_count):
        wide = kin_ref[m].astype(jnp.float32)
        inverse = lax.rsqrt(jnp.mean(wide * wide, axis=-1, keepdims=True) + 1e-06)
        normed = (wide * inverse * gain_ref[...]).astype(jnp.bfloat16)
        for e in range(rows // seq_len):
            span = slice(e * seq_len, (e + 1) * seq_len)
            pairs = ((normed[span], kdv_ref[m, span]), (kval_ref[m, span], kgrad_ref[m, span]))
            term = 0.0
            for left_part, right_part in pairs:
                gram_left = lax.dot_general(left_part, left_part, contract, preferred_element_type=jnp.float32)
                gram_right = lax.dot_general(right_part, right_part, contract, preferred_element_type=jnp.float32)
                term = term + jnp.sum(gram_left * gram_right)
            squares = jnp.where((row == m) & (lane == e), term, squares)
    sq_mine[...] = squares

    def share(k):
        return pltpu.make_async_remote_copy(
            src_ref=sq_mine, dst_ref=sq_all.at[k - 1], send_sem=sq_send.at[k - 1], recv_sem=sq_recv.at[k - 1],
            device_id={"section": lax.rem(place + k, sections)}, device_id_type=pl.DeviceIdType.MESH,
        )

    for k in range(1, sections):
        share(k).start()
    total = squares
    for k in range(1, sections):
        share(k).wait_recv()
        total = total + sq_all[k - 1]
    total_ref[...] = total

    for k in range(1, sections):
        share(k).wait_send()
    for m in range(micro_count):
        @pl.when(place < sections - 1)
        def _():
            forward_copy(m).wait_send()

        @pl.when(place > 0)
        def _():
            backward_copy(m).wait_send()


def run_chain(feed_rows, cot_rows, gains, value_matrix, output_matrix, seq_len):
    sections = lax.axis_size("section")
    micro_count, rows, width = feed_rows.shape
    heads = value_matrix.shape[1]
    vmem = pl.BlockSpec(memory_space=pltpu.VMEM)
    act = jax.ShapeDtypeStruct((micro_count, rows, width), jnp.bfloat16)
    head_act = jax.ShapeDtypeStruct((micro_count, rows, heads), jnp.bfloat16)
    return pl.pallas_call(
        functools.partial(chain_kernel, sections, seq_len),
        out_shape=(act, head_act, act, head_act, jax.ShapeDtypeStruct((8, 128), jnp.float32)),
        in_specs=[vmem] * 5,
        out_specs=(vmem,) * 5,
        scratch_shapes=[
            pltpu.VMEM((micro_count, rows, width), jnp.bfloat16),
            pltpu.VMEM((micro_count, rows, width), jnp.bfloat16),
            pltpu.VMEM((micro_count, rows, width), jnp.bfloat16),
            pltpu.VMEM((micro_count, rows, width), jnp.bfloat16),
            pltpu.VMEM((rows, width), jnp.float32),
            pltpu.SemaphoreType.DMA((micro_count,)),
            pltpu.SemaphoreType.DMA((micro_count,)),
            pltpu.SemaphoreType.DMA((micro_count,)),
            pltpu.SemaphoreType.DMA((micro_count,)),
            pltpu.VMEM((8, 128), jnp.float32),
            pltpu.VMEM((sections - 1, 8, 128), jnp.float32),
            pltpu.SemaphoreType.DMA((sections - 1,)),
            pltpu.SemaphoreType.DMA((sections - 1,)),
        ],
        compiler_params=pltpu.CompilerParams(
            collective_id=0, has_side_effects=True, vmem_limit_bytes=48 * 1024 * 1024
        ),
    )(feed_rows, cot_rows, gains.reshape(1, width), value_matrix, output_matrix)


def ring_copies(window, first_src, z, zs, sems):
    mesh_ids = pl.DeviceIdType.MESH
    right_send, right_recv, left_send, left_recv = sems
    rights, lefts = zs // 2, (zs - 1) // 2

    def right(t):
        slot = lax.rem(z + zs - t, zs)
        return pltpu.make_async_remote_copy(
            src_ref=first_src if t == 0 else window(slot), dst_ref=window(slot),
            send_sem=right_send.at[t], recv_sem=right_recv.at[t],
            device_id={"z": lax.rem(z + 1, zs)}, device_id_type=mesh_ids,
        )

    def left(t):
        slot = lax.rem(z + t, zs)
        return pltpu.make_async_remote_copy(
            src_ref=first_src if t == 0 else window(slot), dst_ref=window(slot),
            send_sem=left_send.at[t], recv_sem=left_recv.at[t],
            device_id={"z": lax.rem(z + zs - 1, zs)}, device_id_type=mesh_ids,
        )

    def right_in(t):
        return pltpu.make_async_remote_copy(
            src_ref=first_src, dst_ref=window(lax.rem(z + 2 * zs - 1 - t, zs)),
            send_sem=right_send.at[t], recv_sem=right_recv.at[t],
            device_id={"z": z}, device_id_type=mesh_ids,
        )

    def left_in(t):
        return pltpu.make_async_remote_copy(
            src_ref=first_src, dst_ref=window(lax.rem(z + 1 + t, zs)),
            send_sem=left_send.at[t], recv_sem=left_recv.at[t],
            device_id={"z": z}, device_id_type=mesh_ids,
        )

    def run():
        for t in range(rights):
            right(t).start()
            if t < lefts:
                left(t).start()
            right_in(t).wait_recv()
            if t < lefts:
                left_in(t).wait_recv()

    def finish():
        for t in range(rights):
            right(t).wait_send()
        for t in range(lefts):
            left(t).wait_send()

    return run, finish


def gather_kernel(ys, zs, wv_ref, wo_ref, wv_all, wo_all, own_sem, va, vb_send, vb_recv, oa_send, oa_recv, ob):
    y = lax.axis_index("y")
    z = lax.axis_index("z")
    mesh_ids = pl.DeviceIdType.MESH
    barrier = pltpu.get_barrier_semaphore()
    pl.semaphore_signal(barrier, inc=1, device_id={"z": lax.rem(z + 1, zs)}, device_id_type=mesh_ids)
    pl.semaphore_signal(barrier, inc=1, device_id={"z": lax.rem(z + zs - 1, zs)}, device_id_type=mesh_ids)
    for k in range(1, ys):
        pl.semaphore_signal(barrier, inc=1, device_id={"y": lax.rem(y + k, ys)}, device_id_type=mesh_ids)
    own_v = pltpu.make_async_copy(wv_ref, wv_all.at[y, z], own_sem.at[0])
    own_o = pltpu.make_async_copy(wo_ref, wo_all.at[y, z], own_sem.at[1])
    own_v.start()
    own_o.start()
    pl.semaphore_wait(barrier, ys + 1)

    def o_first(k, target):
        return pltpu.make_async_remote_copy(
            src_ref=wo_ref, dst_ref=wo_all.at[y, z], send_sem=oa_send.at[k - 1],
            recv_sem=oa_recv.at[k - 1], device_id={"y": target}, device_id_type=mesh_ids,
        )

    def o_first_in(k):
        return pltpu.make_async_remote_copy(
            src_ref=wo_ref, dst_ref=wo_all.at[lax.rem(y + ys - k, ys), z], send_sem=oa_send.at[k - 1],
            recv_sem=oa_recv.at[k - 1], device_id={"y": y}, device_id_type=mesh_ids,
        )

    def v_second(k, row, target):
        return pltpu.make_async_remote_copy(
            src_ref=wv_all.at[pl.ds(row, 1)], dst_ref=wv_all.at[pl.ds(row, 1)],
            send_sem=vb_send.at[k - 1], recv_sem=vb_recv.at[k - 1],
            device_id={"y": target}, device_id_type=mesh_ids,
        )

    for k in range(1, ys):
        o_first(k, lax.rem(y + k, ys)).start()
    v_ring, v_ring_done = ring_copies(lambda o: wv_all.at[y, o], wv_ref, z, zs, va)
    v_ring()
    own_v.wait()
    own_o.wait()
    for k in range(1, ys):
        o_first_in(k).wait_recv()
    for k in range(1, ys):
        v_second(k, y, lax.rem(y + k, ys)).start()
    o_ring, o_ring_done = ring_copies(
        lambda o: wo_all.at[:, pl.ds(o, 1)], wo_all.at[:, pl.ds(z, 1)], z, zs, ob
    )
    o_ring()
    v_ring_done()
    for k in range(1, ys):
        o_first(k, lax.rem(y + k, ys)).wait_send()
    for k in range(1, ys):
        v_second(k, lax.rem(y + ys - k, ys), y).wait_recv()
    o_ring_done()
    for k in range(1, ys):
        v_second(k, y, lax.rem(y + k, ys)).wait_send()


def gather_weights(value_shard, output_shard):
    ys = lax.axis_size("y")
    zs = lax.axis_size("z")
    anywhere = pl.BlockSpec(memory_space=pl.ANY)
    ring_sems = [
        pltpu.SemaphoreType.DMA((zs // 2,)),
        pltpu.SemaphoreType.DMA((zs // 2,)),
        pltpu.SemaphoreType.DMA((max((zs - 1) // 2, 1),)),
        pltpu.SemaphoreType.DMA((max((zs - 1) // 2, 1),)),
    ]
    wv_all, wo_all = pl.pallas_call(
        functools.partial(gather_kernel, ys, zs),
        out_shape=(
            jax.ShapeDtypeStruct((ys, zs) + value_shard.shape, value_shard.dtype),
            jax.ShapeDtypeStruct((ys, zs) + output_shard.shape, output_shard.dtype),
        ),
        in_specs=[anywhere] * 2,
        out_specs=(anywhere, anywhere),
        scratch_shapes=[pltpu.SemaphoreType.DMA((2,)), ring_sems]
        + [pltpu.SemaphoreType.DMA((ys - 1,))] * 4
        + [ring_sems],
        compiler_params=pltpu.CompilerParams(collective_id=1, has_side_effects=True),
    )(value_shard, output_shard)
    return (
        wv_all.reshape((-1,) + value_shard.shape[1:]),
        wo_all.reshape((-1,) + output_shard.shape[1:]),
    )


def ring_sum(get, z, zs, bufs, sems):
    mesh_ids = pl.DeviceIdType.MESH
    rsend, rrecv, lsend, lrecv = bufs
    rs_send, rs_recv, ls_send, ls_recv = sems
    rights, lefts = zs // 2, (zs - 1) // 2

    def right(t):
        return pltpu.make_async_remote_copy(
            src_ref=rsend.at[t], dst_ref=rrecv.at[t], send_sem=rs_send.at[t], recv_sem=rs_recv.at[t],
            device_id={"z": lax.rem(z + 1, zs)}, device_id_type=mesh_ids,
        )

    def left(t):
        return pltpu.make_async_remote_copy(
            src_ref=lsend.at[t], dst_ref=lrecv.at[t], send_sem=ls_send.at[t], recv_sem=ls_recv.at[t],
            device_id={"z": lax.rem(z + zs - 1, zs)}, device_id_type=mesh_ids,
        )

    for t in range(rights):
        value = get(lax.rem(z + rights - t, zs))
        if t > 0:
            value = value + rrecv[t - 1].astype(jnp.float32)
        rsend[t] = value.astype(rsend.dtype)
        right(t).start()
        if t < lefts:
            value = get(lax.rem(z + zs - lefts + t, zs))
            if t > 0:
                value = value + lrecv[t - 1].astype(jnp.float32)
            lsend[t] = value.astype(lsend.dtype)
            left(t).start()
        right(t).wait_recv()
        if t < lefts:
            left(t).wait_recv()
    total = get(z) + rrecv[rights - 1].astype(jnp.float32)
    if lefts > 0:
        total = total + lrecv[lefts - 1].astype(jnp.float32)

    def finish():
        for t in range(rights):
            right(t).wait_send()
        for t in range(lefts):
            left(t).wait_send()

    return total, finish


def direct_copies(source, landing, axis, me, count, send_sems, recv_sems):
    def copy(k):
        return pltpu.make_async_remote_copy(
            src_ref=source.at[lax.rem(me + k, count)], dst_ref=landing.at[k - 1],
            send_sem=send_sems.at[k - 1], recv_sem=recv_sems.at[k - 1],
            device_id={axis: lax.rem(me + k, count)}, device_id_type=pl.DeviceIdType.MESH,
        )

    return [copy(k) for k in range(1, count)]


def scatter_kernel(
    ys, zs, ht_ref, sdu_ref, ut_ref, sg_ref, out_v, out_o,
    xv_ref, xo_ref, v_land, v_part, o_part, o_send, o_land, v_ring, o_ring, v_sems, o_sems, vd_send, vd_recv, od_send, od_recv,
):
    y = lax.axis_index("y")
    z = lax.axis_index("z")
    mesh_ids = pl.DeviceIdType.MESH
    barrier = pltpu.get_barrier_semaphore()
    pl.semaphore_signal(barrier, inc=1, device_id={"z": lax.rem(z + 1, zs)}, device_id_type=mesh_ids)
    pl.semaphore_signal(barrier, inc=1, device_id={"z": lax.rem(z + zs - 1, zs)}, device_id_type=mesh_ids)
    for k in range(1, ys):
        pl.semaphore_signal(barrier, inc=1, device_id={"y": lax.rem(y + k, ys)}, device_id_type=mesh_ids)
    v_rows, o_rows = xv_ref.shape[2], xo_ref.shape[2]
    for a in range(ys):
        group = jnp.dot(
            ht_ref[a * zs * v_rows:(a + 1) * zs * v_rows, :], sdu_ref[...], preferred_element_type=jnp.float32
        )
        for b in range(zs):
            xv_ref[a, b] = group[b * v_rows:(b + 1) * v_rows].astype(xv_ref.dtype)
    for a in range(ys):
        group = jnp.dot(
            ut_ref[a * zs * o_rows:(a + 1) * zs * o_rows, :], sg_ref[...], preferred_element_type=jnp.float32
        )
        for b in range(zs):
            xo_ref[b, a] = group[b * o_rows:(b + 1) * o_rows].astype(xo_ref.dtype)
    pl.semaphore_wait(barrier, ys + 1)

    v_copies = direct_copies(xv_ref, v_land, "y", y, ys, vd_send, vd_recv)
    for c in v_copies:
        c.start()
    o_total, o_finish = ring_sum(lambda d: xo_ref[d].astype(jnp.float32), z, zs, o_ring, o_sems)
    o_part[...] = o_total
    o_send[...] = o_total.astype(o_send.dtype)
    o_copies = direct_copies(o_send, o_land, "y", y, ys, od_send, od_recv)
    for c in o_copies:
        c.start()
    v_sum = xv_ref[y].astype(jnp.float32)
    for k, c in enumerate(v_copies):
        c.wait_recv()
        v_sum = v_sum + v_land[k].astype(jnp.float32)
    v_part[...] = v_sum
    v_total, v_finish = ring_sum(lambda d: v_part[d], z, zs, v_ring, v_sems)
    out_v[...] = v_total
    o_sum = o_part[y]
    for k, c in enumerate(o_copies):
        c.wait_recv()
        o_sum = o_sum + o_land[k].astype(jnp.float32)
    out_o[...] = o_sum
    o_finish()
    v_finish()
    for c in v_copies + o_copies:
        c.wait_send()


def scatter_grads(normed_rows, scaled_dvalues, value_rows, scaled_grads):
    ys = lax.axis_size("y")
    zs = lax.axis_size("z")
    rows_v, cols_v = normed_rows.shape[1], scaled_dvalues.shape[1]
    rows_o, cols_o = value_rows.shape[1], scaled_grads.shape[1]
    v_rows = rows_v // (ys * zs)
    o_rows = rows_o // (ys * zs)
    vmem = pl.BlockSpec(memory_space=pltpu.VMEM)
    rights, lefts = zs // 2, max((zs - 1) // 2, 1)
    bf = scaled_dvalues.dtype

    def ring_space(block):
        return [
            pltpu.VMEM((rights,) + block, bf),
            pltpu.VMEM((rights,) + block, bf),
            pltpu.VMEM((lefts,) + block, bf),
            pltpu.VMEM((lefts,) + block, bf),
        ]

    ring_sems = [
        pltpu.SemaphoreType.DMA((rights,)),
        pltpu.SemaphoreType.DMA((rights,)),
        pltpu.SemaphoreType.DMA((lefts,)),
        pltpu.SemaphoreType.DMA((lefts,)),
    ]
    return pl.pallas_call(
        functools.partial(scatter_kernel, ys, zs),
        out_shape=(
            jax.ShapeDtypeStruct((v_rows, cols_v), jnp.float32),
            jax.ShapeDtypeStruct((o_rows, cols_o), jnp.float32),
        ),
        in_specs=[vmem] * 4,
        out_specs=(vmem, vmem),
        scratch_shapes=[
            pltpu.VMEM((ys, zs, v_rows, cols_v), bf),
            pltpu.VMEM((zs, ys, o_rows, cols_o), bf),
            pltpu.VMEM((ys - 1, zs, v_rows, cols_v), bf),
            pltpu.VMEM((zs, v_rows, cols_v), jnp.float32),
            pltpu.VMEM((ys, o_rows, cols_o), jnp.float32),
            pltpu.VMEM((ys, o_rows, cols_o), bf),
            pltpu.VMEM((ys - 1, o_rows, cols_o), bf),
            ring_space((v_rows, cols_v)),
            ring_space((ys, o_rows, cols_o)),
            ring_sems,
            ring_sems,
            pltpu.SemaphoreType.DMA((ys - 1,)),
            pltpu.SemaphoreType.DMA((ys - 1,)),
            pltpu.SemaphoreType.DMA((ys - 1,)),
            pltpu.SemaphoreType.DMA((ys - 1,)),
        ],
        compiler_params=pltpu.CompilerParams(
            collective_id=2, has_side_effects=True, vmem_limit_bytes=48 * 1024 * 1024
        ),
    )(normed_rows.T, scaled_dvalues, value_rows.T, scaled_grads)


DP = ("y", "z")


def on_device(inputs, cotangent, value_weight, output_weight, norm_gain, value_noise, output_noise):
    micro_count, example_count, seq_len, feature_width = inputs.shape
    feed_rows = inputs.reshape(micro_count, example_count * seq_len, feature_width)
    cot_rows = cotangent.reshape(micro_count, example_count * seq_len, feature_width)
    value_matrix, output_matrix = gather_weights(value_weight[0], output_weight[0])
    head_width = value_matrix.shape[1]
    gains = norm_gain[0]
    kept_inputs, kept_values, kept_grads, kept_dvalues, square_table = run_chain(
        feed_rows, cot_rows, gains, value_matrix, output_matrix, seq_len
    )
    unused_wide, unused_inverse, normed_rows = norm_parts(
        kept_inputs.reshape(-1, feature_width), gains
    )
    total_squares = square_table[:micro_count, : example_count]
    clip_weight = 1.0 / (jnp.sqrt(total_squares) + 0.01)
    token_weight = jnp.repeat(clip_weight, seq_len, axis=1)[:, :, None]
    scaled_dvalues = (
        (kept_dvalues.astype(jnp.float32) * token_weight)
        .astype(jnp.bfloat16)
        .reshape(-1, head_width)
    )
    scaled_grads = (
        (kept_grads.astype(jnp.float32) * token_weight)
        .astype(jnp.bfloat16)
        .reshape(-1, feature_width)
    )
    value_rows = kept_values.reshape(-1, head_width)
    columns = normed_rows
    value_part, output_part = scatter_grads(normed_rows, scaled_dvalues, value_rows, scaled_grads)
    grad_scale = math.sqrt(feature_width * head_width)
    value_grad = (value_part * grad_scale + value_noise[0])[None]
    output_grad = (output_part * grad_scale + output_noise[0])[None]
    return (value_grad, output_grad)


def split_dp(mesh):
    devices = mesh.devices
    sections, count = devices.shape
    try:
        across = len({d.coords[1] for d in devices[0]})
    except (AttributeError, IndexError, TypeError):
        across = 1
    if across < 1 or count % across:
        across = 1
    return Mesh(devices.reshape(sections, across, count // across), ("section",) + DP)


def solution(mesh):
    grid = split_dp(mesh)
    return jax.shard_map(
        on_device,
        mesh=grid,
        in_specs=(
            P(None, DP, None, None),
            P(None, DP, None, None),
            P("section", DP, None),
            P("section", DP, None),
            P("section", None),
            P("section", DP, None),
            P("section", DP, None),
        ),
        out_specs=(P("section", DP, None), P("section", DP, None)),
        check_vma=False,
    )
```
